32 devices in a mesh: dp: 8 (over y, x, core), seq: 4 (over z).
Axes of the slice: x: 2, y: 2, z: 4, core: 2. Of those that a mesh axis runs over, the one named last changes fastest.
Arguments:
- tokens: bfloat16 [2, 8, 1024, 1024], P(None, 'dp', 'seq'), may hold values from -6 to 6
- segments: int32 [2, 8, 1024], P(None, 'dp'), may hold values from 0 to 3, never falling along the last dimension, each value on 1 to 800 neighbouring positions
- ln1_gain: float32 [1024], P(('dp', 'seq')), may hold values from 0.1 to 1.9
- in_weight: float32 [1024, 3072], P(('dp', 'seq')), may hold values from -0.1875 to 0.1875
- conv_kernel: float32 [3, 1024], P(None, ('dp', 'seq')), may hold values from -3 to 3
- out_weight: float32 [1024, 1024], P(('dp', 'seq')), may hold values from -0.1875 to 0.1875
- ln2_gain: float32 [1024], P(('dp', 'seq')), may hold values from 0.1 to 1.9
- gate_weight: float32 [1024, 4608], P(('dp', 'seq')), may hold values from -0.1875 to 0.1875
- up_weight: float32 [1024, 4608], P(('dp', 'seq')), may hold values from -0.1875 to 0.1875
- down_weight: float32 [4608, 1024], P(('dp', 'seq')), may hold values from -0.09375 to 0.09375
- cotangent: bfloat16 [2, 8, 1024, 1024], P(None, 'dp', 'seq'), may hold values from -6 to 6
Outputs:
- output: bfloat16 [2, 8, 1024, 1024], P(None, 'dp', 'seq')
- grad_tokens: bfloat16 [2, 8, 1024, 1024], P(None, 'dp', 'seq')
- grad_ln1: float32 [1024], P(('dp', 'seq'))
- grad_in: float32 [1024, 3072], P(('dp', 'seq'))
- grad_kernel: float32 [3, 1024], P(None, ('dp', 'seq'))
- grad_out: float32 [1024, 1024], P(('dp', 'seq'))
- grad_ln2: float32 [1024], P(('dp', 'seq'))
- grad_gate: float32 [1024, 4608], P(('dp', 'seq'))
- grad_up: float32 [1024, 4608], P(('dp', 'seq'))
- grad_down: float32 [4608, 1024], P(('dp', 'seq'))
The draws below stay inside these ranges and needn't reach their ends.
Inputs may be any that keep to these rules, and one draw needn't show every extreme that they name: `segments`: along each sequence the document numbers start at 0 and never fall; equal numbers mark one document.
All inputs are finite; a program needn't handle non-finite values.
Results may differ from the reference program's by a relative error of at most 0.012.
The reference program's roundings to bfloat16 on the way count: a program that leaves them out, or rounds other values in their place, can miss the bound.
Values may be sent and summed in bfloat16 or wider, within the bound.
A program may use at most 192 MiB of HBM per device.

```python
import math
import jax
import jax.numpy as jnp
import numpy as np
from jax import lax

D = 1024
FF = 4608
CONV = 3
LEN = 1024
MB = 2
BATCH = 8


def level_of(own_key, dims, shards, low, largest):
    level = 1.0
    for dim, shards_of in shards:
        steps = jax.random.uniform(jax.random.fold_in(jax.random.fold_in(own_key, 6), dim), (shards_of,), jnp.float32, low / len(shards), largest / len(shards))
        level = level * jnp.repeat(jnp.exp(steps), dims[dim] // shards_of).reshape((-1,) + (1,) * (len(dims) - 1 - dim))
    return level


def split_up(amount, total, bound, skew):
    portions = [(1 << 20) // math.isqrt(standing ** skew) + 1 for standing in range(2, amount + 1)]
    rest, holding = total - bound - (amount - 1), [1] * (amount - 1)
    while rest > 0:
        free = [i for i in range(amount - 1) if holding[i] < bound]
        pool, budget = sum([portions[i] for i in free]), rest
        for i in free:
            addition = min(bound - holding[i], max(1, budget * portions[i] // pool), rest)
            holding[i] = holding[i] + addition
            rest = rest - addition
    return np.array([bound] + holding)


def ragged(stream_key, number_of, total, limit, skew):
    if number_of == 2:
        one = jax.random.randint(stream_key, (), max(1, total - limit), min(limit, total - 1) + 1)
        return jnp.stack([one, total - one])
    lengths = jnp.asarray(split_up(number_of, total, limit, skew), jnp.int32)
    pairs = (number_of - 1) // 2
    source_of, sink = lengths[1:1 + 2 * pairs:2], lengths[2:2 + 2 * pairs:2]
    room = jnp.minimum(source_of - 1, limit - sink)
    moved = jax.random.randint(jax.random.fold_in(stream_key, 1), (pairs,), 0, 1 << 20) % (room + 1)
    lengths = lengths.at[1:1 + 2 * pairs:2].set(source_of - moved).at[2:2 + 2 * pairs:2].set(sink + moved)
    return lengths[jax.random.permutation(jax.random.fold_in(stream_key, 2), number_of)]


def gaussian(rng, extent, deviation, bound, cuts=(), held_as=jnp.bfloat16):
    level = level_of(rng, extent, cuts, -0.22, 0.18) if cuts else 1.0
    values = jax.random.normal(rng, extent, jnp.float32) * deviation * level
    return jnp.minimum(jnp.maximum(values, -bound), bound).astype(held_as)


def setup_inputs(seed: int = 0) -> dict:
    splits = jax.random.split(jax.random.key(seed), 12)
    tokens = gaussian(splits[0], (MB, BATCH, LEN, D), 1.0, 6.0, ((1, 8), (2, 4)))
    segments = jax.vmap(lambda own: jnp.searchsorted(jnp.cumsum(ragged(own, max(2, LEN // 256), LEN, min(800, LEN - LEN // 8), 1)), jnp.arange(LEN), side="right"))(jax.random.split(splits[1], MB * BATCH)).reshape((MB, BATCH, LEN)).astype(jnp.int32)
    ln1_gain = jnp.clip(1.0 + 0.18 * jax.random.normal(splits[2], (D,), jnp.float32), 0.1, 1.9)
    in_weight = gaussian(splits[3], (D, 3 * D), D ** -0.5, 0.1875, ((0, 32),), jnp.float32)
    conv_kernel = gaussian(splits[4], (CONV, D), 0.6, 3.0, ((1, 32),), jnp.float32)
    out_weight = gaussian(splits[5], (D, D), D ** -0.5, 0.1875, ((0, 32),), jnp.float32)
    ln2_gain = jnp.clip(1.0 + 0.18 * jax.random.normal(splits[6], (D,), jnp.float32), 0.1, 1.9)
    gate_weight = gaussian(splits[7], (D, FF), D ** -0.5, 0.1875, ((0, 32),), jnp.float32)
    up_weight = gaussian(splits[8], (D, FF), D ** -0.5, 0.1875, ((0, 32),), jnp.float32)
    down_weight = gaussian(splits[9], (FF, D), FF ** -0.5, 0.09375, ((0, 32),), jnp.float32)
    cotangent = gaussian(splits[10], (MB, BATCH, LEN, D), 1.0, 6.0, ((1, 8), (2, 4)))
    return {"tokens": tokens, "segments": segments, "ln1_gain": ln1_gain, "in_weight": in_weight, "conv_kernel": conv_kernel, "out_weight": out_weight, "ln2_gain": ln2_gain, "gate_weight": gate_weight, "up_weight": up_weight, "down_weight": down_weight, "cotangent": cotangent}


@jax.custom_vjp
def low(v):
    return lax.optimization_barrier(v.astype(jnp.bfloat16)).astype(jnp.float32)

@jax.custom_vjp
def low_back(v):
    return v

def low_keep(v):
    return (low(v), None)

def low_pass(kept, grad):
    return (grad,)

def back_keep(v):
    return (v, None)

def back_low(kept, grad):
    return (low(grad),)
low.defvjp(low_keep, low_pass)
low_back.defvjp(back_keep, back_low)
eps = 1e-05

def matmul(left, right):
    return jnp.dot(left, right, precision=lax.Precision.HIGHEST)

def rmsnorm(values, gain):
    return values * lax.rsqrt(lax.optimization_barrier(jnp.mean(values * values, axis=-1, keepdims=True)) + eps) * gain

def forward(params, tokens_seq, seg_line):
    gain_one = low(params[0])
    w_in = low(params[1])
    kernel = low(params[2])
    w_out = low(params[3])
    gain_two = low(params[4])
    w_gate = low(params[5])
    w_up = low(params[6])
    w_down = low(params[7])
    hidden_one = low(rmsnorm(tokens_seq, gain_one))
    projected = low_back(matmul(hidden_one, w_in))
    b_part = projected[:, :D]
    c_part = projected[:, D:2 * D]
    x_part = projected[:, 2 * D:]
    mixed = low(b_part * x_part)
    extended = jnp.concatenate([jnp.zeros((2, D), tokens_seq.dtype), mixed], axis=0)
    seg_pad = jnp.concatenate([jnp.full((2,), -1, jnp.int32), seg_line.astype(jnp.int32)])
    conv_out = jnp.zeros_like(mixed)
    for tap in range(CONV):
        same_doc = (seg_pad[tap:tap + LEN] == seg_line).astype(tokens_seq.dtype)
        conv_out = conv_out + kernel[tap] * extended[tap:tap + LEN] * same_doc[:, None]
    conv_out = low_back(conv_out)
    gated = low(c_part * conv_out)
    branch = low_back(matmul(gated, w_out))
    resid = tokens_seq + branch
    hidden_two = low(rmsnorm(resid, gain_two))
    gate_pre = low_back(matmul(hidden_two, w_gate))
    up_pre = low_back(matmul(hidden_two, w_up))
    inner = low(jax.nn.silu(gate_pre) * up_pre)
    ffn_out = low_back(matmul(inner, w_down))
    return resid + ffn_out

def reference(tokens, segments, ln1_gain, in_weight, conv_kernel, out_weight, ln2_gain, gate_weight, up_weight, down_weight, cotangent):
    params = (ln1_gain, in_weight, conv_kernel, out_weight, ln2_gain, gate_weight, up_weight, down_weight)
    count = MB * BATCH
    flat_tokens = tokens.astype(jnp.float32).reshape(count, LEN, D)
    flat_segs = segments.reshape(count, LEN)
    flat_cot = cotangent.astype(jnp.float32).reshape(count, LEN, D)
    zeros = jax.tree.map(jnp.zeros_like, params)

    def visit(carry, item):
        seq_tokens, seq_segs, seq_cot = item
        result, pull = jax.vjp(lambda p, v: forward(p, v, seq_segs), params, seq_tokens)
        grad_params, grad_seq = pull(seq_cot)
        carry = jax.tree.map(jnp.add, carry, grad_params)
        return (carry, (result.astype(jnp.bfloat16), grad_seq.astype(jnp.bfloat16)))
    totals, (outputs, grads) = lax.scan(visit, zeros, (flat_tokens, flat_segs, flat_cot))
    return (outputs.reshape(MB, BATCH, LEN, D), grads.reshape(MB, BATCH, LEN, D), totals[0], totals[1], totals[2], totals[3], totals[4], totals[5], totals[6], totals[7])
```

```python
import functools
import jax
import jax.numpy as jnp
from jax import lax
from jax.experimental import pallas as pl
from jax.experimental.pallas import tpu as pltpu
from jax.sharding import PartitionSpec as P

BF = jnp.bfloat16
F32 = jnp.float32
eps = 1e-05
MESH = pl.DeviceIdType.MESH
NN = (((1,), (0,)), ((), ()))
NT = (((1,), (1,)), ((), ()))
TN = (((0,), (0,)), ((), ()))
TP = 4


def mm(left, right, dims):
    return lax.dot_general(left, right, dims, preferred_element_type=F32)


def when(pred, body):
    if pred is True:
        body()
    else:
        pl.when(pred)(body)


class Place:
    def __init__(self, nz):
        dp = lax.axis_index("dp")
        self.y = dp // TP
        self.i = dp % TP
        self.z = lax.axis_index("seq")
        self.nz = nz
        self.x = self.i // 2
        self.c = self.i % 2

    def member(self, t):
        x = 1 - self.x if t // 2 else self.x
        c = 1 - self.c if t % 2 else self.c
        return x * 2 + c

    def at(self, y=None, i=None, z=None):
        y = self.y if y is None else y
        i = self.i if i is None else i
        z = self.z if z is None else z
        return (y * TP + i, z)


class Copies:
    def __init__(self):
        self.pending = []

    def send(self, src, dst, ssem, rsem, device, pred=True):
        def make():
            return pltpu.make_async_remote_copy(
                src_ref=src, dst_ref=dst, send_sem=ssem, recv_sem=rsem,
                device_id=device, device_id_type=MESH)
        when(pred, lambda: make().start())
        self.pending.append((pred, make))

    def local(self, src, dst, sem):
        pltpu.make_async_copy(src, dst, sem).start()

    def arrived(self, ref, ssem, rsem, device, pred=True):
        when(pred, lambda: pltpu.make_async_remote_copy(
            src_ref=ref, dst_ref=ref, send_sem=ssem, recv_sem=rsem,
            device_id=device, device_id_type=MESH).wait_recv())

    def drain(self, count=None):
        done = self.pending[:count]
        self.pending = self.pending[len(done):]
        for pred, make in done:
            when(pred, lambda make=make: make().wait_send())


def entry_barrier(p):
    bar = pltpu.get_barrier_semaphore()
    for t in range(1, TP):
        pl.semaphore_signal(bar, inc=1, device_id=p.at(i=p.member(t)), device_id_type=MESH)
    pl.semaphore_signal(bar, inc=1, device_id=p.at(y=1 - p.y), device_id_type=MESH)
    for step, pred in ((-1, p.z > 0), (1, p.z < p.nz - 1)):
        pl.when(pred)(lambda step=step: pl.semaphore_signal(
            bar, inc=1, device_id=p.at(z=p.z + step), device_id_type=MESH))
    count = TP + (p.z > 0).astype(jnp.int32) + (p.z < p.nz - 1).astype(jnp.int32)
    pl.semaphore_wait(bar, count)


def ffn_body(parts, nz, h_in, df_in, gus, ds, f_out, dh_out, ogu_out, od_out,
             H, dF, WGU, WD, dHa, Zb, dAb, dGb, GGU, GD, RY, ZGU, OGU, ZD, YD, FD, FIN,
             LX, SX, sem_h, sem_l, s_p0, r_p0, s_z, r_z, s_y, r_y,
             s_dz, r_dz, s_dy, r_dy, s_gy, r_gy, s_gz, r_gz, s_gt, r_gt,
             s_ez, r_ez, s_ey, r_ey, s_x, r_x):
    p = Place(nz)
    z = p.z
    rows = h_in.shape[0]
    width = h_in.shape[1]
    shard = gus.shape[2]
    npos = 2 * nz
    offs = [sum(parts[:k]) for k in range(len(parts))]
    CH = [(offs[k] * npos, parts[k] * npos) for k in range(len(parts))]
    K = len(parts)
    cp = Copies()
    first, last = z == 0, z == nz - 1
    inner_l, inner_r = z > 0, z < nz - 1

    def cols(k):
        return slice(CH[k][0], CH[k][0] + CH[k][1])

    def rws(k):
        return slice(offs[k], offs[k] + parts[k])

    cx = Copies()
    cp.local(h_in, H.at[0], sem_l.at[0])
    cp.local(df_in, dF.at[0], sem_l.at[1])
    cp.local(gus.at[p.i], WGU.at[p.y, p.i, z], sem_l.at[2])
    for k in range(K):
        cp.local(ds.at[rws(k)], WD[k].at[p.y, z], sem_l.at[3 + k])
    entry_barrier(p)

    def p0(k):
        for t in (2, 3, 1):
            m = p.member(t)
            cp.send(gus.at[m, :, :, cols(k)], WGU.at[p.y, p.i, z, :, :, cols(k)],
                    s_p0.at[k, t - 1], r_p0.at[k, t - 1], p.at(i=m))

    def acts(src, dst, q):
        pltpu.make_async_copy(src, dst.at[0], sem_l.at[q]).wait()
        for t in (2, 1):
            cp.send(dst.at[0], dst.at[t], sem_h.at[q, 0, t - 1], sem_h.at[q, 1, t - 1], p.at(i=p.member(t)))

    def acts_wait(dst, q, t):
        cp.arrived(dst.at[t], sem_h.at[q, 0, t - 1], sem_h.at[q, 1, t - 1], p.at(i=p.member(t)))

    def acts_forward(dst, q):
        acts_wait(dst, q, 2)
        cp.send(dst.at[2], dst.at[3], sem_h.at[q, 0, 2], sem_h.at[q, 1, 2], p.at(i=p.member(1)))

    def gu_blk(k, y, zz):
        return WGU.at[y, :, zz, :, :, cols(k)]

    def gu_zsend(k, zz, right):
        pred = inner_r if right else inner_l
        d = 1 if right else 0
        b = gu_blk(k, p.y, zz)
        cp.send(b, b, s_z.at[k, d, zz], r_z.at[k, zz], p.at(z=z + 1 if right else z - 1), pred)

    def gu_ysend(k, zz, pred=True):
        b = gu_blk(k, p.y, zz)
        cp.send(b, b, s_y.at[k, zz], r_y.at[k, zz], p.at(y=1 - p.y), pred)

    def flow_ag_gu(k):
        for t in (1, 2, 3):
            m = p.member(t)
            cp.arrived(WGU.at[p.y, m, z, :, :, cols(k)], s_p0.at[k, t - 1], r_p0.at[k, t - 1], p.at(i=m))
        gu_zsend(k, z, True)
        gu_zsend(k, z, False)
        gu_ysend(k, z)
        for s in range(1, nz):
            for right in (True, False):
                yield
                zz = z - s if right else z + s
                got = zz >= 0 if right else zz <= nz - 1
                more = got & (inner_r if right else inner_l)

                def arrive(zz=zz):
                    cp2 = gu_blk(k, p.y, zz)
                    cp.arrived(cp2, s_z.at[k, 0, zz], r_z.at[k, zz], p.at())
                pl.when(got)(arrive)
                b = gu_blk(k, p.y, zz)
                d = 1 if right else 0
                cp.send(b, b, s_z.at[k, d, zz], r_z.at[k, zz], p.at(z=z + 1 if right else z - 1), more)
                gu_ysend(k, zz, got)
        for zz in range(nz):
            yield
            cp.arrived(gu_blk(k, 1 - p.y, zz), s_y.at[k, zz], r_y.at[k, zz], p.at(y=1 - p.y))

    def flow_ag_d(k):
        W = WD[k]
        own = W.at[p.y, z]
        cp.send(own, own, s_dy.at[k], r_dy.at[k], p.at(y=1 - p.y))

        def zs(y, yi, zz, right, pred):
            b = W.at[y, zz]
            d = 1 if right else 0
            cp.send(b, b, s_dz.at[k, yi, d, zz], r_dz.at[k, yi, zz], p.at(z=z + 1 if right else z - 1), pred)
        zs(p.y, p.y, z, True, inner_r)
        zs(p.y, p.y, z, False, inner_l)
        yield
        cp.arrived(W.at[1 - p.y, z], s_dy.at[k], r_dy.at[k], p.at(y=1 - p.y))
        zs(1 - p.y, 1 - p.y, z, True, inner_r)
        zs(1 - p.y, 1 - p.y, z, False, inner_l)
        for s in range(1, nz):
            for right in (True, False):
                yield
                zz = z - s if right else z + s
                got = zz >= 0 if right else zz <= nz - 1
                more = got & (inner_r if right else inner_l)
                for y in (p.y, 1 - p.y):
                    pl.when(got)(lambda y=y, zz=zz: cp.arrived(
                        W.at[y, zz], s_dz.at[k, y, 0, zz], r_dz.at[k, y, zz], p.at()))
                    zs(y, y, zz, right, more)

    order = [nz - 1, 0] + list(range(1, nz - 1))[::-1]

    def flow_rs_gu(k):
        c = cols(k)
        for zz in order:
            cp.send(GGU.at[1 - p.y, :, zz, :, :, c], RY.at[:, zz, :, :, c],
                    s_gy.at[k, zz], r_gy.at[k, zz], p.at(y=1 - p.y))

        def ry_wait(zz):
            cp.arrived(RY.at[:, zz, :, :, c], s_gy.at[k, zz], r_gy.at[k, zz], p.at(y=1 - p.y))

        def zwait(sl):
            cp.arrived(ZGU.at[sl, :, :, :, c], s_gz.at[k, 0, 0], r_gz.at[k, sl], p.at())
        for zz in order:
            yield
            right, left = z < zz, z > zz
            ry_wait(zz)
            both = (right & inner_l) | (left & inner_r)

            def add3(zz=zz):
                zwait(zz)
                for j in range(TP):
                    GGU[p.y, j, zz, :, :, c] = (
                        GGU[p.y, j, zz, :, :, c].astype(F32) + RY[j, zz, :, :, c].astype(F32)
                        + ZGU[zz, j, :, :, c].astype(F32)).astype(BF)

            def add2(zz=zz):
                for j in range(TP):
                    GGU[p.y, j, zz, :, :, c] = (
                        GGU[p.y, j, zz, :, :, c].astype(F32) + RY[j, zz, :, :, c].astype(F32)).astype(BF)
            pl.when(both)(add3)
            pl.when(jnp.logical_and(z != zz, jnp.logical_not(both)))(add2)
            src = GGU.at[p.y, :, zz, :, :, c]
            sl_r = zz
            cp.send(src, ZGU.at[sl_r, :, :, :, c], s_gz.at[k, 1, zz], r_gz.at[k, sl_r], p.at(z=z + 1), right)
            sl_l = jnp.where(z - 1 == zz, nz, zz)
            cp.send(src, ZGU.at[sl_l, :, :, :, c], s_gz.at[k, 0, zz], r_gz.at[k, sl_l], p.at(z=z - 1), left)
        yield
        pl.when(inner_l)(lambda: zwait(z))
        pl.when(inner_r)(lambda: zwait(nz))
        for j in range(TP):
            FIN[j, :, :, c] = (
                GGU[p.y, j, z, :, :, c].astype(F32) + RY[j, z, :, :, c].astype(F32)
                + ZGU[z, j, :, :, c].astype(F32) + ZGU[nz, j, :, :, c].astype(F32)).astype(BF)
        for t in (2, 3, 1):
            m = p.member(t)
            cp.send(FIN.at[m, :, :, c], OGU.at[p.i, :, :, c], s_gt.at[k, t - 1], r_gt.at[k, t - 1], p.at(i=m))
        OGU[p.i, :, :, c] = FIN[p.i, :, :, c]
        yield
        for t in (1, 2, 3):
            m = p.member(t)
            cp.arrived(OGU.at[m, :, :, c], s_gt.at[k, t - 1], r_gt.at[k, t - 1], p.at(i=m))

    def flow_rs_d(k):
        G, L = GD[k], ZD[k]

        def zwait(sl):
            cp.arrived(L.at[sl], s_ez.at[k, 0, 0], r_ez.at[k, sl], p.at())
        for zz in order:
            yield
            right, left = z < zz, z > zz
            both = (right & inner_l) | (left & inner_r)

            def add2(zz=zz):
                zwait(zz)
                for y in range(2):
                    G[y, zz] = (G[y, zz].astype(F32) + L[zz, y].astype(F32)).astype(BF)
            pl.when(both)(add2)
            src = G.at[:, zz]
            cp.send(src, L.at[zz], s_ez.at[k, 1, zz], r_ez.at[k, zz], p.at(z=z + 1), right)
            sl_l = jnp.where(z - 1 == zz, nz, zz)
            cp.send(src, L.at[sl_l], s_ez.at[k, 0, zz], r_ez.at[k, sl_l], p.at(z=z - 1), left)
        yield
        pl.when(inner_l)(lambda: zwait(z))
        pl.when(inner_r)(lambda: zwait(nz))
        for y in range(2):
            FD[k][y] = (G[y, z].astype(F32) + L[z, y].astype(F32) + L[nz, y].astype(F32)).astype(BF)
        cp.send(FD[k].at[1 - p.y], YD[k], s_ey.at[k], r_ey.at[k], p.at(y=1 - p.y))
        yield
        cp.arrived(YD[k], s_ey.at[k], r_ey.at[k], p.at(y=1 - p.y))
        od_out[rws(k), :] = FD[k][p.y].astype(F32) + YD[k][...].astype(F32)

    def zero_left():
        ZGU[0] = jnp.zeros(ZGU.shape[1:], BF)
        for k in range(K):
            ZD[k][0] = jnp.zeros(ZD[k].shape[1:], BF)

    def zero_right():
        ZGU[nz] = jnp.zeros(ZGU.shape[1:], BF)
        for k in range(K):
            ZD[k][nz] = jnp.zeros(ZD[k].shape[1:], BF)

    for k in range(K):
        p0(k)
    acts(h_in, H, 0)
    acts(df_in, dF, 1)
    pl.when(first)(zero_left)
    pl.when(last)(zero_right)
    pltpu.make_async_copy(gus.at[p.i], WGU.at[p.y, p.i, z], sem_l.at[2]).wait()
    for k in range(K):
        pltpu.make_async_copy(ds.at[rws(k)], WD[k].at[p.y, z], sem_l.at[3 + k]).wait()

    flows = []

    def pump(n=1):
        for _ in range(n):
            for f in list(flows):
                if next(f, "end") == "end":
                    flows.remove(f)

    def run(gen):
        for _ in gen:
            pass
        if gen in flows:
            flows.remove(gen)

    ag = [(flow_ag_gu(k), flow_ag_d(k)) for k in range(K)]
    live = []
    for k in range(K):
        for g in ag[k]:
            next(g)
            flows.append(g)
        if k < K - 1:
            pump(2)
    acts_forward(H, 0)
    acts_forward(dF, 1)

    def fwd_mid(k, t):
        c0, cn = CH[k]
        c = cols(k)
        wg = WGU[:, :, :, 0, :, c].reshape(width, cn)
        wu = WGU[:, :, :, 1, :, c].reshape(width, cn)
        wd = WD[k][...].reshape(cn, width)
        a = mm(H[t], wg, NN)
        g = mm(H[t], wu, NN)
        dz = mm(dF[t], wd, NT)
        sg = 1.0 / (1.0 + jnp.exp(-a))
        act = a * sg
        Zb[t, :, c] = (act * g).astype(BF)
        dAb[t, :, :cn] = (dz * g * sg * (1.0 + a * (1.0 - sg))).astype(BF)
        dGb[t, :, :cn] = (dz * act).astype(BF)
        d = mm(dAb[t, :, :cn], wg, NT) + mm(dGb[t, :, :cn], wu, NT)
        if k == 0:
            dHa[t] = d
        else:
            dHa[t] += d

    def ffn_out(t):
        f = None
        for k in range(K):
            v = mm(Zb[t, :, cols(k)], WD[k][...].reshape(CH[k][1], width), NN)
            f = v if f is None else f + v
        return f

    def grads(k):
        c0, cn = CH[k]
        c = cols(k)
        tok = TP * rows
        for w, src in ((0, dAb), (1, dGb)):
            def body(m, _, w=w, src=src):
                y, j = m // 2, (m % 2) * 2
                f = 2 * nz * shard
                ms = pl.ds(pl.multiple_of(m * f, f), f)
                v = mm(H[:, :, ms].reshape(tok, f), src[:, :, :cn].reshape(tok, cn), TN)
                GGU[y, pl.ds(j, 2), :, w, :, c] = v.astype(BF).reshape(2, nz, shard, cn)
                return 0
            lax.fori_loop(0, TP, body, 0)
        r = parts[k]
        for b in range(cn // 128):
            v = mm(Zb[:, :, c0 + b * 128:c0 + (b + 1) * 128].reshape(tok, 128), dF[...].reshape(tok, width), TN).astype(BF)
            lo = b * 128
            while lo < (b + 1) * 128:
                pos, q = lo // r, lo % r
                n = min(r - q, (b + 1) * 128 - lo)
                GD[k][pos // nz, pos % nz, q:q + n] = v[lo - b * 128:lo - b * 128 + n]
                lo += n

    def x_send1(q, e, value):
        SX[e] = value.astype(BF)
        cx.send(SX.at[e], LX.at[q, e], s_x.at[q, e], r_x.at[q, e], p.at(i=p.member(1)))

    def x_wait(q, e):
        cx.arrived(LX.at[q, e], s_x.at[q, e], r_x.at[q, e], p.at(i=p.member(2 if e == 2 else 1)))

    def x_send2(q, acc):
        x_wait(q, 1)
        SX[2] = (acc[...] + LX[q, 1].astype(F32)).astype(BF)
        cx.send(SX.at[2], LX.at[q, 2], s_x.at[q, 2], r_x.at[q, 2], p.at(i=p.member(2)))

    def x_final(q, acc, out):
        x_wait(q, 0)
        x_wait(q, 2)
        acc[...] += LX[q, 0].astype(F32) + LX[q, 2].astype(F32)
        pltpu.make_async_copy(acc, out, sem_l.at[q]).start()

    for k in range(K):
        for g in ag[k]:
            run(g)
        if k == 0:
            for t in (1, 3):
                for q, dst in ((0, H), (1, dF)):
                    acts_wait(dst, q, t)

        def tbody(n, _, k=k):
            fwd_mid(k, n)
            return 0
        lax.fori_loop(0, TP, tbody, 0)
        pump(2)
        if k == K - 1:
            x_send1(0, 0, dHa[1])
            x_send1(0, 1, dHa[3])
        grads(k)
        for g in (flow_rs_d(k), flow_rs_gu(k)):
            next(g)
            flows.append(g)
        pump(1)
    x_send2(0, dHa.at[2])
    pump(1)
    cx.drain(2)
    x_send1(1, 0, ffn_out(1))
    x_send1(1, 1, ffn_out(3))
    pump(1)
    dHa[1] = ffn_out(2)
    dHa[3] = ffn_out(0)
    pump(1)
    x_final(0, dHa.at[0], dh_out)
    cx.drain(1)
    x_send2(1, dHa.at[1])
    while flows:
        pump(1)
    x_final(1, dHa.at[3], f_out)
    ogu_out[...] = OGU[...]
    pltpu.make_async_copy(dHa.at[0], dh_out, sem_l.at[0]).wait()
    pltpu.make_async_copy(dHa.at[3], f_out, sem_l.at[1]).wait()
    cp.drain()
    cx.drain()


def ffn_call(h, df, gus, ds, parts, nz, cid):
    rows, width = h.shape
    shard, cols = gus.shape[2], gus.shape[3]
    K = len(parts)
    dr = ds.shape[0]
    V = pl.BlockSpec(memory_space=pltpu.VMEM)
    A = pl.BlockSpec(memory_space=pl.ANY)
    D = pltpu.SemaphoreType.DMA
    maxc = max(parts) * 2 * nz
    scratch = [
        pltpu.VMEM((TP, rows, width), BF),
        pltpu.VMEM((TP, rows, width), BF),
        pltpu.VMEM((2, TP, nz, 2, shard, cols), BF),
        [pltpu.VMEM((2, nz, r, width), BF) for r in parts],
        pltpu.VMEM((TP, rows, width), F32),
        pltpu.VMEM((TP, rows, cols), BF),
        pltpu.VMEM((TP, rows, maxc), BF),
        pltpu.VMEM((TP, rows, maxc), BF),
        pltpu.VMEM((2, TP, nz, 2, shard, cols), BF),
        [pltpu.VMEM((2, nz, r, width), BF) for r in parts],
        pltpu.VMEM((TP, nz, 2, shard, cols), BF),
        pltpu.VMEM((nz + 1, TP, 2, shard, cols), BF),
        pltpu.VMEM((TP, 2, shard, cols), BF),
        [pltpu.VMEM((nz + 1, 2, r, width), BF) for r in parts],
        [pltpu.VMEM((r, width), BF) for r in parts],
        [pltpu.VMEM((2, r, width), BF) for r in parts],
        pltpu.VMEM((TP, 2, shard, cols), BF),
        pltpu.VMEM((2, 3, rows, width), BF),
        pltpu.VMEM((3, rows, width), BF),
        D((2, 2, 3)), D((3 + K,)),
        D((K, 3)), D((K, 3)),
        D((K, 2, nz)), D((K, nz)), D((K, nz)), D((K, nz)),
        D((K, 2, 2, nz)), D((K, 2, nz)), D((K,)), D((K,)),
        D((K, nz)), D((K, nz)), D((K, 2, nz)), D((K, nz + 1)), D((K, 3)), D((K, 3)),
        D((K, 2, nz)), D((K, nz + 1)), D((K,)), D((K,)),
        D((2, 3)), D((2, 3)),
    ]
    return pl.pallas_call(
        functools.partial(ffn_body, parts, nz),
        name="ffn",
        out_shape=(
            jax.ShapeDtypeStruct((rows, width), F32),
            jax.ShapeDtypeStruct((rows, width), F32),
            jax.ShapeDtypeStruct((TP, 2, shard, cols), BF),
            jax.ShapeDtypeStruct((dr, width), F32),
        ),
        in_specs=[A, A, V, V],
        out_specs=[A, A, V, V],
        scratch_shapes=scratch,
        compiler_params=pltpu.CompilerParams(
            collective_id=cid, has_side_effects=True, vmem_limit_bytes=66_900_000),
    )(h, df, gus, ds)


def shifted(block, axis, distance):
    devices = range(lax.axis_size(axis))
    route = [(i - distance, i) for i in devices if i - distance in devices]
    return lax.ppermute(block, axis, route)


def matmul(left, right):
    return jnp.dot(left, right, preferred_element_type=jnp.float32)


def norm_parts(values):
    inverse = lax.rsqrt(jnp.mean(values * values, axis=-1, keepdims=True) + eps)
    return (inverse, values * inverse)


def norm_back(grad_hidden, normed, inverse, gain):
    grad_normed = grad_hidden * gain
    inner_mean = jnp.mean(grad_normed * normed, axis=-1, keepdims=True)
    return inverse * (grad_normed - normed * inner_mean)


def plain_device(
    tokens,
    segments,
    ln1_gain,
    in_weight,
    conv_kernel,
    out_weight,
    ln2_gain,
    gate_weight,
    up_weight,
    down_weight,
    cotangent,
):
    micro_count = tokens.shape[0]
    row_count = tokens.shape[2]
    width = tokens.shape[3]
    taps = conv_kernel.shape[0]
    offset = lax.axis_index("seq") * row_count
    low_gain1 = ln1_gain.astype(jnp.bfloat16)
    low_in = in_weight.astype(jnp.bfloat16)
    low_kernel = conv_kernel.astype(jnp.bfloat16)
    low_out = out_weight.astype(jnp.bfloat16)
    low_gain2 = ln2_gain.astype(jnp.bfloat16)
    low_gate = gate_weight.astype(jnp.bfloat16)
    low_up = up_weight.astype(jnp.bfloat16)
    low_down = down_weight.astype(jnp.bfloat16)
    shard_totals = None
    full_totals = None
    out_list = []
    grad_list = []
    for micro_index in range(micro_count):
        weights = (
            lax.all_gather(low_gain1, ("dp", "seq"), axis=0, tiled=True),
            lax.all_gather(low_in, ("dp", "seq"), axis=0, tiled=True),
            lax.all_gather(low_kernel, ("dp", "seq"), axis=1, tiled=True),
            lax.all_gather(low_out, ("dp", "seq"), axis=0, tiled=True),
            lax.all_gather(low_gain2, ("dp", "seq"), axis=0, tiled=True),
            lax.all_gather(low_gate, ("dp", "seq"), axis=0, tiled=True),
            lax.all_gather(low_up, ("dp", "seq"), axis=0, tiled=True),
            lax.all_gather(low_down, ("dp", "seq"), axis=0, tiled=True),
        )
        gain_one = weights[0].astype(jnp.float32)
        kernel = weights[2].astype(jnp.float32)
        gain_two = weights[4].astype(jnp.float32)
        seg_line = segments[micro_index, 0]
        fill = jnp.full((2,), -1, jnp.int32)
        seg_pad = jnp.concatenate([fill, seg_line, fill])
        window = lax.dynamic_slice_in_dim(seg_pad, offset, row_count + 4)
        masks = [
            (window[tap : tap + row_count + 2] == window[2 : row_count + 4]).astype(jnp.float32)
            for tap in range(taps)
        ]
        tokens_f = tokens[micro_index, 0].astype(jnp.float32)
        inverse_one, normed_one = norm_parts(tokens_f)
        hidden_one = (normed_one * gain_one).astype(jnp.bfloat16)
        projected = matmul(hidden_one, weights[1])
        b_part = projected[:, :width]
        c_part = projected[:, width : 2 * width]
        x_part = projected[:, 2 * width :]
        mixed = (b_part * x_part).astype(jnp.bfloat16)
        prev_rows = shifted(mixed[row_count - 2 :], "seq", 1)
        extended = jnp.concatenate([prev_rows, mixed], axis=0).astype(jnp.float32)
        conv_out = jnp.zeros((row_count, width), jnp.float32)
        for tap in range(taps):
            conv_out = (
                conv_out
                + kernel[tap] * extended[tap : tap + row_count] * masks[tap][:row_count, None]
            )
        gated = (c_part * conv_out).astype(jnp.bfloat16)
        resid = tokens_f + matmul(gated, weights[3])
        inverse_two, normed_two = norm_parts(resid)
        hidden_two = (normed_two * gain_two).astype(jnp.bfloat16)
        gate_pre = matmul(hidden_two, weights[5])
        up_pre = matmul(hidden_two, weights[6])
        sigmoid_gate = jax.nn.sigmoid(gate_pre)
        activated = gate_pre * sigmoid_gate
        inner = (activated * up_pre).astype(jnp.bfloat16)
        ffn_out = matmul(inner, weights[7])
        out_list.append((resid + ffn_out).astype(jnp.bfloat16))
        back_weights = (
            lax.all_gather(low_gain1, ("dp", "seq"), axis=0, tiled=True),
            lax.all_gather(low_in, ("dp", "seq"), axis=0, tiled=True),
            lax.all_gather(low_kernel, ("dp", "seq"), axis=1, tiled=True),
            lax.all_gather(low_out, ("dp", "seq"), axis=0, tiled=True),
            lax.all_gather(low_gain2, ("dp", "seq"), axis=0, tiled=True),
            lax.all_gather(low_gate, ("dp", "seq"), axis=0, tiled=True),
            lax.all_gather(low_up, ("dp", "seq"), axis=0, tiled=True),
            lax.all_gather(low_down, ("dp", "seq"), axis=0, tiled=True),
        )
        grad_final = cotangent[micro_index, 0]
        grad_inner = matmul(grad_final, back_weights[7].T)
        part_down = matmul(inner.T, grad_final)
        grad_gate_pre = (
            grad_inner * up_pre * sigmoid_gate * (1.0 + gate_pre * (1.0 - sigmoid_gate))
        ).astype(jnp.bfloat16)
        grad_up_pre = (grad_inner * activated).astype(jnp.bfloat16)
        grad_hidden_two = matmul(grad_gate_pre, back_weights[5].T) + matmul(
            grad_up_pre, back_weights[6].T
        )
        part_gate = matmul(hidden_two.T, grad_gate_pre)
        part_up = matmul(hidden_two.T, grad_up_pre)
        part_gain2 = jnp.sum(grad_hidden_two * normed_two, axis=0)
        grad_resid = grad_final.astype(jnp.float32) + norm_back(
            grad_hidden_two, normed_two, inverse_two, gain_two
        )
        grad_branch = grad_resid.astype(jnp.bfloat16)
        grad_gated = matmul(grad_branch, back_weights[3].T)
        part_out = matmul(gated.T, grad_branch)
        grad_c = grad_gated * conv_out
        grad_conv = (grad_gated * c_part).astype(jnp.bfloat16)
        next_rows = shifted(grad_conv[:2], "seq", -1)
        grad_extended = jnp.concatenate([grad_conv, next_rows], axis=0).astype(jnp.float32)
        grad_mixed = jnp.zeros((row_count, width), jnp.float32)
        kernel_terms = []
        for tap in range(taps):
            weighted = grad_extended * masks[tap][:, None]
            grad_mixed = grad_mixed + kernel[tap] * weighted[2 - tap : 2 - tap + row_count]
            kernel_terms.append(
                jnp.sum(weighted[:row_count] * extended[tap : tap + row_count], axis=0)
            )
        part_kernel = jnp.stack(kernel_terms, axis=0)
        grad_proj = jnp.concatenate(
            [grad_mixed * x_part, grad_c, grad_mixed * b_part], axis=1
        ).astype(jnp.bfloat16)
        grad_hidden_one = matmul(grad_proj, back_weights[1].T)
        part_in = matmul(hidden_one.T, grad_proj)
        part_gain1 = jnp.sum(grad_hidden_one * normed_one, axis=0)
        grad_input = grad_resid + norm_back(grad_hidden_one, normed_one, inverse_one, gain_one)
        grad_list.append(grad_input.astype(jnp.bfloat16))
        parts = (
            part_gain1,
            part_in,
            part_kernel,
            part_out,
            part_gain2,
            part_gate,
            part_up,
            part_down,
        )
        full_totals = (
            parts
            if full_totals is None
            else tuple((first + second for first, second in zip(full_totals, parts)))
        )
    shard_totals = (
        lax.psum_scatter(full_totals[0], ("dp", "seq"), scatter_dimension=0, tiled=True),
        lax.psum_scatter(full_totals[1], ("dp", "seq"), scatter_dimension=0, tiled=True),
        lax.psum_scatter(full_totals[2], ("dp", "seq"), scatter_dimension=1, tiled=True),
        lax.psum_scatter(full_totals[3], ("dp", "seq"), scatter_dimension=0, tiled=True),
        lax.psum_scatter(full_totals[4], ("dp", "seq"), scatter_dimension=0, tiled=True),
        lax.psum_scatter(full_totals[5], ("dp", "seq"), scatter_dimension=0, tiled=True),
        lax.psum_scatter(full_totals[6], ("dp", "seq"), scatter_dimension=0, tiled=True),
        lax.psum_scatter(full_totals[7], ("dp", "seq"), scatter_dimension=0, tiled=True),
    )
    output = jnp.stack(out_list, axis=0)[:, None]
    grad_tokens = jnp.stack(grad_list, axis=0)[:, None]
    return (
        output,
        grad_tokens,
        shard_totals[0],
        shard_totals[1],
        shard_totals[2],
        shard_totals[3],
        shard_totals[4],
        shard_totals[5],
        shard_totals[6],
        shard_totals[7],
    )


def cut_columns(w, parts, ny, nz):
    rows, shard = w.shape[0], w.shape[1] // (ny * TP * nz)
    cut = w.astype(BF).reshape(rows, ny, TP, nz, shard)
    pieces, start = [], 0
    for size in parts:
        piece = cut[..., start : start + size].transpose(2, 0, 1, 3, 4)
        pieces.append(piece.reshape(TP, rows, ny * nz * size))
        start += size
    return jnp.concatenate(pieces, axis=-1)


def join_columns(g, parts, ny, nz):
    rows = g.shape[1]
    pieces, start, npos = [], 0, ny * nz
    for size in parts:
        piece = g[:, :, npos * start : npos * (start + size)].reshape(TP, rows, ny, nz, size)
        pieces.append(piece.transpose(1, 2, 0, 3, 4))
        start += size
    return jnp.concatenate(pieces, axis=-1).reshape(rows, -1).astype(F32)


def fast_device(
    parts,
    tokens,
    segments,
    ln1_gain,
    in_weight,
    conv_kernel,
    out_weight,
    ln2_gain,
    gate_weight,
    up_weight,
    down_weight,
    cotangent,
):
    micro, _, count, width = tokens.shape
    taps = conv_kernel.shape[0]
    nz = lax.axis_size("seq")
    ny = lax.axis_size("dp") // TP
    rows = micro * count
    both = ("dp", "seq")
    x = tokens.reshape(rows, width).astype(F32)
    w_in = lax.all_gather(in_weight.astype(BF), both, axis=0, tiled=True)
    w_out = lax.all_gather(out_weight.astype(BF), both, axis=0, tiled=True)
    small = jnp.concatenate([ln1_gain[None], ln2_gain[None], conv_kernel], axis=0).astype(BF)
    small = lax.all_gather(small, both, axis=1, tiled=True).astype(F32)
    gain_one, gain_two, kernel = small[0], small[1], small[2:]

    offset = lax.axis_index("seq") * count
    fill = jnp.full((micro, 2), -1, jnp.int32)
    seg_pad = jnp.concatenate([fill, segments[:, 0], fill], axis=1)
    window = lax.dynamic_slice_in_dim(seg_pad, offset, count + 4, axis=1)
    masks = [
        (window[:, tap : tap + count + 2] == window[:, 2 : count + 4]).astype(F32)[..., None]
        for tap in range(taps)
    ]
    inv1, norm1 = norm_parts(x)
    h1 = (norm1 * gain_one).astype(BF)
    proj = matmul(h1, w_in)
    b, c, u = (proj[:, k * width : (k + 1) * width] for k in range(3))
    mixed = (b * u).astype(BF).reshape(micro, count, width)
    prev = shifted(mixed[:, count - 2 :], "seq", 1)
    ext = jnp.concatenate([prev, mixed], axis=1).astype(F32)
    conv = sum(kernel[t] * ext[:, t : t + count] * masks[t][:, :count] for t in range(taps))
    conv = conv.reshape(rows, width)
    gated = (c * conv).astype(BF)
    resid = x + matmul(gated, w_out)
    inv2, norm2 = norm_parts(resid)
    h2 = (norm2 * gain_two).astype(BF)

    df = cotangent.reshape(rows, width)
    gus = jnp.stack([cut_columns(gate_weight, parts, ny, nz), cut_columns(up_weight, parts, ny, nz)], axis=1)
    f, dh2, gu, gd = ffn_call(h2, df, gus, down_weight.astype(BF), parts, nz, 0)
    output = (resid + f).astype(BF)
    g_gate = join_columns(gu[:, 0], parts, ny, nz)
    g_up = join_columns(gu[:, 1], parts, ny, nz)

    g_gain2 = jnp.sum(dh2 * norm2, axis=0)
    dr = df.astype(F32) + norm_back(dh2, norm2, inv2, gain_two)
    do = dr.astype(BF)
    dy = matmul(do, w_out.T)
    g_out = matmul(gated.T, do)
    dc = dy * conv
    dconv = (dy * c).astype(BF).reshape(micro, count, width)
    after = shifted(dconv[:, :2], "seq", -1)
    gext = jnp.concatenate([dconv, after], axis=1).astype(F32)
    dmix = jnp.zeros((micro, count, width), F32)
    kterms = []
    for t in range(taps):
        weighted = gext * masks[t]
        dmix = dmix + kernel[t] * weighted[:, 2 - t : 2 - t + count]
        kterms.append(jnp.sum(weighted[:, :count] * ext[:, t : t + count], axis=(0, 1)))
    dmix = dmix.reshape(rows, width)
    dproj = jnp.concatenate([dmix * u, dc, dmix * b], axis=1).astype(BF)
    dh1 = matmul(dproj, w_in.T)
    g_in = matmul(h1.T, dproj)
    g_gain1 = jnp.sum(dh1 * norm1, axis=0)
    gx = (dr + norm_back(dh1, norm1, inv1, gain_one)).astype(BF)
    g_small = jnp.stack([g_gain1, g_gain2] + kterms, axis=0)
    g_small = lax.psum_scatter(g_small, both, scatter_dimension=1, tiled=True)
    g_in = lax.psum_scatter(g_in, both, scatter_dimension=0, tiled=True)
    g_out = lax.psum_scatter(g_out, both, scatter_dimension=0, tiled=True)
    shape = tokens.shape
    return (
        output.reshape(shape), gx.reshape(shape), g_small[0], g_in, g_small[2:], g_out,
        g_small[1], g_gate, g_up, gd,
    )


def row_parts(mesh, down_shape):
    nd, nz = mesh.shape["dp"], mesh.shape["seq"]
    if nd != 2 * TP:
        return None
    per = down_shape[0] // (nd * nz)
    if per % 16:
        return None
    sizes, left = [], per
    while left:
        sizes.append(min(64, left))
        left -= sizes[-1]
    return tuple(sizes)


def solution(mesh):
    in_specs = (
        P(None, "dp", "seq", None),
        P(None, "dp", None),
        P(("dp", "seq")),
        P(("dp", "seq"), None),
        P(None, ("dp", "seq")),
        P(("dp", "seq"), None),
        P(("dp", "seq")),
        P(("dp", "seq"), None),
        P(("dp", "seq"), None),
        P(("dp", "seq"), None),
        P(None, "dp", "seq", None),
    )
    out_specs = (
        P(None, "dp", "seq", None),
        P(None, "dp", "seq", None),
        P(("dp", "seq")),
        P(("dp", "seq"), None),
        P(None, ("dp", "seq")),
        P(("dp", "seq"), None),
        P(("dp", "seq")),
        P(("dp", "seq"), None),
        P(("dp", "seq"), None),
        P(("dp", "seq"), None),
    )

    def run(*arrays):
        parts = row_parts(mesh, arrays[9].shape)
        device = plain_device if parts is None else functools.partial(fast_device, parts)
        return jax.shard_map(
            device, mesh=mesh, in_specs=in_specs, out_specs=out_specs, check_vma=False
        )(*arrays)

    return run
```

```python
import functools
import jax
import jax.numpy as jnp
from jax import lax
from jax.experimental import pallas as pl
from jax.experimental.pallas import tpu as pltpu
from jax.sharding import PartitionSpec as P

BF = jnp.bfloat16
F32 = jnp.float32
eps = 1e-05
MESH = pl.DeviceIdType.MESH
NN = (((1,), (0,)), ((), ()))
NT = (((1,), (1,)), ((), ()))
TN = (((0,), (0,)), ((), ()))
TP = 4
LANES = 128


def mm(left, right, dims):
    return lax.dot_general(left, right, dims, preferred_element_type=F32)


def when(pred, body):
    if pred is True:
        body()
    else:
        pl.when(pred)(body)


class Place:
    def __init__(self, nz):
        dp = lax.axis_index("dp")
        self.y = dp // TP
        self.i = dp % TP
        self.z = lax.axis_index("seq")
        self.nz = nz
        self.x = self.i // 2
        self.c = self.i % 2

    def member(self, t):
        x = 1 - self.x if t // 2 else self.x
        c = 1 - self.c if t % 2 else self.c
        return x * 2 + c

    def at(self, y=None, i=None, z=None):
        y = self.y if y is None else y
        i = self.i if i is None else i
        z = self.z if z is None else z
        return (y * TP + i, z)


class Copies:
    def __init__(self):
        self.pending = []

    def send(self, src, dst, ssem, rsem, device, pred=True, group=None):
        def make():
            return pltpu.make_async_remote_copy(
                src_ref=src, dst_ref=dst, send_sem=ssem, recv_sem=rsem,
                device_id=device, device_id_type=MESH)
        when(pred, lambda: make().start())
        if group is None:
            self.pending.append((pred, make))

    def local(self, src, dst, sem):
        pltpu.make_async_copy(src, dst, sem).start()

    def arrived(self, ref, ssem, rsem, device, pred=True):
        when(pred, lambda: pltpu.make_async_remote_copy(
            src_ref=ref, dst_ref=ref, send_sem=ssem, recv_sem=rsem,
            device_id=device, device_id_type=MESH).wait_recv())

    def drain(self, count=None):
        done = self.pending[:count]
        self.pending = self.pending[len(done):]
        for pred, make in done:
            when(pred, lambda make=make: make().wait_send())


def entry_barrier(p):
    bar = pltpu.get_barrier_semaphore()
    for t in range(1, TP):
        pl.semaphore_signal(bar, inc=1, device_id=p.at(i=p.member(t)), device_id_type=MESH)
    pl.semaphore_signal(bar, inc=1, device_id=p.at(y=1 - p.y), device_id_type=MESH)
    for step, pred in ((-1, p.z > 0), (1, p.z < p.nz - 1)):
        pl.when(pred)(lambda step=step: pl.semaphore_signal(
            bar, inc=1, device_id=p.at(z=p.z + step), device_id_type=MESH))
    count = TP + (p.z > 0).astype(jnp.int32) + (p.z < p.nz - 1).astype(jnp.int32)
    pl.semaphore_wait(bar, count)


def ffn_body(parts, nz, h_in, df_in, gus, ds, f_out, dh_out, ogu_out, od_out,
             H, dF, WGU, WD, dHa, Zb, dAb, dGb, GGU, GD, RY, ZGU, OGU, ZD, YD, FD, FIN,
             LX, SX, sem_h, sem_l, s_p0, r_p0, s_z, r_z, s_y, r_y,
             s_dz, r_dz, s_dy, r_dy, s_gy, r_gy, s_gz, r_gz, s_gt, r_gt,
             s_ez, r_ez, s_ey, r_ey, s_x, r_x):
    p = Place(nz)
    z = p.z
    rows = h_in.shape[0]
    width = h_in.shape[1]
    shard = gus.shape[2]
    npos = 2 * nz
    offs = [sum(parts[:k]) for k in range(len(parts))]
    CH = [(offs[k] * npos, parts[k] * npos) for k in range(len(parts))]
    K = len(parts)
    cp = Copies()
    first, last = z == 0, z == nz - 1
    inner_l, inner_r = z > 0, z < nz - 1

    def cols(k):
        return slice(CH[k][0], CH[k][0] + CH[k][1])

    def rws(k):
        return slice(offs[k], offs[k] + parts[k])

    cx = Copies()
    cp.local(h_in, H.at[0], sem_l.at[0])
    cp.local(df_in, dF.at[0], sem_l.at[1])
    cp.local(gus.at[p.i], WGU.at[p.y, p.i, z], sem_l.at[2])
    for k in range(K):
        cp.local(ds.at[rws(k)], WD[k].at[p.y, z], sem_l.at[3 + k])
    entry_barrier(p)

    def p0(k):
        for t in (2, 3, 1):
            m = p.member(t)
            cp.send(gus.at[m, :, :, cols(k)], WGU.at[p.y, p.i, z, :, :, cols(k)],
                    s_p0.at[k, t - 1], r_p0.at[k, t - 1], p.at(i=m))

    def acts(src, dst, q):
        pltpu.make_async_copy(src, dst.at[0], sem_l.at[q]).wait()
        for t in (2, 1):
            cp.send(dst.at[0], dst.at[t], sem_h.at[q, 0, t - 1], sem_h.at[q, 1, t - 1], p.at(i=p.member(t)))

    def acts_wait(dst, q, t):
        cp.arrived(dst.at[t], sem_h.at[q, 0, t - 1], sem_h.at[q, 1, t - 1], p.at(i=p.member(t)))

    def acts_forward(dst, q):
        acts_wait(dst, q, 2)
        cp.send(dst.at[2], dst.at[3], sem_h.at[q, 0, 2], sem_h.at[q, 1, 2], p.at(i=p.member(1)))

    def gu_blk(k, y, zz):
        return WGU.at[y, :, zz, :, :, cols(k)]

    def gu_zsend(k, zz, right):
        pred = inner_r if right else inner_l
        d = 1 if right else 0
        b = gu_blk(k, p.y, zz)
        cp.send(b, b, s_z.at[k, d, zz], r_z.at[k, zz], p.at(z=z + 1 if right else z - 1), pred)

    def gu_ysend(k, zz, pred=True):
        b = gu_blk(k, p.y, zz)
        cp.send(b, b, s_y.at[k, zz], r_y.at[k, zz], p.at(y=1 - p.y), pred)

    def flow_ag_gu(k):
        for t in (1, 2, 3):
            m = p.member(t)
            cp.arrived(WGU.at[p.y, m, z, :, :, cols(k)], s_p0.at[k, t - 1], r_p0.at[k, t - 1], p.at(i=m))
        gu_zsend(k, z, True)
        gu_zsend(k, z, False)
        gu_ysend(k, z)
        for s in range(1, nz):
            for right in (True, False):
                yield
                zz = z - s if right else z + s
                got = zz >= 0 if right else zz <= nz - 1
                more = got & (inner_r if right else inner_l)

                def arrive(zz=zz):
                    cp2 = gu_blk(k, p.y, zz)
                    cp.arrived(cp2, s_z.at[k, 0, zz], r_z.at[k, zz], p.at())
                pl.when(got)(arrive)
                b = gu_blk(k, p.y, zz)
                d = 1 if right else 0
                cp.send(b, b, s_z.at[k, d, zz], r_z.at[k, zz], p.at(z=z + 1 if right else z - 1), more)
                gu_ysend(k, zz, got)
        for zz in range(nz):
            yield
            cp.arrived(gu_blk(k, 1 - p.y, zz), s_y.at[k, zz], r_y.at[k, zz], p.at(y=1 - p.y))

    def flow_ag_d(k):
        W = WD[k]
        own = W.at[p.y, z]
        cp.send(own, own, s_dy.at[k], r_dy.at[k], p.at(y=1 - p.y))

        def zs(y, yi, zz, right, pred):
            b = W.at[y, zz]
            d = 1 if right else 0
            cp.send(b, b, s_dz.at[k, yi, d, zz], r_dz.at[k, yi, zz], p.at(z=z + 1 if right else z - 1), pred)
        zs(p.y, p.y, z, True, inner_r)
        zs(p.y, p.y, z, False, inner_l)
        yield
        cp.arrived(W.at[1 - p.y, z], s_dy.at[k], r_dy.at[k], p.at(y=1 - p.y))
        zs(1 - p.y, 1 - p.y, z, True, inner_r)
        zs(1 - p.y, 1 - p.y, z, False, inner_l)
        for s in range(1, nz):
            for right in (True, False):
                yield
                zz = z - s if right else z + s
                got = zz >= 0 if right else zz <= nz - 1
                more = got & (inner_r if right else inner_l)
                for y in (p.y, 1 - p.y):
                    pl.when(got)(lambda y=y, zz=zz: cp.arrived(
                        W.at[y, zz], s_dz.at[k, y, 0, zz], r_dz.at[k, y, zz], p.at()))
                    zs(y, y, zz, right, more)

    order = [nz - 1, 0] + list(range(1, nz - 1))[::-1]

    def flow_rs_gu(k):
        c = cols(k)
        for zz in order:
            cp.send(GGU.at[1 - p.y, :, zz, :, :, c], RY.at[:, zz, :, :, c],
                    s_gy.at[k, zz], r_gy.at[k, zz], p.at(y=1 - p.y))

        def ry_wait(zz):
            cp.arrived(RY.at[:, zz, :, :, c], s_gy.at[k, zz], r_gy.at[k, zz], p.at(y=1 - p.y))

        def zwait(sl):
            cp.arrived(ZGU.at[sl, :, :, :, c], s_gz.at[k, 0, 0], r_gz.at[k, sl], p.at())
        for zz in order:
            yield
            right, left = z < zz, z > zz
            ry_wait(zz)
            both = (right & inner_l) | (left & inner_r)

            def add3(zz=zz):
                zwait(zz)
                for j in range(TP):
                    GGU[p.y, j, zz, :, :, c] = (
                        GGU[p.y, j, zz, :, :, c].astype(F32) + RY[j, zz, :, :, c].astype(F32)
                        + ZGU[zz, j, :, :, c].astype(F32)).astype(BF)

            def add2(zz=zz):
                for j in range(TP):
                    GGU[p.y, j, zz, :, :, c] = (
                        GGU[p.y, j, zz, :, :, c].astype(F32) + RY[j, zz, :, :, c].astype(F32)).astype(BF)
            pl.when(both)(add3)
            pl.when(jnp.logical_and(z != zz, jnp.logical_not(both)))(add2)
            src = GGU.at[p.y, :, zz, :, :, c]
            sl_r = zz
            cp.send(src, ZGU.at[sl_r, :, :, :, c], s_gz.at[k, 1, zz], r_gz.at[k, sl_r], p.at(z=z + 1), right)
            sl_l = jnp.where(z - 1 == zz, nz, zz)
            cp.send(src, ZGU.at[sl_l, :, :, :, c], s_gz.at[k, 0, zz], r_gz.at[k, sl_l], p.at(z=z - 1), left)
        yield
        pl.when(inner_l)(lambda: zwait(z))
        pl.when(inner_r)(lambda: zwait(nz))
        for j in range(TP):
            FIN[j, :, :, c] = (
                GGU[p.y, j, z, :, :, c].astype(F32) + RY[j, z, :, :, c].astype(F32)
                + ZGU[z, j, :, :, c].astype(F32) + ZGU[nz, j, :, :, c].astype(F32)).astype(BF)
        for t in (2, 3, 1):
            m = p.member(t)
            cp.send(FIN.at[m, :, :, c], OGU.at[p.i, :, :, c], s_gt.at[k, t - 1], r_gt.at[k, t - 1], p.at(i=m))
        OGU[p.i, :, :, c] = FIN[p.i, :, :, c]
        yield
        for t in (1, 2, 3):
            m = p.member(t)
            cp.arrived(OGU.at[m, :, :, c], s_gt.at[k, t - 1], r_gt.at[k, t - 1], p.at(i=m))

    def flow_rs_d(k):
        G, L = GD[k], ZD[k]

        def zwait(sl):
            cp.arrived(L.at[sl], s_ez.at[k, 0, 0], r_ez.at[k, sl], p.at())
        for zz in order:
            yield
            right, left = z < zz, z > zz
            both = (right & inner_l) | (left & inner_r)

            def add2(zz=zz):
                zwait(zz)
                for y in range(2):
                    G[y, zz] = (G[y, zz].astype(F32) + L[zz, y].astype(F32)).astype(BF)
            pl.when(both)(add2)
            src = G.at[:, zz]
            cp.send(src, L.at[zz], s_ez.at[k, 1, zz], r_ez.at[k, zz], p.at(z=z + 1), right)
            sl_l = jnp.where(z - 1 == zz, nz, zz)
            cp.send(src, L.at[sl_l], s_ez.at[k, 0, zz], r_ez.at[k, sl_l], p.at(z=z - 1), left)
        yield
        pl.when(inner_l)(lambda: zwait(z))
        pl.when(inner_r)(lambda: zwait(nz))
        for y in range(2):
            FD[k][y] = (G[y, z].astype(F32) + L[z, y].astype(F32) + L[nz, y].astype(F32)).astype(BF)
        cp.send(FD[k].at[1 - p.y], YD[k], s_ey.at[k], r_ey.at[k], p.at(y=1 - p.y))
        yield
        cp.arrived(YD[k], s_ey.at[k], r_ey.at[k], p.at(y=1 - p.y))
        od_out[rws(k), :] = FD[k][p.y].astype(F32) + YD[k][...].astype(F32)

    def zero_left():
        ZGU[0] = jnp.zeros(ZGU.shape[1:], BF)
        for k in range(K):
            ZD[k][0] = jnp.zeros(ZD[k].shape[1:], BF)

    def zero_right():
        ZGU[nz] = jnp.zeros(ZGU.shape[1:], BF)
        for k in range(K):
            ZD[k][nz] = jnp.zeros(ZD[k].shape[1:], BF)

    for k in range(K):
        p0(k)
    acts(h_in, H, 0)
    acts(df_in, dF, 1)
    pl.when(first)(zero_left)
    pl.when(last)(zero_right)
    pltpu.make_async_copy(gus.at[p.i], WGU.at[p.y, p.i, z], sem_l.at[2]).wait()
    for k in range(K):
        pltpu.make_async_copy(ds.at[rws(k)], WD[k].at[p.y, z], sem_l.at[3 + k]).wait()

    flows = []

    def pump(n=1):
        for _ in range(n):
            for f in list(flows):
                if next(f, "end") == "end":
                    flows.remove(f)

    def run(gen):
        for _ in gen:
            pass
        if gen in flows:
            flows.remove(gen)

    ag = [(flow_ag_gu(k), flow_ag_d(k)) for k in range(K)]
    live = []
    for k in range(K):
        for g in ag[k]:
            next(g)
            flows.append(g)
        if k < K - 1:
            pump(2)
    acts_forward(H, 0)
    acts_forward(dF, 1)

    def fwd_mid(k, t):
        c0, cn = CH[k]
        c = cols(k)
        wg = WGU[:, :, :, 0, :, c].reshape(width, cn)
        wu = WGU[:, :, :, 1, :, c].reshape(width, cn)
        wd = WD[k][...].reshape(cn, width)
        a = mm(H[t], wg, NN)
        g = mm(H[t], wu, NN)
        dz = mm(dF[t], wd, NT)
        sg = 1.0 / (1.0 + jnp.exp(-a))
        act = a * sg
        Zb[t, :, c] = (act * g).astype(BF)
        dAb[t, :, :cn] = (dz * g * sg * (1.0 + a * (1.0 - sg))).astype(BF)
        dGb[t, :, :cn] = (dz * act).astype(BF)
        d = mm(dAb[t, :, :cn], wg, NT) + mm(dGb[t, :, :cn], wu, NT)
        if k == 0:
            dHa[t] = d
        else:
            dHa[t] += d

    def ffn_out(t):
        f = None
        for k in range(K):
            v = mm(Zb[t, :, cols(k)], WD[k][...].reshape(CH[k][1], width), NN)
            f = v if f is None else f + v
        return f

    def grads(k):
        c0, cn = CH[k]
        c = cols(k)
        tok = TP * rows
        for w, src in ((0, dAb), (1, dGb)):
            def body(m, _, w=w, src=src):
                y, j = m // 2, (m % 2) * 2
                f = 2 * nz * shard
                ms = pl.ds(pl.multiple_of(m * f, f), f)
                v = mm(H[:, :, ms].reshape(tok, f), src[:, :, :cn].reshape(tok, cn), TN)
                GGU[y, pl.ds(j, 2), :, w, :, c] = v.astype(BF).reshape(2, nz, shard, cn)
                return 0
            lax.fori_loop(0, TP, body, 0)
        r = parts[k]
        for b in range(cn // 128):
            v = mm(Zb[:, :, c0 + b * 128:c0 + (b + 1) * 128].reshape(tok, 128), dF[...].reshape(tok, width), TN).astype(BF)
            lo = b * 128
            while lo < (b + 1) * 128:
                pos, q = lo // r, lo % r
                n = min(r - q, (b + 1) * 128 - lo)
                GD[k][pos // nz, pos % nz, q:q + n] = v[lo - b * 128:lo - b * 128 + n]
                lo += n

    def x_send1(q, e, value):
        SX[e] = value.astype(BF)
        cx.send(SX.at[e], LX.at[q, e], s_x.at[q, e], r_x.at[q, e], p.at(i=p.member(1)))

    def x_wait(q, e):
        cx.arrived(LX.at[q, e], s_x.at[q, e], r_x.at[q, e], p.at(i=p.member(2 if e == 2 else 1)))

    def x_send2(q, acc):
        x_wait(q, 1)
        SX[2] = (acc[...] + LX[q, 1].astype(F32)).astype(BF)
        cx.send(SX.at[2], LX.at[q, 2], s_x.at[q, 2], r_x.at[q, 2], p.at(i=p.member(2)))

    def x_final(q, acc, out):
        x_wait(q, 0)
        x_wait(q, 2)
        acc[...] += LX[q, 0].astype(F32) + LX[q, 2].astype(F32)
        pltpu.make_async_copy(acc, out, sem_l.at[q]).start()

    for k in range(K):
        for g in ag[k]:
            run(g)
        if k == 0:
            for t in (1, 3):
                for q, dst in ((0, H), (1, dF)):
                    acts_wait(dst, q, t)

        def tbody(n, _, k=k):
            fwd_mid(k, n)
            return 0
        lax.fori_loop(0, TP, tbody, 0)
        pump(2)
        if k == K - 1:
            x_send1(0, 0, dHa[1])
            x_send1(0, 1, dHa[3])
        grads(k)
        for g in (flow_rs_d(k), flow_rs_gu(k)):
            next(g)
            flows.append(g)
        pump(1)
    x_send2(0, dHa.at[2])
    pump(1)
    cx.drain(2)
    x_send1(1, 0, ffn_out(1))
    x_send1(1, 1, ffn_out(3))
    pump(1)
    dHa[1] = ffn_out(2)
    dHa[3] = ffn_out(0)
    pump(1)
    x_final(0, dHa.at[0], dh_out)
    cx.drain(1)
    x_send2(1, dHa.at[1])
    while flows:
        pump(1)
    x_final(1, dHa.at[3], f_out)
    ogu_out[...] = OGU[...]
    pltpu.make_async_copy(dHa.at[0], dh_out, sem_l.at[0]).wait()
    pltpu.make_async_copy(dHa.at[3], f_out, sem_l.at[1]).wait()
    cp.drain()
    cx.drain()


def ffn_call(h, df, gus, ds, parts, nz, cid):
    rows, width = h.shape
    shard, cols = gus.shape[2], gus.shape[3]
    K = len(parts)
    dr = ds.shape[0]
    V = pl.BlockSpec(memory_space=pltpu.VMEM)
    A = pl.BlockSpec(memory_space=pl.ANY)
    D = pltpu.SemaphoreType.DMA
    maxc = max(parts) * 2 * nz
    scratch = [
        pltpu.VMEM((TP, rows, width), BF),
        pltpu.VMEM((TP, rows, width), BF),
        pltpu.VMEM((2, TP, nz, 2, shard, cols), BF),
        [pltpu.VMEM((2, nz, r, width), BF) for r in parts],
        pltpu.VMEM((TP, rows, width), F32),
        pltpu.VMEM((TP, rows, cols), BF),
        pltpu.VMEM((TP, rows, maxc), BF),
        pltpu.VMEM((TP, rows, maxc), BF),
        pltpu.VMEM((2, TP, nz, 2, shard, cols), BF),
        [pltpu.VMEM((2, nz, r, width), BF) for r in parts],
        pltpu.VMEM((TP, nz, 2, shard, cols), BF),
        pltpu.VMEM((nz + 1, TP, 2, shard, cols), BF),
        pltpu.VMEM((TP, 2, shard, cols), BF),
        [pltpu.VMEM((nz + 1, 2, r, width), BF) for r in parts],
        [pltpu.VMEM((r, width), BF) for r in parts],
        [pltpu.VMEM((2, r, width), BF) for r in parts],
        pltpu.VMEM((TP, 2, shard, cols), BF),
        pltpu.VMEM((2, 3, rows, width), BF),
        pltpu.VMEM((3, rows, width), BF),
        D((2, 2, 3)), D((3 + K,)),
        D((K, 3)), D((K, 3)),
        D((K, 2, nz)), D((K, nz)), D((K, nz)), D((K, nz)),
        D((K, 2, 2, nz)), D((K, 2, nz)), D((K,)), D((K,)),
        D((K, nz)), D((K, nz)), D((K, 2, nz)), D((K, nz + 1)), D((K, 3)), D((K, 3)),
        D((K, 2, nz)), D((K, nz + 1)), D((K,)), D((K,)),
        D((2, 3)), D((2, 3)),
    ]
    return pl.pallas_call(
        functools.partial(ffn_body, parts, nz),
        name="ffn",
        out_shape=(
            jax.ShapeDtypeStruct((rows, width), F32),
            jax.ShapeDtypeStruct((rows, width), F32),
            jax.ShapeDtypeStruct((TP, 2, shard, cols), BF),
            jax.ShapeDtypeStruct((dr, width), F32),
        ),
        in_specs=[A, A, V, V],
        out_specs=[A, A, V, V],
        scratch_shapes=scratch,
        compiler_params=pltpu.CompilerParams(
            collective_id=cid, has_side_effects=True, vmem_limit_bytes=66_900_000),
    )(h, df, gus, ds)


def pieces_of(width):
    half = width // 2
    return (
        (0, 0, width, "xzy"),
        (1, 0, width, "yzx"),
        (2, 0, width, "zxy"),
        (3, 0, half, "xzy"),
        (3, half, half, "yzx"),
        (4, 0, LANES, "zxy"),
    )


def gather_sems(nz, count):
    D = pltpu.SemaphoreType.DMA
    return [D((count, 2, 2, nz)), D((count, 2, nz)), D((count, nz)), D((count, nz)), D((count, 2, nz)),
            D((count, 2, nz)), D((count,)), D((count,))]


def gather_flow(p, cp, n, piece, W, sems):
    s_z, r_z, s_1, r_1, s_2, r_2, s_c, r_c = sems
    _, c0, cn, order = piece
    cs = slice(c0, c0 + cn)
    z, nz = p.z, p.nz
    inner_l, inner_r = z > 0, z < nz - 1
    a_is_x = order != "yzx"

    def blk(a, b, zz, c=None):
        y, x = (b, a) if a_is_x else (a, b)
        return W.at[y, x, p.c if c is None else c, zz, :, cs]
    a, b = (p.x, p.y) if a_is_x else (p.y, p.x)

    def other(axis):
        return p.at(i=p.member(2)) if axis == "x" else p.at(y=1 - p.y)
    axis_a, axis_b = ("x", "y") if a_is_x else ("y", "x")

    def core(aa, bb, zz, pred=True):
        r = blk(aa, bb, zz)
        cp.send(r, r, s_c.at[n], r_c.at[n], p.at(i=p.member(1)), pred, group=(n, "c"))

    def zsend(aa, zz, right, pred):
        r = blk(aa, b, zz)
        cp.send(r, r, s_z.at[n, aa, 1 if right else 0, zz], r_z.at[n, aa, zz],
                p.at(z=z + 1 if right else z - 1), pred)

    def asend(zz, pred=True):
        r = blk(a, b, zz)
        cp.send(r, r, s_1.at[n, zz], r_1.at[n, zz], other(axis_a), pred)

    def bsend(aa, zz, pred=True):
        r = blk(aa, b, zz)
        cp.send(r, r, s_2.at[n, aa, zz], r_2.at[n, aa, zz], other(axis_b), pred)

    zfirst = order == "zxy"
    asend(z)
    zsend(a, z, True, inner_r)
    zsend(a, z, False, inner_l)
    bsend(a, z)
    core(a, b, z)
    if not zfirst:
        yield
        cp.arrived(blk(1 - a, b, z), s_1.at[n, z], r_1.at[n, z], p.at())
        zsend(1 - a, z, True, inner_r)
        zsend(1 - a, z, False, inner_l)
        bsend(1 - a, z)
        core(1 - a, b, z)
    for s in range(1, nz):
        for right in (True, False):
            yield
            zz = z - s if right else z + s
            got = zz >= 0 if right else zz <= nz - 1
            more = got & (inner_r if right else inner_l)
            for aa in ((a,) if zfirst else (a, 1 - a)):
                pl.when(got)(lambda aa=aa, zz=zz: cp.arrived(
                    blk(aa, b, zz), s_z.at[n, aa, 0, zz], r_z.at[n, aa, zz], p.at()))
                zsend(aa, zz, right, more)
                if zfirst:
                    asend(zz, got)
                bsend(aa, zz, got)
                core(aa, b, zz, got)
    if zfirst:
        for zz in range(nz):
            yield
            cp.arrived(blk(1 - a, b, zz), s_1.at[n, zz], r_1.at[n, zz], p.at())
            bsend(1 - a, zz)
            core(1 - a, b, zz)
    for zz in range(nz):
        for aa in (a, 1 - a):
            yield
            cp.arrived(blk(aa, 1 - b, zz), s_2.at[n, aa, zz], r_2.at[n, aa, zz], p.at())
            core(aa, 1 - b, zz)
    yield
    cp.arrived(W.at[:, :, 1 - p.c, :, :, cs], s_c.at[n], r_c.at[n], p.at())
    cp.pending.append((True, lambda: pltpu.make_async_remote_copy(
        src_ref=W.at[:, :, p.c, :, :, cs], dst_ref=W.at[:, :, p.c, :, :, cs], send_sem=s_c.at[n],
        recv_sem=r_c.at[n], device_id=p.at(i=p.member(1)), device_id_type=MESH)))


def sum_sems(nz, count):
    D = pltpu.SemaphoreType.DMA
    return [D((count,)), D((count,)), D((count, nz)), D((count, nz)), D((count, nz)), D((count, nz)),
            D((count, 2, nz)), D((count, nz + 1))]


def sum_scratch(nz, shard, pieces):
    core = [pltpu.VMEM((2, 2, nz, shard, q[2]), BF) for q in pieces]
    one = [pltpu.VMEM((2, nz, shard, q[2]), BF) for q in pieces]
    two = [pltpu.VMEM((nz if q[3] == "zxy" else 1, shard, q[2]), BF) for q in pieces]
    path = [pltpu.VMEM((nz + 1, 1 if q[3] == "zxy" else 2, shard, q[2]), BF) for q in pieces]
    return [core, one, two, path]


def sum_flow(p, cp, n, piece, G, land, out, sems):
    s_c, r_c, s_1, r_1, s_2, r_2, s_z, r_z = sems
    LC, L1, L2, LZ = (l[n] for l in land)
    _, c0, cn, order = piece
    cs = slice(c0, c0 + cn)
    z, nz = p.z, p.nz
    inner_l, inner_r = z > 0, z < nz - 1
    targets = [nz - 1, 0] + list(range(1, nz - 1))[::-1]
    zlast = order == "zxy"
    b_is_y = order != "yzx"
    b, a = (p.y, p.x) if b_is_y else (p.x, p.y)
    dev_b = p.at(y=1 - p.y) if b_is_y else p.at(i=p.member(2))
    dev_a = p.at(i=p.member(2)) if b_is_y else p.at(y=1 - p.y)

    def g(bb, aa, zz):
        y, x = (bb, aa) if b_is_y else (aa, bb)
        return (y, x, p.c, zz, slice(None), cs)

    def f(v):
        return v.astype(F32)

    cp.send(G.at[:, :, 1 - p.c, :, :, cs], LC, s_c.at[n], r_c.at[n], p.at(i=p.member(1)))
    pl.when(jnp.logical_not(inner_l))(lambda: LZ.__setitem__(0, jnp.zeros(LZ.shape[1:], BF)))
    pl.when(jnp.logical_not(inner_r))(lambda: LZ.__setitem__(nz, jnp.zeros(LZ.shape[1:], BF)))
    yield
    cp.arrived(LC, s_c.at[n], r_c.at[n], p.at())

    def lc(bb, aa, zz):
        y, x = (bb, aa) if b_is_y else (aa, bb)
        return (y, x, zz)
    for zz in targets:
        for aa in range(2):
            i = g(1 - b, aa, zz)
            G[i] = (f(G[i]) + f(LC[lc(1 - b, aa, zz)])).astype(BF)
        y, x = (1 - b, slice(None)) if b_is_y else (slice(None), 1 - b)
        cp.send(G.at[y, x, p.c, zz, :, cs], L1.at[:, zz], s_1.at[n, zz], r_1.at[n, zz], dev_b)
    for zz in targets:
        for aa in range(2):
            i = g(b, aa, zz)
            G[i] = (f(G[i]) + f(LC[lc(b, aa, zz)])).astype(BF)
    if zlast:
        for zz in targets:
            yield
            cp.arrived(L1.at[:, zz], s_1.at[n, zz], r_1.at[n, zz], p.at())
            i = g(b, 1 - a, zz)
            G[i] = (f(G[i]) + f(L1[1 - a, zz])).astype(BF)
            cp.send(G.at[i], L2.at[zz], s_2.at[n, zz], r_2.at[n, zz], dev_a)

    def own(zz, k):
        if zlast:
            return f(G[g(b, a, zz)]) + f(L1[a, zz]) + f(L2[zz])
        return f(G[g(b, k, zz)]) + f(L1[k, zz])

    def put(zz, k, v):
        G[g(b, a if zlast else k, zz)] = v.astype(BF)
    ks = range(1) if zlast else range(2)

    def zwait(sl):
        cp.arrived(LZ.at[sl], s_z.at[n, 0, 0], r_z.at[n, sl], p.at())
    for zz in targets:
        yield
        if zlast:
            cp.arrived(L2.at[zz], s_2.at[n, zz], r_2.at[n, zz], p.at())
        else:
            cp.arrived(L1.at[:, zz], s_1.at[n, zz], r_1.at[n, zz], p.at())
        right, left = z < zz, z > zz
        both = (right & inner_l) | (left & inner_r)

        def add3(zz=zz):
            zwait(zz)
            for k in ks:
                put(zz, k, own(zz, k) + f(LZ[zz, k]))

        def add2(zz=zz):
            for k in ks:
                put(zz, k, own(zz, k))
        pl.when(both)(add3)
        pl.when(jnp.logical_and(z != zz, jnp.logical_not(both)))(add2)
        if zlast:
            src = G.at[p.y, pl.ds(p.x, 1), p.c, zz, :, cs]
        elif b_is_y:
            src = G.at[p.y, :, p.c, zz, :, cs]
        else:
            src = G.at[:, p.x, p.c, zz, :, cs]
        cp.send(src, LZ.at[zz], s_z.at[n, 1, zz], r_z.at[n, zz], p.at(z=z + 1), right)
        sl = jnp.where(z - 1 == zz, nz, zz)
        cp.send(src, LZ.at[sl], s_z.at[n, 0, zz], r_z.at[n, sl], p.at(z=z - 1), left)
    yield
    pl.when(inner_l)(lambda: zwait(z))
    pl.when(inner_r)(lambda: zwait(nz))

    def total(k):
        return own(z, k) + f(LZ[z, k]) + f(LZ[nz, k])
    if zlast:
        out[:, cs] = total(0)
        return
    G[g(b, 1 - a, z)] = total(1 - a).astype(BF)
    cp.send(G.at[g(b, 1 - a, z)], L2.at[0], s_2.at[n, 0], r_2.at[n, 0], dev_a)
    out[:, cs] = total(a)
    yield
    cp.arrived(L2.at[0], s_2.at[n, 0], r_2.at[n, 0], p.at())
    out[:, cs] += f(L2[0])


def interleave(flows):
    flows = list(flows)
    while flows:
        for flow in list(flows):
            if next(flow, "end") == "end":
                flows.remove(flow)


def gather_body(nz, pieces, *refs):
    blocks, outs = refs[:5], refs[5:10]
    sem_l, sems = refs[10], refs[11:]
    p, cp = Place(nz), Copies()
    for q in range(5):
        cp.local(blocks[q], outs[q].at[p.y, p.x, p.c, p.z], sem_l.at[q])
    entry_barrier(p)
    for q in range(5):
        pltpu.make_async_copy(blocks[q], outs[q].at[p.y, p.x, p.c, p.z], sem_l.at[q]).wait()
    interleave(gather_flow(p, cp, n, piece, outs[piece[0]], sems) for n, piece in enumerate(pieces))
    cp.drain()


def gather_call(blocks, nz, cid):
    shard, width = blocks[0].shape
    pieces = pieces_of(width)
    A = pl.BlockSpec(memory_space=pl.ANY)
    V = pl.BlockSpec(memory_space=pltpu.VMEM)
    outs = [jax.ShapeDtypeStruct((2, 2, 2, nz, shard, b.shape[1]), BF) for b in blocks]
    return pl.pallas_call(
        functools.partial(gather_body, nz, pieces),
        name="mixer_gather",
        out_shape=outs,
        in_specs=[V] * 5,
        out_specs=[A] * 5,
        scratch_shapes=[pltpu.SemaphoreType.DMA((5,))] + gather_sems(nz, len(pieces)),
        compiler_params=pltpu.CompilerParams(collective_id=cid, has_side_effects=True),
    )(*blocks)


def sum_body(nz, pieces, *refs):
    g_in, g_out, g_small = refs[:3]
    outs = refs[3:8]
    G = refs[8:13]
    land = refs[13:17]
    sem_l, sems = refs[17], refs[18:]
    p, cp = Place(nz), Copies()
    width = g_out.shape[-1]

    def pairs():
        return [(g_in.at[:, :, :, :, :, q * width:(q + 1) * width], G[q]) for q in range(3)] + [
            (g_out, G[3]), (g_small, G[4])]
    for q, (src, dst) in enumerate(pairs()):
        cp.local(src, dst, sem_l.at[q])
    entry_barrier(p)
    for q, (src, dst) in enumerate(pairs()):
        pltpu.make_async_copy(src, dst, sem_l.at[q]).wait()
    interleave(sum_flow(p, cp, n, piece, G[piece[0]], land, outs[piece[0]], sems) for n, piece in enumerate(pieces))
    cp.drain()


def sum_call(g_in, g_out, g_small, nz, cid):
    width = g_out.shape[-1]
    shard = g_out.shape[0] // (8 * nz)
    pieces = pieces_of(width)
    A = pl.BlockSpec(memory_space=pl.ANY)
    V = pl.BlockSpec(memory_space=pltpu.VMEM)
    view = lambda v: v.reshape(2, 2, 2, nz, shard, v.shape[-1])
    wide = [width] * 4 + [LANES]
    return pl.pallas_call(
        functools.partial(sum_body, nz, pieces),
        name="mixer_sum",
        out_shape=[jax.ShapeDtypeStruct((shard, w), F32) for w in wide],
        in_specs=[A] * 3,
        out_specs=[V] * 5,
        scratch_shapes=[pltpu.VMEM((2, 2, 2, nz, shard, w), BF) for w in wide] + sum_scratch(nz, shard, pieces)
        + [pltpu.SemaphoreType.DMA((5,))] + sum_sems(nz, len(pieces)),
        compiler_params=pltpu.CompilerParams(collective_id=cid, has_side_effects=True, vmem_limit_bytes=66_900_000),
    )(view(g_in), view(g_out), view(g_small))


def shifted(block, axis, distance):
    devices = range(lax.axis_size(axis))
    route = [(i - distance, i) for i in devices if i - distance in devices]
    return lax.ppermute(block, axis, route)


def matmul(left, right):
    return jnp.dot(left, right, preferred_element_type=jnp.float32)


def norm_parts(values):
    inverse = lax.rsqrt(jnp.mean(values * values, axis=-1, keepdims=True) + eps)
    return (inverse, values * inverse)


def norm_back(grad_hidden, normed, inverse, gain):
    grad_normed = grad_hidden * gain
    inner_mean = jnp.mean(grad_normed * normed, axis=-1, keepdims=True)
    return inverse * (grad_normed - normed * inner_mean)


def plain_device(
    tokens,
    segments,
    ln1_gain,
    in_weight,
    conv_kernel,
    out_weight,
    ln2_gain,
    gate_weight,
    up_weight,
    down_weight,
    cotangent,
):
    micro_count = tokens.shape[0]
    row_count = tokens.shape[2]
    width = tokens.shape[3]
    taps = conv_kernel.shape[0]
    offset = lax.axis_index("seq") * row_count
    low_gain1 = ln1_gain.astype(jnp.bfloat16)
    low_in = in_weight.astype(jnp.bfloat16)
    low_kernel = conv_kernel.astype(jnp.bfloat16)
    low_out = out_weight.astype(jnp.bfloat16)
    low_gain2 = ln2_gain.astype(jnp.bfloat16)
    low_gate = gate_weight.astype(jnp.bfloat16)
    low_up = up_weight.astype(jnp.bfloat16)
    low_down = down_weight.astype(jnp.bfloat16)
    shard_totals = None
    full_totals = None
    out_list = []
    grad_list = []
    for micro_index in range(micro_count):
        weights = (
            lax.all_gather(low_gain1, ("dp", "seq"), axis=0, tiled=True),
            lax.all_gather(low_in, ("dp", "seq"), axis=0, tiled=True),
            lax.all_gather(low_kernel, ("dp", "seq"), axis=1, tiled=True),
            lax.all_gather(low_out, ("dp", "seq"), axis=0, tiled=True),
            lax.all_gather(low_gain2, ("dp", "seq"), axis=0, tiled=True),
            lax.all_gather(low_gate, ("dp", "seq"), axis=0, tiled=True),
            lax.all_gather(low_up, ("dp", "seq"), axis=0, tiled=True),
            lax.all_gather(low_down, ("dp", "seq"), axis=0, tiled=True),
        )
        gain_one = weights[0].astype(jnp.float32)
        kernel = weights[2].astype(jnp.float32)
        gain_two = weights[4].astype(jnp.float32)
        seg_line = segments[micro_index, 0]
        fill = jnp.full((2,), -1, jnp.int32)
        seg_pad = jnp.concatenate([fill, seg_line, fill])
        window = lax.dynamic_slice_in_dim(seg_pad, offset, row_count + 4)
        masks = [
            (window[tap : tap + row_count + 2] == window[2 : row_count + 4]).astype(jnp.float32)
            for tap in range(taps)
        ]
        tokens_f = tokens[micro_index, 0].astype(jnp.float32)
        inverse_one, normed_one = norm_parts(tokens_f)
        hidden_one = (normed_one * gain_one).astype(jnp.bfloat16)
        projected = matmul(hidden_one, weights[1])
        b_part = projected[:, :width]
        c_part = projected[:, width : 2 * width]
        x_part = projected[:, 2 * width :]
        mixed = (b_part * x_part).astype(jnp.bfloat16)
        prev_rows = shifted(mixed[row_count - 2 :], "seq", 1)
        extended = jnp.concatenate([prev_rows, mixed], axis=0).astype(jnp.float32)
        conv_out = jnp.zeros((row_count, width), jnp.float32)
        for tap in range(taps):
            conv_out = (
                conv_out
                + kernel[tap] * extended[tap : tap + row_count] * masks[tap][:row_count, None]
            )
        gated = (c_part * conv_out).astype(jnp.bfloat16)
        resid = tokens_f + matmul(gated, weights[3])
        inverse_two, normed_two = norm_parts(resid)
        hidden_two = (normed_two * gain_two).astype(jnp.bfloat16)
        gate_pre = matmul(hidden_two, weights[5])
        up_pre = matmul(hidden_two, weights[6])
        sigmoid_gate = jax.nn.sigmoid(gate_pre)
        activated = gate_pre * sigmoid_gate
        inner = (activated * up_pre).astype(jnp.bfloat16)
        ffn_out = matmul(inner, weights[7])
        out_list.append((resid + ffn_out).astype(jnp.bfloat16))
        back_weights = (
            lax.all_gather(low_gain1, ("dp", "seq"), axis=0, tiled=True),
            lax.all_gather(low_in, ("dp", "seq"), axis=0, tiled=True),
            lax.all_gather(low_kernel, ("dp", "seq"), axis=1, tiled=True),
            lax.all_gather(low_out, ("dp", "seq"), axis=0, tiled=True),
            lax.all_gather(low_gain2, ("dp", "seq"), axis=0, tiled=True),
            lax.all_gather(low_gate, ("dp", "seq"), axis=0, tiled=True),
            lax.all_gather(low_up, ("dp", "seq"), axis=0, tiled=True),
            lax.all_gather(low_down, ("dp", "seq"), axis=0, tiled=True),
        )
        grad_final = cotangent[micro_index, 0]
        grad_inner = matmul(grad_final, back_weights[7].T)
        part_down = matmul(inner.T, grad_final)
        grad_gate_pre = (
            grad_inner * up_pre * sigmoid_gate * (1.0 + gate_pre * (1.0 - sigmoid_gate))
        ).astype(jnp.bfloat16)
        grad_up_pre = (grad_inner * activated).astype(jnp.bfloat16)
        grad_hidden_two = matmul(grad_gate_pre, back_weights[5].T) + matmul(
            grad_up_pre, back_weights[6].T
        )
        part_gate = matmul(hidden_two.T, grad_gate_pre)
        part_up = matmul(hidden_two.T, grad_up_pre)
        part_gain2 = jnp.sum(grad_hidden_two * normed_two, axis=0)
        grad_resid = grad_final.astype(jnp.float32) + norm_back(
            grad_hidden_two, normed_two, inverse_two, gain_two
        )
        grad_branch = grad_resid.astype(jnp.bfloat16)
        grad_gated = matmul(grad_branch, back_weights[3].T)
        part_out = matmul(gated.T, grad_branch)
        grad_c = grad_gated * conv_out
        grad_conv = (grad_gated * c_part).astype(jnp.bfloat16)
        next_rows = shifted(grad_conv[:2], "seq", -1)
        grad_extended = jnp.concatenate([grad_conv, next_rows], axis=0).astype(jnp.float32)
        grad_mixed = jnp.zeros((row_count, width), jnp.float32)
        kernel_terms = []
        for tap in range(taps):
            weighted = grad_extended * masks[tap][:, None]
            grad_mixed = grad_mixed + kernel[tap] * weighted[2 - tap : 2 - tap + row_count]
            kernel_terms.append(
                jnp.sum(weighted[:row_count] * extended[tap : tap + row_count], axis=0)
            )
        part_kernel = jnp.stack(kernel_terms, axis=0)
        grad_proj = jnp.concatenate(
            [grad_mixed * x_part, grad_c, grad_mixed * b_part], axis=1
        ).astype(jnp.bfloat16)
        grad_hidden_one = matmul(grad_proj, back_weights[1].T)
        part_in = matmul(hidden_one.T, grad_proj)
        part_gain1 = jnp.sum(grad_hidden_one * normed_one, axis=0)
        grad_input = grad_resid + norm_back(grad_hidden_one, normed_one, inverse_one, gain_one)
        grad_list.append(grad_input.astype(jnp.bfloat16))
        parts = (
            part_gain1,
            part_in,
            part_kernel,
            part_out,
            part_gain2,
            part_gate,
            part_up,
            part_down,
        )
        full_totals = (
            parts
            if full_totals is None
            else tuple((first + second for first, second in zip(full_totals, parts)))
        )
    shard_totals = (
        lax.psum_scatter(full_totals[0], ("dp", "seq"), scatter_dimension=0, tiled=True),
        lax.psum_scatter(full_totals[1], ("dp", "seq"), scatter_dimension=0, tiled=True),
        lax.psum_scatter(full_totals[2], ("dp", "seq"), scatter_dimension=1, tiled=True),
        lax.psum_scatter(full_totals[3], ("dp", "seq"), scatter_dimension=0, tiled=True),
        lax.psum_scatter(full_totals[4], ("dp", "seq"), scatter_dimension=0, tiled=True),
        lax.psum_scatter(full_totals[5], ("dp", "seq"), scatter_dimension=0, tiled=True),
        lax.psum_scatter(full_totals[6], ("dp", "seq"), scatter_dimension=0, tiled=True),
        lax.psum_scatter(full_totals[7], ("dp", "seq"), scatter_dimension=0, tiled=True),
    )
    output = jnp.stack(out_list, axis=0)[:, None]
    grad_tokens = jnp.stack(grad_list, axis=0)[:, None]
    return (
        output,
        grad_tokens,
        shard_totals[0],
        shard_totals[1],
        shard_totals[2],
        shard_totals[3],
        shard_totals[4],
        shard_totals[5],
        shard_totals[6],
        shard_totals[7],
    )


def cut_columns(w, parts, ny, nz):
    rows, shard = w.shape[0], w.shape[1] // (ny * TP * nz)
    cut = w.astype(BF).reshape(rows, ny, TP, nz, shard)
    pieces, start = [], 0
    for size in parts:
        piece = cut[..., start : start + size].transpose(2, 0, 1, 3, 4)
        pieces.append(piece.reshape(TP, rows, ny * nz * size))
        start += size
    return jnp.concatenate(pieces, axis=-1)


def join_columns(g, parts, ny, nz):
    rows = g.shape[1]
    pieces, start, npos = [], 0, ny * nz
    for size in parts:
        piece = g[:, :, npos * start : npos * (start + size)].reshape(TP, rows, ny, nz, size)
        pieces.append(piece.transpose(1, 2, 0, 3, 4))
        start += size
    return jnp.concatenate(pieces, axis=-1).reshape(rows, -1).astype(F32)


def fast_device(
    parts,
    tokens,
    segments,
    ln1_gain,
    in_weight,
    conv_kernel,
    out_weight,
    ln2_gain,
    gate_weight,
    up_weight,
    down_weight,
    cotangent,
):
    micro, _, count, width = tokens.shape
    taps = conv_kernel.shape[0]
    nz = lax.axis_size("seq")
    ny = lax.axis_size("dp") // TP
    rows = micro * count
    x = tokens.reshape(rows, width).astype(F32)
    low_in = in_weight.astype(BF)
    small = jnp.concatenate([ln1_gain[None], ln2_gain[None], conv_kernel], axis=0).astype(BF)
    small = jnp.pad(small.T, ((0, 0), (0, LANES - taps - 2)))
    blocks = [low_in[:, q * width : (q + 1) * width] for q in range(3)]
    blocks += [out_weight.astype(BF), small]
    gathered = gather_call(blocks, nz, 1)
    w_b, w_c, w_u, w_out, small = (v.reshape(width, -1) for v in gathered)
    small = small[:, : taps + 2].T.astype(F32)
    gain_one, gain_two, kernel = small[0], small[1], small[2:]

    offset = lax.axis_index("seq") * count
    fill = jnp.full((micro, 2), -1, jnp.int32)
    seg_pad = jnp.concatenate([fill, segments[:, 0], fill], axis=1)
    window = lax.dynamic_slice_in_dim(seg_pad, offset, count + 4, axis=1)
    masks = [
        (window[:, tap : tap + count + 2] == window[:, 2 : count + 4]).astype(F32)[..., None]
        for tap in range(taps)
    ]
    inv1, norm1 = norm_parts(x)
    h1 = (norm1 * gain_one).astype(BF)
    b, c, u = (matmul(h1, w) for w in (w_b, w_c, w_u))
    mixed = (b * u).astype(BF).reshape(micro, count, width)
    prev = shifted(mixed[:, count - 2 :], "seq", 1)
    ext = jnp.concatenate([prev, mixed], axis=1).astype(F32)
    conv = sum(kernel[t] * ext[:, t : t + count] * masks[t][:, :count] for t in range(taps))
    conv = conv.reshape(rows, width)
    gated = (c * conv).astype(BF)
    resid = x + matmul(gated, w_out)
    inv2, norm2 = norm_parts(resid)
    h2 = (norm2 * gain_two).astype(BF)

    df = cotangent.reshape(rows, width)
    gus = jnp.stack([cut_columns(gate_weight, parts, ny, nz), cut_columns(up_weight, parts, ny, nz)], axis=1)
    f, dh2, gu, gd = ffn_call(h2, df, gus, down_weight.astype(BF), parts, nz, 0)
    output = (resid + f).astype(BF)
    g_gate = join_columns(gu[:, 0], parts, ny, nz)
    g_up = join_columns(gu[:, 1], parts, ny, nz)

    g_gain2 = jnp.sum(dh2 * norm2, axis=0)
    dr = df.astype(F32) + norm_back(dh2, norm2, inv2, gain_two)
    do = dr.astype(BF)
    dy = matmul(do, w_out.T)
    g_out = matmul(gated.T, do).astype(BF)
    dc = dy * conv
    dconv = (dy * c).astype(BF).reshape(micro, count, width)
    after = shifted(dconv[:, :2], "seq", -1)
    gext = jnp.concatenate([dconv, after], axis=1).astype(F32)
    dmix = jnp.zeros((micro, count, width), F32)
    kterms = []
    for t in range(taps):
        weighted = gext * masks[t]
        dmix = dmix + kernel[t] * weighted[:, 2 - t : 2 - t + count]
        kterms.append(jnp.sum(weighted[:, :count] * ext[:, t : t + count], axis=(0, 1)))
    dmix = dmix.reshape(rows, width)
    dps = [v.astype(BF) for v in (dmix * u, dc, dmix * b)]
    dh1 = sum(matmul(v, w.T) for v, w in zip(dps, (w_b, w_c, w_u)))
    g_in = matmul(h1.T, jnp.concatenate(dps, axis=1)).astype(BF)
    g_gain1 = jnp.sum(dh1 * norm1, axis=0)
    gx = (dr + norm_back(dh1, norm1, inv1, gain_one)).astype(BF)
    g_small = jnp.stack([g_gain1, g_gain2] + kterms, axis=0)
    g_small = jnp.pad(g_small.T, ((0, 0), (0, LANES - taps - 2))).astype(BF)
    sums = sum_call(g_in, g_out, g_small, nz, 2)
    g_in = jnp.concatenate(sums[:3], axis=1)
    g_out = sums[3]
    g_small = sums[4][:, : taps + 2].T
    shape = tokens.shape
    return (
        output.reshape(shape), gx.reshape(shape), g_small[0], g_in, g_small[2:], g_out,
        g_small[1], g_gate, g_up, gd,
    )


def row_parts(mesh, down_shape):
    nd, nz = mesh.shape["dp"], mesh.shape["seq"]
    if nd != 2 * TP:
        return None
    per = down_shape[0] // (nd * nz)
    if per % 16:
        return None
    sizes, left = [], per
    while left:
        sizes.append(min(64, left))
        left -= sizes[-1]
    return tuple(sizes)


def solution(mesh):
    in_specs = (
        P(None, "dp", "seq", None),
        P(None, "dp", None),
        P(("dp", "seq")),
        P(("dp", "seq"), None),
        P(None, ("dp", "seq")),
        P(("dp", "seq"), None),
        P(("dp", "seq")),
        P(("dp", "seq"), None),
        P(("dp", "seq"), None),
        P(("dp", "seq"), None),
        P(None, "dp", "seq", None),
    )
    out_specs = (
        P(None, "dp", "seq", None),
        P(None, "dp", "seq", None),
        P(("dp", "seq")),
        P(("dp", "seq"), None),
        P(None, ("dp", "seq")),
        P(("dp", "seq"), None),
        P(("dp", "seq")),
        P(("dp", "seq"), None),
        P(("dp", "seq"), None),
        P(("dp", "seq"), None),
    )

    def run(*arrays):
        parts = row_parts(mesh, arrays[9].shape)
        device = plain_device if parts is None else functools.partial(fast_device, parts)
        return jax.shard_map(
            device, mesh=mesh, in_specs=in_specs, out_specs=out_specs, check_vma=False
        )(*arrays)

    return run
```

```python
import functools
import jax
import jax.numpy as jnp
from jax import lax
from jax.experimental import pallas as pl
from jax.experimental.pallas import tpu as pltpu
from jax.sharding import PartitionSpec as P

BF = jnp.bfloat16
F32 = jnp.float32
eps = 1e-05
MESH = pl.DeviceIdType.MESH
NN = (((1,), (0,)), ((), ()))
NT = (((1,), (1,)), ((), ()))
TN = (((0,), (0,)), ((), ()))
TP = 4
LANES = 128


def mm(left, right, dims):
    return lax.dot_general(left, right, dims, preferred_element_type=F32)


def when(pred, body):
    if pred is True:
        body()
    else:
        pl.when(pred)(body)


class Place:
    def __init__(self, nz):
        dp = lax.axis_index("dp")
        self.y = dp // TP
        self.i = dp % TP
        self.z = lax.axis_index("seq")
        self.nz = nz
        self.x = self.i // 2
        self.c = self.i % 2
        self.others = tuple(self._near(k) for k in range(nz - 1))

    def _near(self, k):
        ranks = [sorted((q for q in range(self.nz) if q != z), key=lambda q: abs(q - z)) for z in range(self.nz)]
        place = jnp.int32(ranks[0][k])
        for z in range(1, self.nz):
            place = jnp.where(self.z == z, ranks[z][k], place)
        return place

    def member(self, t):
        x = 1 - self.x if t // 2 else self.x
        c = 1 - self.c if t % 2 else self.c
        return x * 2 + c

    def at(self, y=None, i=None, z=None):
        y = self.y if y is None else y
        i = self.i if i is None else i
        z = self.z if z is None else z
        return (y * TP + i, z)


class Copies:
    def __init__(self):
        self.pending = []

    def send(self, src, dst, ssem, rsem, device, pred=True, group=None):
        def make():
            return pltpu.make_async_remote_copy(
                src_ref=src, dst_ref=dst, send_sem=ssem, recv_sem=rsem,
                device_id=device, device_id_type=MESH)
        when(pred, lambda: make().start())
        if group is None:
            self.pending.append((pred, make))

    def local(self, src, dst, sem):
        pltpu.make_async_copy(src, dst, sem).start()

    def arrived(self, ref, ssem, rsem, device, pred=True):
        when(pred, lambda: pltpu.make_async_remote_copy(
            src_ref=ref, dst_ref=ref, send_sem=ssem, recv_sem=rsem,
            device_id=device, device_id_type=MESH).wait_recv())

    def drain(self, count=None):
        done = self.pending[:count]
        self.pending = self.pending[len(done):]
        for pred, make in done:
            when(pred, lambda make=make: make().wait_send())


def entry_barrier(p):
    bar = pltpu.get_barrier_semaphore()
    there = [p.at(i=p.member(t)) for t in range(1, TP)] + [p.at(y=1 - p.y)] + [p.at(z=q) for q in p.others]
    for device in there:
        pl.semaphore_signal(bar, inc=1, device_id=device, device_id_type=MESH)
    pl.semaphore_wait(bar, len(there))


def gather_pieces(width):
    half = width // 2
    return (
        (4, 0, LANES, "zxy"),
        (0, 0, half, "zxy"), (0, half, half, "zyx"),
        (2, 0, half, "xzy"), (2, half, half, "yzx"),
        (1, 0, half, "zxy"), (1, half, half, "zyx"),
        (3, 0, half, "xzy"), (3, half, half, "zyx"),
    )


def sum_pieces(width):
    half = width // 2
    return (
        (3, 0, half, "xzy"), (3, half, half, "yzx"),
        (1, 0, half, "zxy"), (1, half, half, "zyx"),
        (0, 0, half, "zxy"), (0, half, half, "yzx"),
        (2, 0, half, "zxy"), (2, half, half, "zyx"),
        (4, 0, LANES, "zxy"),
    )


def gather_sems(nz, count):
    D = pltpu.SemaphoreType.DMA
    return [D((count, 2, nz)), D((count, 2, nz)), D((count, nz)), D((count, nz)), D((count, 2, nz)),
            D((count, 2, nz)), D((count,)), D((count,))]


def gather_flow(p, cp, n, piece, W, sems):
    s_z, r_z, s_1, r_1, s_2, r_2, s_c, r_c = sems
    _, c0, cn, order = piece
    cs = slice(c0, c0 + cn)
    z, nz = p.z, p.nz
    a_is_x = order.index("x") < order.index("y")
    zfirst = order[0] == "z"

    def blk(a, b, zz):
        y, x = (b, a) if a_is_x else (a, b)
        return W.at[y, x, p.c, zz, :, cs]
    a, b = (p.x, p.y) if a_is_x else (p.y, p.x)
    dev_x, dev_y = p.at(i=p.member(2)), p.at(y=1 - p.y)
    dev_a, dev_b = (dev_x, dev_y) if a_is_x else (dev_y, dev_x)

    def core(aa, bb, zz):
        r = blk(aa, bb, zz)
        cp.send(r, r, s_c.at[n], r_c.at[n], p.at(i=p.member(1)), group=True)

    def zsend(aa):
        r = blk(aa, b, z)
        for to in p.others:
            cp.send(r, r, s_z.at[n, aa, to], r_z.at[n, aa, z], p.at(z=to))

    def asend(zz):
        r = blk(a, b, zz)
        cp.send(r, r, s_1.at[n, zz], r_1.at[n, zz], dev_a)

    def bsend(aa, zz):
        r = blk(aa, b, zz)
        cp.send(r, r, s_2.at[n, aa, zz], r_2.at[n, aa, zz], dev_b)

    asend(z)
    zsend(a)
    bsend(a, z)
    core(a, b, z)
    yield "first"
    if not zfirst:
        cp.arrived(blk(1 - a, b, z), s_1.at[n, z], r_1.at[n, z], p.at())
        zsend(1 - a)
        bsend(1 - a, z)
        core(1 - a, b, z)
    for zz in p.others:
        yield "z"
        for aa in ((a,) if zfirst else (a, 1 - a)):
            cp.arrived(blk(aa, b, zz), s_z.at[n, aa, zz], r_z.at[n, aa, zz], p.at())
            if zfirst:
                asend(zz)
            bsend(aa, zz)
            core(aa, b, zz)
    if zfirst:
        yield "second"
        for zz in (z,) + p.others:
            cp.arrived(blk(1 - a, b, zz), s_1.at[n, zz], r_1.at[n, zz], p.at())
            bsend(1 - a, zz)
            core(1 - a, b, zz)
    for zz in (z,) + p.others:
        yield "last axis"
        for aa in (a, 1 - a):
            cp.arrived(blk(aa, 1 - b, zz), s_2.at[n, aa, zz], r_2.at[n, aa, zz], p.at())
            core(aa, 1 - b, zz)
    yield "core"
    cp.arrived(W.at[:, :, 1 - p.c, :, :, cs], s_c.at[n], r_c.at[n], p.at())
    cp.pending.append((True, lambda: pltpu.make_async_remote_copy(
        src_ref=W.at[:, :, p.c, :, :, cs], dst_ref=W.at[:, :, p.c, :, :, cs], send_sem=s_c.at[n],
        recv_sem=r_c.at[n], device_id=p.at(i=p.member(1)), device_id_type=MESH)))


def sum_sems(nz, count):
    D = pltpu.SemaphoreType.DMA
    return [D((count,)), D((count,)), D((count, nz)), D((count, nz)), D((count, nz)), D((count, nz)),
            D((count, nz)), D((count, nz))]


def sum_scratch(nz, shard, pieces):
    return dict(
        one=[pltpu.VMEM((2, nz, shard, q[2]), BF) for q in pieces],
        two=[pltpu.VMEM((nz if q[3][0] == "z" else 1, shard, q[2]), BF) for q in pieces],
        path=[pltpu.VMEM((nz, 1 if q[3][0] == "z" else 2, shard, q[2]), BF) for q in pieces],
    )


def sum_flow(p, cp, n, piece, G, LC, L1, L2, LZ, out, sems):
    s_c, r_c, s_1, r_1, s_2, r_2, s_z, r_z = sems
    _, c0, cn, order = piece
    cs = slice(c0, c0 + cn)
    z = p.z
    targets = p.others[::-1] + (z,)
    zlast = order[0] == "z"
    b_is_y = order.index("x") < order.index("y")
    b, a = (p.y, p.x) if b_is_y else (p.x, p.y)
    dev_x, dev_y = p.at(i=p.member(2)), p.at(y=1 - p.y)
    dev_b, dev_a = (dev_y, dev_x) if b_is_y else (dev_x, dev_y)

    def g(bb, aa, zz):
        y, x = (bb, aa) if b_is_y else (aa, bb)
        return (y, x, p.c, zz, slice(None), cs)

    def f(v):
        return v.astype(F32)

    def lc(bb, aa, zz):
        y, x = (bb, aa) if b_is_y else (aa, bb)
        return (y, x, zz)

    def row(bb, zz, aa=None):
        aa = slice(None) if aa is None else pl.ds(aa, 1)
        y, x = (bb, aa) if b_is_y else (aa, bb)
        return G.at[y, x, p.c, zz, :, cs]
    cp.send(G.at[:, :, 1 - p.c, :, :, cs], LC, s_c.at[n], r_c.at[n], p.at(i=p.member(1)))
    LZ[z] = jnp.zeros(LZ.shape[1:], BF)
    yield
    cp.arrived(LC, s_c.at[n], r_c.at[n], p.at())
    for zz in targets:
        for aa in range(2):
            i = g(1 - b, aa, zz)
            G[i] = (f(G[i]) + f(LC[lc(1 - b, aa, zz)])).astype(BF)
        cp.send(row(1 - b, zz), L1.at[:, zz], s_1.at[n, zz], r_1.at[n, zz], dev_b)
    for zz in targets:
        for aa in range(2):
            i = g(b, aa, zz)
            G[i] = (f(G[i]) + f(LC[lc(b, aa, zz)])).astype(BF)
    if zlast:
        yield
        for zz in targets:
            cp.arrived(L1.at[:, zz], s_1.at[n, zz], r_1.at[n, zz], p.at())
            i = g(b, 1 - a, zz)
            G[i] = (f(G[i]) + f(L1[1 - a, zz])).astype(BF)
            cp.send(G.at[i], L2.at[zz], s_2.at[n, zz], r_2.at[n, zz], dev_a)

    def own(zz, k):
        if zlast:
            return f(G[g(b, a, zz)]) + f(L1[a, zz]) + f(L2[zz])
        return f(G[g(b, k, zz)]) + f(L1[k, zz])
    yield
    for zz in targets:
        if zlast:
            cp.arrived(L2.at[zz], s_2.at[n, zz], r_2.at[n, zz], p.at())
        else:
            cp.arrived(L1.at[:, zz], s_1.at[n, zz], r_1.at[n, zz], p.at())
        if zz is z:
            continue
        for k in range(1 if zlast else 2):
            G[g(b, a if zlast else k, zz)] = own(zz, k).astype(BF)
        cp.send(row(b, zz, a if zlast else None), LZ.at[z], s_z.at[n, zz], r_z.at[n, z], p.at(z=zz))
    yield
    for zz in p.others:
        cp.arrived(LZ.at[zz], s_z.at[n, zz], r_z.at[n, zz], p.at())

    def total(k):
        v = own(z, k)
        for zz in range(p.nz):
            v = v + f(LZ[zz, k])
        return v
    if zlast:
        out[:, cs] = total(0)
        return
    G[g(b, 1 - a, z)] = total(1 - a).astype(BF)
    cp.send(G.at[g(b, 1 - a, z)], L2.at[0], s_2.at[n, 0], r_2.at[n, 0], dev_a)
    out[:, cs] = total(a)
    yield
    cp.arrived(L2.at[0], s_2.at[n, 0], r_2.at[n, 0], p.at())
    out[:, cs] += f(L2[0])


def slot(ref, t):
    return ref.at[t // 2, t % 2]


def block_body(parts, nz, x_in, df_in, masks, b0, b1, b2, b3, b4, gus, ds,
               out_o, gx_o, ogu_o, od_o, m0, m1, m2, m3, m4, W0, W1, W2, W3, W4, SV32, SV16, s):
    p = Place(nz)
    z = p.z
    rows, width = x_in.shape
    shard = gus.shape[2]
    npos = 2 * nz
    count = rows // 2
    half = width // 2
    offs = [sum(parts[:k]) for k in range(len(parts))]
    CH = [(offs[k] * npos, parts[k] * npos) for k in range(len(parts))]
    K = len(parts)
    cp, cx, ct = Copies(), Copies(), Copies()
    cg = [Copies() for _ in range(K)]
    first, last = z == 0, z == nz - 1
    inner_l, inner_r = z > 0, z < nz - 1
    H, dF, WGU, WD, dHa, Zb, dAb, dGb = (s[k] for k in ("H", "dF", "WGU", "WD", "dHa", "Zb", "dAb", "dGb"))
    GGU = WGU
    GD, RY, ZGU, ZD, YD, LX, SX = (s[k] for k in ("GD", "RY", "ZGU", "ZD", "YD", "LX", "SX"))
    sem_h, s_p0, r_p0, s_z, r_z, s_y, r_y, s_dz, r_dz, s_dy, r_dy = (
        s[k] for k in ("sem_h", "s_p0", "r_p0", "s_z", "r_z", "s_y", "r_y", "s_dz", "r_dz", "s_dy", "r_dy"))
    s_gy, r_gy, s_gz, r_gz, s_gt, r_gt, s_ez, r_ez, s_ey, r_ey, s_x, r_x = (
        s[k] for k in ("s_gy", "r_gy", "s_gz", "r_gz", "s_gt", "r_gt", "s_ez", "r_ez", "s_ey", "r_ey", "s_x", "r_x"))
    sem = s["sem"]
    GN, SG, SM, PV, NX = (s[k] for k in ("GN", "SG", "SM", "PV", "NX"))
    GS = SM
    W = (W0, W1, W2, W3, W4)
    sums = (m0, m1, m2, m3, m4)

    def cols(k):
        return slice(CH[k][0], CH[k][0] + CH[k][1])

    def rws(k):
        return slice(offs[k], offs[k] + parts[k])

    class Load:
        def __init__(self, n, *pairs):
            self.copies = [pltpu.make_async_copy(a, b, sem.at[n + k]) for k, (a, b) in enumerate(pairs)]

        def start(self):
            for c in self.copies:
                c.start()
            return self

        def wait(self):
            for c in self.copies:
                c.wait()

    own_w = Load(0, *[(b, w.at[p.y, p.x, p.c, z]) for b, w in zip((b0, b1, b2, b3, b4), W)]).start()
    own_x = Load(5, (x_in, SX.at[0])).start()
    df_blocks = df_in
    own_df = Load(6, (df_blocks, slot(dF, 0))).start()
    own_gu = Load(7, (gus.at[p.i], WGU.at[p.y, p.i, z])).start()
    own_d = Load(8, *[(ds.at[rws(k)], WD[k].at[p.y, z]) for k in range(K)]).start()
    entry_barrier(p)

    ZGU[z] = jnp.zeros(ZGU.shape[1:], BF)
    for k in range(K):
        ZD[k][z] = jnp.zeros(ZD[k].shape[1:], BF)

    @pl.when(first)
    def _():
        PV[...] = jnp.zeros(PV.shape, BF)

    @pl.when(last)
    def _():
        NX[...] = jnp.zeros(NX.shape, BF)

    def p0(k):
        for t in (2, 3, 1):
            m = p.member(t)
            cg[k].send(gus.at[m, :, :, cols(k)], WGU.at[p.y, p.i, z, :, :, cols(k)],
                       s_p0.at[k, t - 1], r_p0.at[k, t - 1], p.at(i=m))

    def acts(dst, q):
        for t in (2, 1):
            cp.send(slot(dst, 0), slot(dst, t), sem_h.at[q, 0, t - 1], sem_h.at[q, 1, t - 1], p.at(i=p.member(t)))

    def acts_wait(dst, q, t):
        cp.arrived(slot(dst, t), sem_h.at[q, 0, t - 1], sem_h.at[q, 1, t - 1], p.at(i=p.member(t)))

    def acts_forward(dst, q):
        acts_wait(dst, q, 2)
        cp.send(slot(dst, 2), slot(dst, 3), sem_h.at[q, 0, 2], sem_h.at[q, 1, 2], p.at(i=p.member(1)))

    def gu_blk(k, y, zz):
        return WGU.at[y, :, zz, :, :, cols(k)]

    def ysend(k, zz):
        b = gu_blk(k, p.y, zz)
        cg[k].send(b, b, s_y.at[k, zz], r_y.at[k, zz], p.at(y=1 - p.y))
        b = WD[k].at[p.y, zz]
        cp.send(b, b, s_dy.at[k, zz], r_dy.at[k, zz], p.at(y=1 - p.y))

    def flow_ag(k):
        for t in (1, 2, 3):
            m = p.member(t)
            cp.arrived(WGU.at[p.y, m, z, :, :, cols(k)], s_p0.at[k, t - 1], r_p0.at[k, t - 1], p.at(i=m))
        for to in p.others:
            b = gu_blk(k, p.y, z)
            cg[k].send(b, b, s_z.at[k, to], r_z.at[k, z], p.at(z=to))
            b = WD[k].at[p.y, z]
            cp.send(b, b, s_dz.at[k, to], r_dz.at[k, z], p.at(z=to))
        yield
        ysend(k, z)
        for zz in p.others:
            yield
            cp.arrived(gu_blk(k, p.y, zz), s_z.at[k, zz], r_z.at[k, zz], p.at())
            cp.arrived(WD[k].at[p.y, zz], s_dz.at[k, zz], r_dz.at[k, zz], p.at())
            ysend(k, zz)
        yield
        for zz in (z,) + p.others:
            cp.arrived(gu_blk(k, 1 - p.y, zz), s_y.at[k, zz], r_y.at[k, zz], p.at())
            cp.arrived(WD[k].at[1 - p.y, zz], s_dy.at[k, zz], r_dy.at[k, zz], p.at())

    targets = p.others[::-1] + (z,)

    def flow_rs_gu(k):
        c = cols(k)
        for zz in targets:
            cp.send(GGU.at[1 - p.y, :, zz, :, :, c], RY.at[:, zz, :, :, c],
                    s_gy.at[k, zz], r_gy.at[k, zz], p.at(y=1 - p.y))
        for zz in p.others[::-1]:
            yield
            cp.arrived(RY.at[:, zz, :, :, c], s_gy.at[k, zz], r_gy.at[k, zz], p.at())
            for j in range(TP):
                GGU[p.y, j, zz, :, :, c] = (
                    GGU[p.y, j, zz, :, :, c].astype(F32) + RY[j, zz, :, :, c].astype(F32)).astype(BF)
            cp.send(GGU.at[p.y, :, zz, :, :, c], ZGU.at[z, :, :, :, c], s_gz.at[k, zz], r_gz.at[k, z], p.at(z=zz))
        yield
        cp.arrived(RY.at[:, z, :, :, c], s_gy.at[k, z], r_gy.at[k, z], p.at())
        for zz in p.others:
            cp.arrived(ZGU.at[zz, :, :, :, c], s_gz.at[k, zz], r_gz.at[k, zz], p.at())
        for j in range(TP):
            v = GGU[p.y, j, z, :, :, c].astype(F32) + RY[j, z, :, :, c].astype(F32)
            for zz in range(nz):
                v = v + ZGU[zz, j, :, :, c].astype(F32)
            GGU[p.y, j, z, :, :, c] = v.astype(BF)
        for t in (2, 3, 1):
            m = p.member(t)
            cp.send(GGU.at[p.y, m, z, :, :, c], ogu_o.at[p.i, :, :, c], s_gt.at[k, t - 1], r_gt.at[k, t - 1],
                    p.at(i=m))
        own_out.append(Load(12 + k, (GGU.at[p.y, p.i, z, :, :, c], ogu_o.at[p.i, :, :, c])).start())
        yield
        for t in (1, 2, 3):
            m = p.member(t)
            cp.arrived(ogu_o.at[m, :, :, c], s_gt.at[k, t - 1], r_gt.at[k, t - 1], p.at(i=m))

    def flow_rs_d(k):
        G, L = GD[k], ZD[k]
        for zz in p.others[::-1]:
            cp.send(G.at[:, zz], L.at[z], s_ez.at[k, zz], r_ez.at[k, z], p.at(z=zz))
        yield
        for zz in p.others:
            cp.arrived(L.at[zz], s_ez.at[k, zz], r_ez.at[k, zz], p.at())
        for y in range(2):
            v = G[y, z].astype(F32)
            for zz in range(nz):
                v = v + L[zz, y].astype(F32)
            G[y, z] = v.astype(BF)
        cp.send(G.at[1 - p.y, z], YD[k], s_ey.at[k], r_ey.at[k], p.at(y=1 - p.y))
        yield
        cp.arrived(YD[k], s_ey.at[k], r_ey.at[k], p.at())
        od_o[rws(k), :] = G[p.y, z].astype(F32) + YD[k][...].astype(F32)

    live, own_out = [], []

    def pump(n=1, which=None):
        for _ in range(n):
            for f in list(live if which is None else which):
                if f in live and next(f, "end") == "end":
                    live.remove(f)

    def run(*gens):
        for g in gens:
            for _ in g:
                pass
            if g in live:
                live.remove(g)

    own_w.wait()
    gp = gather_pieces(width)
    gather = [gather_flow(p, cp, n, q, W[q[0]], s["gather"]) for n, q in enumerate(gp)]
    states = {}

    def gather_to(*stops):
        left = list(gather)
        while left:
            for f in list(left):
                if states.get(f) in stops:
                    left.remove(f)
                else:
                    states[f] = next(f)
    gather_to("first")
    own_gu.wait()
    own_d.wait()
    own_df.wait()
    for k in range(K):
        p0(k)
    gather_to("z")
    ag = [flow_ag(k) for k in range(K)]
    for g in ag:
        next(g)
    gather_to("last axis")
    acts(dF, 1)
    for g in ag:
        next(g)
    gather_to("core")

    def need(*panels):
        for f, q in zip(gather, gp):
            if q[0] in panels:
                next(f, None)

    def panel(q, buf, n):
        return Load(n, *[(W[q].at[:, :, :, :, :, h * half:(h + 1) * half], buf.at[:, h]) for h in range(2)])

    def half_panel(buf, h):
        return buf[:, h].reshape(width, half)

    need(4)
    Load(20, (W4, SM)).start().wait()
    GN[...] = SM[...].reshape(width, LANES).astype(F32).T[:8]
    need(0)
    wb = panel(0, dAb, 21).start()
    own_x.wait()

    def norm(v):
        inv = lax.rsqrt(jnp.mean(v * v, axis=-1, keepdims=True) + eps)
        return inv, v * inv

    def tiles(size):
        return [slice(t * size, (t + 1) * size) for t in range(rows // size)]

    def norm_one(m, _):
        rs = pl.ds(pl.multiple_of(m * 128, 128), 128)
        _, n1 = norm(SX[0, rs].astype(F32))
        SX[1, rs] = (n1 * GN[0:1]).astype(BF)
        return 0
    lax.fori_loop(0, rows // 128, norm_one, 0)
    save_h1 = Load(30, (SX.at[1], SV16.at[0])).start()

    def project(buf, dst):
        for h in range(2):
            dHa[dst, :, h * half:(h + 1) * half] = mm(SX[1], half_panel(buf, h), NN)
    need(2)
    wu = panel(2, dGb, 23).start()
    wb.wait()
    project(dAb, 0)
    need(1)
    wc = panel(1, dAb, 21).start()
    wu.wait()
    project(dGb, 2)
    save_bu = Load(31, (dHa.at[0], SV32.at[0]), (dHa.at[2], SV32.at[2])).start()

    def make_bx(m, _):
        rs = pl.ds(pl.multiple_of(m * 128, 128), 128)
        SX[2, rs] = (dHa[0, rs] * dHa[2, rs]).astype(BF)
        return 0
    lax.fori_loop(0, rows // 128, make_bx, 0)
    s_h, r_h = s["s_h"], s["r_h"]
    for m in range(2):
        cp.send(SX.at[2, pl.ds((m + 1) * count - 16, 16)], PV.at[m], s_h.at[0, m], r_h.at[0, m],
                p.at(z=z + 1), inner_r)
    save_bx = Load(33, (SX.at[2], SV16.at[1])).start()
    need(3)
    wo = panel(3, dGb, 23).start()
    wc.wait()
    project(dAb, 1)
    save_c = Load(34, (dHa.at[1], SV32.at[1])).start()
    for m in range(2):
        cp.arrived(PV.at[m], s_h.at[0, m], r_h.at[0, m], p.at(), inner_l)

    def earlier(v, prev, back):
        r = lax.broadcasted_iota(jnp.int32, v.shape, 0)
        n = prev.shape[0]
        moved = pltpu.roll(v, back, 0)
        moved = jnp.where(r == back - 1, prev[n - 1:n], moved)
        return jnp.where(r == 0, prev[n - back:n - back + 1], moved)

    def later(v, after, ahead):
        r = lax.broadcasted_iota(jnp.int32, v.shape, 0)
        n = v.shape[0]
        moved = pltpu.roll(v, n - ahead, 0)
        moved = jnp.where(r == n - ahead, after[0:1], moved)
        return jnp.where(r == n - 1, after[ahead - 1:ahead], moved)

    lanes = 256
    nl = width // lanes

    def conv(q, _):
        m, c = q // nl, q % nl
        ls = pl.ds(pl.multiple_of(c * lanes, lanes), lanes)
        rs = pl.ds(pl.multiple_of(m * count, count), count)
        v = SX[2, rs, ls].astype(F32)
        prev = PV[m, :, ls].astype(F32)
        mk = masks[m]
        total = GN[2:3, ls] * earlier(v, prev, 2) * mk[:count, 0:1]
        total = total + GN[3:4, ls] * earlier(v, prev, 1) * mk[:count, 1:2]
        total = total + GN[4:5, ls] * v * mk[:count, 2:3]
        dHa[3, rs, ls] = total
        LX[0, rs, ls] = (dHa[1, rs, ls] * total).astype(BF)
        return 0
    lax.fori_loop(0, 2 * nl, conv, 0)
    save_cv = Load(35, (dHa.at[3], SV32.at[3]), (LX.at[0], SV16.at[2])).start()
    save_bu.wait()
    wo.wait()
    for h in range(2):
        hs = slice(h * half, (h + 1) * half)
        dHa[0, :, hs] = SX[0, :, hs].astype(F32) + mm(LX[0], half_panel(dGb, h), NN)

    def norm_two(m, _):
        rs = pl.ds(pl.multiple_of(m * nz * shard, nz * shard), nz * shard)
        _, n2 = norm(dHa[0, rs])
        H[0, 0, m // 2, m % 2] = (n2 * GN[1:2]).astype(BF).reshape(nz, shard, width)
        return 0
    lax.fori_loop(0, 4, norm_two, 0)
    save_r = Load(37, (dHa.at[0], SV32.at[4])).start()
    save_cv.wait()
    acts(H, 0)
    save_h1.wait()
    save_bx.wait()
    save_c.wait()
    save_r.wait()
    live.extend(ag)
    pump(3, ag[:1])

    def val(ref, t):
        return ref[t // 2, t % 2].reshape(rows, -1)

    def blocks(v):
        return v.reshape(2, 2, nz, shard, v.shape[-1])

    def fwd_mid(k, t):
        c0, cn = CH[k]
        c = cols(k)
        wg = WGU[:, :, :, 0, :, c].reshape(width, cn)
        wu = WGU[:, :, :, 1, :, c].reshape(width, cn)
        wd = WD[k][...].reshape(cn, width)
        a = mm(val(H, t), wg, NN)
        g = mm(val(H, t), wu, NN)
        dz = mm(val(dF, t), wd, NT)
        sg = 1.0 / (1.0 + jnp.exp(-a))
        act = a * sg
        Zb[t, :, :, :, :, c] = blocks((act * g).astype(BF))
        da = (dz * g * sg * (1.0 + a * (1.0 - sg))).astype(BF)
        dg = (dz * act).astype(BF)
        dAb[t // 2, t % 2, :, :, :, :, :cn] = blocks(da)
        dGb[t // 2, t % 2, :, :, :, :, :cn] = blocks(dg)
        d = mm(da, wg, NT) + mm(dg, wu, NT)
        if k == 0:
            dHa[t] = d
        else:
            dHa[t] += d

    def ffn_out(t):
        f = None
        for k in range(K):
            v = mm(Zb[t, :, :, :, :, cols(k)].reshape(rows, CH[k][1]), WD[k][...].reshape(CH[k][1], width), NN)
            f = v if f is None else f + v
        return f

    tok = TP * rows

    def grads(k):
        c0, cn = CH[k]
        c = cols(k)
        for w, src in ((0, dAb), (1, dGb)):
            def body(m, _, w=w, src=src):
                y, j = m // 2, (m % 2) * 2
                f = 2 * nz * shard
                ms = pl.ds(pl.multiple_of(m * f, f), f)
                v = mm(H[:, :, :, :, :, :, ms].reshape(tok, f), src[:, :, :, :, :, :, :cn].reshape(tok, cn), TN)
                GGU[y, pl.ds(j, 2), :, w, :, c] = v.astype(BF).reshape(2, nz, shard, cn)
                return 0
            lax.fori_loop(0, TP, body, 0)
        r = parts[k]
        for b in range(cn // 128):
            zb = Zb[:, :, :, :, :, c0 + b * 128:c0 + (b + 1) * 128].reshape(tok, 128)
            v = mm(zb, dF[...].reshape(tok, width), TN).astype(BF)
            lo = b * 128
            while lo < (b + 1) * 128:
                pos, q = lo // r, lo % r
                n = min(r - q, (b + 1) * 128 - lo)
                GD[k][pos // nz, pos % nz, q:q + n] = v[lo - b * 128:lo - b * 128 + n]
                lo += n

    def x_land(q, e):
        return LX.at[2 + q] if e == 2 else LX.at[e]

    def x_send1(q, e, value):
        SX[e] = value.astype(BF)
        cx.send(SX.at[e], x_land(q, e), s_x.at[q, e], r_x.at[q, e], p.at(i=p.member(1)))

    def x_wait(q, e):
        cx.arrived(x_land(q, e), s_x.at[q, e], r_x.at[q, e], p.at(i=p.member(2 if e == 2 else 1)))

    def x_send2(q, acc):
        x_wait(q, 1)
        SX[2] = (acc[...] + LX[1].astype(F32)).astype(BF)
        cx.send(SX.at[2], x_land(q, 2), s_x.at[q, 2], r_x.at[q, 2], p.at(i=p.member(2)))

    def x_add(q, acc, e):
        x_wait(q, e)
        acc[...] += x_land(q, e)[...].astype(F32)

    acts_forward(dF, 1)
    for k in range(K):
        run(ag[k])
        if k == 0:
            acts_wait(H, 0, 1)
            acts_wait(dF, 1, 1)
            fwd_mid(0, 0)
            fwd_mid(0, 1)
            pump(1, ag[1:2])
            acts_forward(H, 0)
            acts_wait(dF, 1, 3)
            fwd_mid(0, 2)
            pump(1, ag[1:2])
            acts_wait(H, 0, 3)
            fwd_mid(0, 3)
            pump(1, ag[1:2])
            pump(1, ag[2:])
        else:
            def tbody(n, _, k=k):
                fwd_mid(k, n)
                return 0
            lax.fori_loop(0, TP, tbody, 0)
        if k == 1:
            pump(2, ag[2:])
        if k == K - 1:
            x_send1(0, 0, dHa[1])
            x_send1(0, 1, dHa[3])
        cg[k].drain()
        if k == K - 1:
            cp.drain()
        grads(k)
        for g in (flow_rs_d(k), flow_rs_gu(k)):
            next(g)
            live.append(g)
        pump(1)
    wo = panel(3, dAb, 21).start()
    x_send2(0, dHa.at[2])
    x_add(0, dHa.at[0], 0)
    pl.semaphore_signal(s["ready"], inc=1, device_id=p.at(i=p.member(1)), device_id_type=MESH)
    pr = Load(40, (SV32.at[4], dHa.at[2])).start()
    pump(1)
    dHa[1] = ffn_out(2)
    dHa[3] = ffn_out(0)
    pump(1)
    f1, f3 = ffn_out(1), ffn_out(3)
    cx.drain(2)
    pl.semaphore_wait(s["ready"], 1)
    x_send1(1, 0, f1)
    x_send1(1, 1, f3)
    pump(1)
    x_add(0, dHa.at[0], 2)
    cx.drain(1)
    x_send2(1, dHa.at[1])
    x_add(1, dHa.at[3], 0)

    pc = Load(41, (SV32.at[1], dHa.at[1])).start()
    cx.drain(2)
    py = Load(42, (SV16.at[2], SX.at[0]), (SV16.at[0], SX.at[1])).start()
    pr.wait()
    SG[...] = jnp.zeros(SG.shape, F32)

    def back_two(m, _):
        n = nz * shard
        rs = pl.ds(pl.multiple_of(m * n, n), n)
        r = dHa[2, rs]
        dHa[3, rs] += r
        inv, n2 = norm(r)
        d = dHa[0, rs]
        SG[1:2] += jnp.sum(d * n2, axis=0, keepdims=True)
        dn = d * GN[1:2]
        df = dF[0, 0, m // 2, m % 2].reshape(n, width).astype(F32)
        dr = df + inv * (dn - n2 * jnp.mean(dn * n2, axis=-1, keepdims=True))
        dHa[0, rs] = dr
        WD[0][m // 2, pl.ds((m % 2) * (nz // 2), nz // 2)] = dr.astype(BF).reshape(nz // 2, parts[0], width)
        return 0
    lax.fori_loop(0, 4, back_two, 0)
    pcv = Load(44, (SV32.at[3], dHa.at[2])).start()
    pump(1)
    wo.wait()
    pc.wait()
    pcv.wait()
    wbk = panel(0, dGb, 23).start()

    def back_y(m, _):
        rs = pl.ds(pl.multiple_of(m * count, count), count)
        do = WD[0][m].reshape(count, width)
        dy = mm(do[:, :half], half_panel(dAb, 0), NT) + mm(do[:, half:], half_panel(dAb, 1), NT)
        LX[1, rs] = (dy * dHa[2, rs]).astype(BF)
        WD[1][m] = (dy * dHa[1, rs]).astype(BF).reshape(nz, parts[0], width)
        return 0
    lax.fori_loop(0, 2, back_y, 0)
    wck = panel(1, dAb, 21).start()
    for m in range(2):
        cp.send(WD[1].at[m, 0, pl.ds(0, 16)], NX.at[m], s_h.at[1, m], r_h.at[1, m], p.at(z=z - 1), inner_l)
    pu = Load(41, (SV32.at[2], dHa.at[1])).start()
    pb = Load(44, (SV32.at[0], dHa.at[2])).start()

    panels = (H.at[0], H.at[1], dF.at[0], dF.at[1], GS)
    sp = sum_pieces(width)

    def start_sums(q):
        for n, piece in enumerate(sp):
            if piece[0] != q:
                continue
            _, c0, cn, _ = piece
            lc = Zb.at[q, :, :, :, :, pl.ds(c0, cn)] if q < 4 else Zb.at[3, :, :, :, :, pl.ds(width, LANES)]
            g = sum_flow(p, ct, n, piece, panels[q], lc, s["land"]["one"][n], s["land"]["two"][n],
                         s["land"]["path"][n], sums[q], s["sum"])
            next(g)
            live.append(g)

    def weight_grad(q, left, right):
        def body(m, _):
            f = 2 * nz * shard
            ms = pl.ds(pl.multiple_of(m * f, f), f)
            v = mm(left(ms), right(), TN)
            panels[q][m // 2, m % 2] = v.astype(BF).reshape(2, nz, shard, width)
            return 0
        lax.fori_loop(0, width // (2 * nz * shard), body, 0)
        start_sums(q)

    py.wait()
    weight_grad(3, lambda ms: SX[0, :, ms], lambda: WD[0][...].reshape(rows, width))
    pump(1)
    weight_grad(1, lambda ms: SX[1, :, ms], lambda: LX[1])
    pbx = Load(42, (SV16.at[1], SX.at[0])).start()
    pump(1)
    for m in range(2):
        cp.arrived(NX.at[m], s_h.at[1, m], r_h.at[1, m], p.at(), inner_r)
    pu.wait()
    pb.wait()
    pbx.wait()

    def back_conv(q, _):
        m, c = q // nl, q % nl
        ls = pl.ds(pl.multiple_of(c * lanes, lanes), lanes)
        rs = pl.ds(pl.multiple_of(m * count, count), count)
        v = SX[0, rs, ls].astype(F32)
        prev = PV[m, :, ls].astype(F32)
        dcv = WD[1][m, :, :, ls].reshape(count, lanes).astype(F32)
        after = NX[m, :, ls].astype(F32)
        mk = masks[m]
        w0, w1, w2 = (dcv * mk[:count, t:t + 1] for t in range(3))
        SG[2:3, ls] += jnp.sum(w0 * earlier(v, prev, 2), axis=0, keepdims=True)
        SG[3:4, ls] += jnp.sum(w1 * earlier(v, prev, 1), axis=0, keepdims=True)
        SG[4:5, ls] += jnp.sum(w2 * v, axis=0, keepdims=True)
        tail = mk[count:count + 8]
        d = GN[2:3, ls] * later(w0, after[:8] * tail[:, 0:1], 2)
        d = d + GN[3:4, ls] * later(w1, after[:8] * tail[:, 1:2], 1)
        d = d + GN[4:5, ls] * w2
        LX[0, rs, ls] = (d * dHa[1, rs, ls]).astype(BF)
        LX[2, rs, ls] = (d * dHa[2, rs, ls]).astype(BF)
        return 0
    lax.fori_loop(0, 2 * nl, back_conv, 0)
    pump(1)
    weight_grad(0, lambda ms: SX[1, :, ms], lambda: LX[0])
    pump(1)
    weight_grad(2, lambda ms: SX[1, :, ms], lambda: LX[2])
    pump(1)
    px = Load(42, (x_in, SX.at[1])).start()
    for e, buf, w in ((0, dGb, wbk), (1, dAb, wck)):
        w.wait()
        v = mm(LX[e, :, :half], half_panel(buf, 0), NT) + mm(LX[e, :, half:], half_panel(buf, 1), NT)
        if e == 0:
            dHa[1] = v
            wuk = panel(2, dGb, 23).start()
        else:
            dHa[1] += v
        pump(1)
    wuk.wait()
    dHa[1] += mm(LX[2, :, :half], half_panel(dGb, 0), NT) + mm(LX[2, :, half:], half_panel(dGb, 1), NT)
    px.wait()

    def back_one(m, _):
        rs = pl.ds(pl.multiple_of(m * 128, 128), 128)
        inv, n1 = norm(SX[1, rs].astype(F32))
        d = dHa[1, rs]
        SG[0:1] += jnp.sum(d * n1, axis=0, keepdims=True)
        dn = d * GN[0:1]
        SX[0, rs] = (dHa[0, rs] + inv * (dn - n1 * jnp.mean(dn * n1, axis=-1, keepdims=True))).astype(BF)
        return 0
    lax.fori_loop(0, rows // 128, back_one, 0)
    save_gx = Load(30, (SX.at[0], gx_o)).start()
    rest = jnp.zeros((LANES - 8, width), F32)
    GS[...] = jnp.concatenate([SG[...], rest], axis=0).T.astype(BF).reshape(GS.shape)
    start_sums(4)
    pump(1)
    x_add(1, dHa.at[3], 2)

    def finish(m, _):
        rs = pl.ds(pl.multiple_of(m * 128, 128), 128)
        SX[1, rs] = dHa[3, rs].astype(BF)
        return 0
    lax.fori_loop(0, rows // 128, finish, 0)
    save_out = Load(31, (SX.at[1], out_o)).start()
    while live:
        pump(1)
    save_gx.wait()
    save_out.wait()
    for c in own_out:
        c.wait()
    cp.drain()
    ct.drain()
    cx.drain()


def block_call(x, df, masks, blocks, gus, ds, parts, nz, cid):
    rows, width = x.shape
    shard, cols = gus.shape[2], gus.shape[3]
    K = len(parts)
    dr = ds.shape[0]
    V = pl.BlockSpec(memory_space=pltpu.VMEM)
    A = pl.BlockSpec(memory_space=pl.ANY)
    D = pltpu.SemaphoreType.DMA
    M = pltpu.VMEM
    maxc = max(parts) * 2 * nz
    sp = sum_pieces(width)
    ngather = len(gather_pieces(width))
    scratch = dict(
        H=M((2, 2, 2, 2, nz, shard, width), BF),
        dF=M((2, 2, 2, 2, nz, shard, width), BF),
        WGU=M((2, TP, nz, 2, shard, cols), BF),
        WD=[M((2, nz, r, width), BF) for r in parts],
        dHa=M((TP, rows, width), F32),
        Zb=M((TP, 2, 2, nz, shard, cols), BF),
        dAb=M((2, 2, 2, 2, nz, shard, maxc), BF),
        dGb=M((2, 2, 2, 2, nz, shard, maxc), BF),
        GD=[M((2, nz, r, width), BF) for r in parts],
        RY=M((TP, nz, 2, shard, cols), BF),
        ZGU=M((nz, TP, 2, shard, cols), BF),
        ZD=[M((nz, 2, r, width), BF) for r in parts],
        YD=[M((r, width), BF) for r in parts],
        LX=M((4, rows, width), BF),
        SX=M((3, rows, width), BF),
        GN=M((8, width), F32),
        SG=M((8, width), F32),
        SM=M((2, 2, 2, nz, shard, LANES), BF),
        PV=M((2, 16, width), BF),
        NX=M((2, 16, width), BF),
        land=sum_scratch(nz, shard, sp),
        gather=gather_sems(nz, ngather),
        sum=sum_sems(nz, len(sp)),
        sem=D((48,)), sem_h=D((2, 2, 3)), s_h=D((2, 2)), r_h=D((2, 2)),
        s_p0=D((K, 3)), r_p0=D((K, 3)),
        s_z=D((K, nz)), r_z=D((K, nz)), s_y=D((K, nz)), r_y=D((K, nz)),
        s_dz=D((K, nz)), r_dz=D((K, nz)), s_dy=D((K, nz)), r_dy=D((K, nz)),
        s_gy=D((K, nz)), r_gy=D((K, nz)), s_gz=D((K, nz)), r_gz=D((K, nz)),
        s_gt=D((K, 3)), r_gt=D((K, 3)),
        s_ez=D((K, nz)), r_ez=D((K, nz)), s_ey=D((K,)), r_ey=D((K,)),
        s_x=D((2, 3)), r_x=D((2, 3)), ready=pltpu.SemaphoreType.REGULAR,
    )
    S = jax.ShapeDtypeStruct
    wide = [width] * 4 + [LANES]
    outs = pl.pallas_call(
        functools.partial(block_body, parts, nz),
        name="block",
        out_shape=[
            S((rows, width), BF), S((rows, width), BF),
            S((TP, 2, shard, cols), BF), S((dr, width), F32),
            *[S((shard, w), F32) for w in wide],
            *[S((2, 2, 2, nz, shard, w), BF) for w in wide],
            S((5, rows, width), F32), S((3, rows, width), BF),
        ],
        in_specs=[A, A] + [V] * 6 + [A, A],
        out_specs=[A, A, A] + [V] * 6 + [A] * 7,
        scratch_shapes=[scratch],
        compiler_params=pltpu.CompilerParams(
            collective_id=cid, has_side_effects=True, vmem_limit_bytes=67_000_000),
    )(x, df.reshape(2, 2, nz, shard, width), masks, *blocks, gus, ds)
    return outs[:9]


def shifted(block, axis, distance):
    devices = range(lax.axis_size(axis))
    route = [(i - distance, i) for i in devices if i - distance in devices]
    return lax.ppermute(block, axis, route)


def matmul(left, right):
    return jnp.dot(left, right, preferred_element_type=jnp.float32)


def norm_parts(values):
    inverse = lax.rsqrt(jnp.mean(values * values, axis=-1, keepdims=True) + eps)
    return (inverse, values * inverse)


def norm_back(grad_hidden, normed, inverse, gain):
    grad_normed = grad_hidden * gain
    inner_mean = jnp.mean(grad_normed * normed, axis=-1, keepdims=True)
    return inverse * (grad_normed - normed * inner_mean)


def plain_device(
    tokens,
    segments,
    ln1_gain,
    in_weight,
    conv_kernel,
    out_weight,
    ln2_gain,
    gate_weight,
    up_weight,
    down_weight,
    cotangent,
):
    micro_count = tokens.shape[0]
    row_count = tokens.shape[2]
    width = tokens.shape[3]
    taps = conv_kernel.shape[0]
    offset = lax.axis_index("seq") * row_count
    low_gain1 = ln1_gain.astype(jnp.bfloat16)
    low_in = in_weight.astype(jnp.bfloat16)
    low_kernel = conv_kernel.astype(jnp.bfloat16)
    low_out = out_weight.astype(jnp.bfloat16)
    low_gain2 = ln2_gain.astype(jnp.bfloat16)
    low_gate = gate_weight.astype(jnp.bfloat16)
    low_up = up_weight.astype(jnp.bfloat16)
    low_down = down_weight.astype(jnp.bfloat16)
    shard_totals = None
    full_totals = None
    out_list = []
    grad_list = []
    for micro_index in range(micro_count):
        weights = (
            lax.all_gather(low_gain1, ("dp", "seq"), axis=0, tiled=True),
            lax.all_gather(low_in, ("dp", "seq"), axis=0, tiled=True),
            lax.all_gather(low_kernel, ("dp", "seq"), axis=1, tiled=True),
            lax.all_gather(low_out, ("dp", "seq"), axis=0, tiled=True),
            lax.all_gather(low_gain2, ("dp", "seq"), axis=0, tiled=True),
            lax.all_gather(low_gate, ("dp", "seq"), axis=0, tiled=True),
            lax.all_gather(low_up, ("dp", "seq"), axis=0, tiled=True),
            lax.all_gather(low_down, ("dp", "seq"), axis=0, tiled=True),
        )
        gain_one = weights[0].astype(jnp.float32)
        kernel = weights[2].astype(jnp.float32)
        gain_two = weights[4].astype(jnp.float32)
        seg_line = segments[micro_index, 0]
        fill = jnp.full((2,), -1, jnp.int32)
        seg_pad = jnp.concatenate([fill, seg_line, fill])
        window = lax.dynamic_slice_in_dim(seg_pad, offset, row_count + 4)
        masks = [
            (window[tap : tap + row_count + 2] == window[2 : row_count + 4]).astype(jnp.float32)
            for tap in range(taps)
        ]
        tokens_f = tokens[micro_index, 0].astype(jnp.float32)
        inverse_one, normed_one = norm_parts(tokens_f)
        hidden_one = (normed_one * gain_one).astype(jnp.bfloat16)
        projected = matmul(hidden_one, weights[1])
        b_part = projected[:, :width]
        c_part = projected[:, width : 2 * width]
        x_part = projected[:, 2 * width :]
        mixed = (b_part * x_part).astype(jnp.bfloat16)
        prev_rows = shifted(mixed[row_count - 2 :], "seq", 1)
        extended = jnp.concatenate([prev_rows, mixed], axis=0).astype(jnp.float32)
        conv_out = jnp.zeros((row_count, width), jnp.float32)
        for tap in range(taps):
            conv_out = (
                conv_out
                + kernel[tap] * extended[tap : tap + row_count] * masks[tap][:row_count, None]
            )
        gated = (c_part * conv_out).astype(jnp.bfloat16)
        resid = tokens_f + matmul(gated, weights[3])
        inverse_two, normed_two = norm_parts(resid)
        hidden_two = (normed_two * gain_two).astype(jnp.bfloat16)
        gate_pre = matmul(hidden_two, weights[5])
        up_pre = matmul(hidden_two, weights[6])
        sigmoid_gate = jax.nn.sigmoid(gate_pre)
        activated = gate_pre * sigmoid_gate
        inner = (activated * up_pre).astype(jnp.bfloat16)
        ffn_out = matmul(inner, weights[7])
        out_list.append((resid + ffn_out).astype(jnp.bfloat16))
        back_weights = (
            lax.all_gather(low_gain1, ("dp", "seq"), axis=0, tiled=True),
            lax.all_gather(low_in, ("dp", "seq"), axis=0, tiled=True),
            lax.all_gather(low_kernel, ("dp", "seq"), axis=1, tiled=True),
            lax.all_gather(low_out, ("dp", "seq"), axis=0, tiled=True),
            lax.all_gather(low_gain2, ("dp", "seq"), axis=0, tiled=True),
            lax.all_gather(low_gate, ("dp", "seq"), axis=0, tiled=True),
            lax.all_gather(low_up, ("dp", "seq"), axis=0, tiled=True),
            lax.all_gather(low_down, ("dp", "seq"), axis=0, tiled=True),
        )
        grad_final = cotangent[micro_index, 0]
        grad_inner = matmul(grad_final, back_weights[7].T)
        part_down = matmul(inner.T, grad_final)
        grad_gate_pre = (
            grad_inner * up_pre * sigmoid_gate * (1.0 + gate_pre * (1.0 - sigmoid_gate))
        ).astype(jnp.bfloat16)
        grad_up_pre = (grad_inner * activated).astype(jnp.bfloat16)
        grad_hidden_two = matmul(grad_gate_pre, back_weights[5].T) + matmul(
            grad_up_pre, back_weights[6].T
        )
        part_gate = matmul(hidden_two.T, grad_gate_pre)
        part_up = matmul(hidden_two.T, grad_up_pre)
        part_gain2 = jnp.sum(grad_hidden_two * normed_two, axis=0)
        grad_resid = grad_final.astype(jnp.float32) + norm_back(
            grad_hidden_two, normed_two, inverse_two, gain_two
        )
        grad_branch = grad_resid.astype(jnp.bfloat16)
        grad_gated = matmul(grad_branch, back_weights[3].T)
        part_out = matmul(gated.T, grad_branch)
        grad_c = grad_gated * conv_out
        grad_conv = (grad_gated * c_part).astype(jnp.bfloat16)
        next_rows = shifted(grad_conv[:2], "seq", -1)
        grad_extended = jnp.concatenate([grad_conv, next_rows], axis=0).astype(jnp.float32)
        grad_mixed = jnp.zeros((row_count, width), jnp.float32)
        kernel_terms = []
        for tap in range(taps):
            weighted = grad_extended * masks[tap][:, None]
            grad_mixed = grad_mixed + kernel[tap] * weighted[2 - tap : 2 - tap + row_count]
            kernel_terms.append(
                jnp.sum(weighted[:row_count] * extended[tap : tap + row_count], axis=0)
            )
        part_kernel = jnp.stack(kernel_terms, axis=0)
        grad_proj = jnp.concatenate(
            [grad_mixed * x_part, grad_c, grad_mixed * b_part], axis=1
        ).astype(jnp.bfloat16)
        grad_hidden_one = matmul(grad_proj, back_weights[1].T)
        part_in = matmul(hidden_one.T, grad_proj)
        part_gain1 = jnp.sum(grad_hidden_one * normed_one, axis=0)
        grad_input = grad_resid + norm_back(grad_hidden_one, normed_one, inverse_one, gain_one)
        grad_list.append(grad_input.astype(jnp.bfloat16))
        parts = (
            part_gain1,
            part_in,
            part_kernel,
            part_out,
            part_gain2,
            part_gate,
            part_up,
            part_down,
        )
        full_totals = (
            parts
            if full_totals is None
            else tuple((first + second for first, second in zip(full_totals, parts)))
        )
    shard_totals = (
        lax.psum_scatter(full_totals[0], ("dp", "seq"), scatter_dimension=0, tiled=True),
        lax.psum_scatter(full_totals[1], ("dp", "seq"), scatter_dimension=0, tiled=True),
        lax.psum_scatter(full_totals[2], ("dp", "seq"), scatter_dimension=1, tiled=True),
        lax.psum_scatter(full_totals[3], ("dp", "seq"), scatter_dimension=0, tiled=True),
        lax.psum_scatter(full_totals[4], ("dp", "seq"), scatter_dimension=0, tiled=True),
        lax.psum_scatter(full_totals[5], ("dp", "seq"), scatter_dimension=0, tiled=True),
        lax.psum_scatter(full_totals[6], ("dp", "seq"), scatter_dimension=0, tiled=True),
        lax.psum_scatter(full_totals[7], ("dp", "seq"), scatter_dimension=0, tiled=True),
    )
    output = jnp.stack(out_list, axis=0)[:, None]
    grad_tokens = jnp.stack(grad_list, axis=0)[:, None]
    return (
        output,
        grad_tokens,
        shard_totals[0],
        shard_totals[1],
        shard_totals[2],
        shard_totals[3],
        shard_totals[4],
        shard_totals[5],
        shard_totals[6],
        shard_totals[7],
    )


def cut_columns(w, parts, ny, nz):
    rows, shard = w.shape[0], w.shape[1] // (ny * TP * nz)
    cut = w.astype(BF).reshape(rows, ny, TP, nz, shard)
    pieces, start = [], 0
    for size in parts:
        piece = cut[..., start : start + size].transpose(2, 0, 1, 3, 4)
        pieces.append(piece.reshape(TP, rows, ny * nz * size))
        start += size
    return jnp.concatenate(pieces, axis=-1)


def join_columns(g, parts, ny, nz):
    rows = g.shape[1]
    pieces, start, npos = [], 0, ny * nz
    for size in parts:
        piece = g[:, :, npos * start : npos * (start + size)].reshape(TP, rows, ny, nz, size)
        pieces.append(piece.transpose(1, 2, 0, 3, 4))
        start += size
    return jnp.concatenate(pieces, axis=-1).reshape(rows, -1).astype(F32)


def fast_device(
    parts,
    tokens,
    segments,
    ln1_gain,
    in_weight,
    conv_kernel,
    out_weight,
    ln2_gain,
    gate_weight,
    up_weight,
    down_weight,
    cotangent,
):
    micro, _, count, width = tokens.shape
    taps = conv_kernel.shape[0]
    nz = lax.axis_size("seq")
    ny = lax.axis_size("dp") // TP
    rows = micro * count
    low_in = in_weight.astype(BF)
    small = jnp.concatenate([ln1_gain[None], ln2_gain[None], conv_kernel], axis=0).astype(BF)
    small = jnp.pad(small.T, ((0, 0), (0, LANES - taps - 2)))
    blocks = [low_in[:, q * width : (q + 1) * width] for q in range(3)]
    blocks += [out_weight.astype(BF), small]
    offset = lax.axis_index("seq") * count
    fill = jnp.full((micro, 2), -1, jnp.int32)
    seg_pad = jnp.concatenate([fill, segments[:, 0], fill, fill, fill, fill], axis=1)
    window = lax.dynamic_slice_in_dim(seg_pad, offset, count + 10, axis=1)
    masks = jnp.stack(
        [window[:, tap : tap + count + 8] == window[:, 2 : count + 10] for tap in range(taps)], axis=-1
    ).astype(F32)
    masks = jnp.pad(masks, ((0, 0), (0, 0), (0, LANES - taps)))
    gus = jnp.stack([cut_columns(w, parts, ny, nz) for w in (gate_weight, up_weight)], axis=1)
    output, gx, gu, gd, *sums = block_call(
        tokens.reshape(rows, width), cotangent.reshape(rows, width), masks, blocks, gus,
        down_weight.astype(BF), parts, nz, 0
    )
    g_gate = join_columns(gu[:, 0], parts, ny, nz)
    g_up = join_columns(gu[:, 1], parts, ny, nz)
    g_in = jnp.concatenate(sums[:3], axis=1)
    g_small = sums[4][:, : taps + 2].T
    shape = tokens.shape
    return (
        output.reshape(shape), gx.reshape(shape), g_small[0], g_in, g_small[2:], sums[3],
        g_small[1], g_gate, g_up, gd,
    )


def row_parts(mesh, token_shape, down_shape):
    nd, nz = mesh.shape["dp"], mesh.shape["seq"]
    if nd != 2 * TP:
        return None
    per = down_shape[0] // (nd * nz)
    shard = token_shape[3] // (nd * nz)
    rows = token_shape[0] * (token_shape[2] // nz)
    if per % 64 % 16 or shard % 16 or token_shape[1] != nd or token_shape[0] != 2:
        return None
    if rows != 4 * nz * shard or token_shape[3] != 2 * rows or 128 * nz != rows:
        return None
    sizes, left = [], per
    while left:
        sizes.append(min(64, left))
        left -= sizes[-1]
    return tuple(sizes)


def solution(mesh):
    in_specs = (
        P(None, "dp", "seq", None),
        P(None, "dp", None),
        P(("dp", "seq")),
        P(("dp", "seq"), None),
        P(None, ("dp", "seq")),
        P(("dp", "seq"), None),
        P(("dp", "seq")),
        P(("dp", "seq"), None),
        P(("dp", "seq"), None),
        P(("dp", "seq"), None),
        P(None, "dp", "seq", None),
    )
    out_specs = (
        P(None, "dp", "seq", None),
        P(None, "dp", "seq", None),
        P(("dp", "seq")),
        P(("dp", "seq"), None),
        P(None, ("dp", "seq")),
        P(("dp", "seq"), None),
        P(("dp", "seq")),
        P(("dp", "seq"), None),
        P(("dp", "seq"), None),
        P(("dp", "seq"), None),
    )

    def run(*arrays):
        parts = row_parts(mesh, arrays[0].shape, arrays[9].shape)
        device = plain_device if parts is None else functools.partial(fast_device, parts)
        return jax.shard_map(
            device, mesh=mesh, in_specs=in_specs, out_specs=out_specs, check_vma=False
        )(*arrays)

    return run
```

```python
import functools
import jax
import jax.numpy as jnp
from jax import lax
from jax.experimental import pallas as pl
from jax.experimental.pallas import tpu as pltpu
from jax.sharding import PartitionSpec as P

BF = jnp.bfloat16
F32 = jnp.float32
eps = 1e-05
MESH = pl.DeviceIdType.MESH
NN = (((1,), (0,)), ((), ()))
NT = (((1,), (1,)), ((), ()))
TN = (((0,), (0,)), ((), ()))
TP = 4
LANES = 128


def mm(left, right, dims):
    return lax.dot_general(left, right, dims, preferred_element_type=F32)


def when(pred, body):
    if pred is True:
        body()
    else:
        pl.when(pred)(body)


class Place:
    def __init__(self, nz):
        dp = lax.axis_index("dp")
        self.y = dp // TP
        self.i = dp % TP
        self.z = lax.axis_index("seq")
        self.nz = nz
        self.x = self.i // 2
        self.c = self.i % 2
        self.others = tuple(self._near(k) for k in range(nz - 1))

    def _near(self, k):
        ranks = [sorted((q for q in range(self.nz) if q != z), key=lambda q: abs(q - z)) for z in range(self.nz)]
        place = jnp.int32(ranks[0][k])
        for z in range(1, self.nz):
            place = jnp.where(self.z == z, ranks[z][k], place)
        return place

    def to_both_sides(self, cp, block, ssem, rsem):
        for to, there in ((self.z - 1, self.z > 0), (self.z + 1, self.z < self.nz - 1)):
            cp.send(block, block, ssem(to), rsem, self.at(z=to), there)

    def relay(self, cp, block, source, ssem, rsem):
        to = jnp.where(source < self.z, self.z + 1, self.z - 1)
        cp.send(block, block, ssem, rsem, self.at(z=to), (to >= 0) & (to < self.nz))

    def member(self, t):
        x = 1 - self.x if t // 2 else self.x
        c = 1 - self.c if t % 2 else self.c
        return x * 2 + c

    def at(self, y=None, i=None, z=None):
        y = self.y if y is None else y
        i = self.i if i is None else i
        z = self.z if z is None else z
        return (y * TP + i, z)


class Copies:
    def __init__(self):
        self.pending = []

    def send(self, src, dst, ssem, rsem, device, pred=True, group=None):
        def make():
            return pltpu.make_async_remote_copy(
                src_ref=src, dst_ref=dst, send_sem=ssem, recv_sem=rsem,
                device_id=device, device_id_type=MESH)
        when(pred, lambda: make().start())
        if group is None:
            self.pending.append((pred, make))

    def local(self, src, dst, sem):
        pltpu.make_async_copy(src, dst, sem).start()

    def arrived(self, ref, ssem, rsem, device, pred=True):
        when(pred, lambda: pltpu.make_async_remote_copy(
            src_ref=ref, dst_ref=ref, send_sem=ssem, recv_sem=rsem,
            device_id=device, device_id_type=MESH).wait_recv())

    def drain(self, count=None):
        done = self.pending[:count]
        self.pending = self.pending[len(done):]
        for pred, make in done:
            when(pred, lambda make=make: make().wait_send())


def entry_barrier(p):
    bar = pltpu.get_barrier_semaphore()
    there = [p.at(i=p.member(t)) for t in range(1, TP)] + [p.at(y=1 - p.y)] + [p.at(z=q) for q in p.others]
    for device in there:
        pl.semaphore_signal(bar, inc=1, device_id=device, device_id_type=MESH)
    pl.semaphore_wait(bar, len(there))


def gather_pieces(width):
    half = width // 2
    return (
        (4, 0, LANES, "zyx"),
        (0, 0, half, "zyx"), (0, half, half, "zxy"),
        (2, 0, half, "xzy"), (2, half, half, "yzx"),
        (1, 0, half, "zyx"), (1, half, half, "zxy"),
        (3, 0, half, "xzy"), (3, half, half, "yzx"),
    )


def sum_pieces(width):
    half = width // 2
    return (
        (3, 0, half, "zyx"), (3, half, half, "zxy"),
        (1, 0, half, "zyx"), (1, half, half, "zxy"),
        (0, 0, half, "zyx"), (0, half, half, "zxy"),
        (2, 0, half, "zyx"), (2, half, half, "zxy"),
        (4, 0, LANES, "zyx"),
    )


def gather_sems(nz, count):
    D = pltpu.SemaphoreType.DMA
    return [D((count, 2, 2 * nz)), D((count, 2, nz)), D((count, nz)), D((count, nz)), D((count, 2, nz)),
            D((count, 2, nz)), D((count,)), D((count,))]


def gather_flow(p, cp, n, piece, W, sems):
    s_z, r_z, s_1, r_1, s_2, r_2, s_c, r_c = sems
    _, c0, cn, order = piece
    cs = slice(c0, c0 + cn)
    z, nz = p.z, p.nz
    a_is_x = order.index("x") < order.index("y")
    zfirst = order[0] == "z"

    def blk(a, b, zz):
        y, x = (b, a) if a_is_x else (a, b)
        return W.at[y, x, p.c, zz, :, cs]
    a, b = (p.x, p.y) if a_is_x else (p.y, p.x)
    dev_x, dev_y = p.at(i=p.member(2)), p.at(y=1 - p.y)
    dev_a, dev_b = (dev_x, dev_y) if a_is_x else (dev_y, dev_x)

    def core(aa, bb, zz):
        r = blk(aa, bb, zz)
        cp.send(r, r, s_c.at[n], r_c.at[n], p.at(i=p.member(1)), group=True)

    def zsend(aa):
        p.to_both_sides(cp, blk(aa, b, z), lambda to: s_z.at[n, aa, to], r_z.at[n, aa, z])

    def asend(zz):
        r = blk(a, b, zz)
        cp.send(r, r, s_1.at[n, zz], r_1.at[n, zz], dev_a)

    def bsend(aa, zz):
        r = blk(aa, b, zz)
        cp.send(r, r, s_2.at[n, aa, zz], r_2.at[n, aa, zz], dev_b)

    asend(z)
    zsend(a)
    bsend(a, z)
    core(a, b, z)
    yield "first"
    if not zfirst:
        cp.arrived(blk(1 - a, b, z), s_1.at[n, z], r_1.at[n, z], p.at())
        zsend(1 - a)
        bsend(1 - a, z)
        core(1 - a, b, z)
    for zz in p.others:
        yield "z"
        for aa in ((a,) if zfirst else (a, 1 - a)):
            cp.arrived(blk(aa, b, zz), s_z.at[n, aa, zz], r_z.at[n, aa, zz], p.at())
            p.relay(cp, blk(aa, b, zz), zz, s_z.at[n, aa, nz + zz], r_z.at[n, aa, zz])
            if zfirst:
                asend(zz)
            bsend(aa, zz)
            core(aa, b, zz)
    if zfirst:
        yield "second"
        for zz in (z,) + p.others:
            cp.arrived(blk(1 - a, b, zz), s_1.at[n, zz], r_1.at[n, zz], p.at())
            bsend(1 - a, zz)
            core(1 - a, b, zz)
    for zz in (z,) + p.others:
        yield "last axis"
        for aa in (a, 1 - a):
            cp.arrived(blk(aa, 1 - b, zz), s_2.at[n, aa, zz], r_2.at[n, aa, zz], p.at())
            core(aa, 1 - b, zz)
    yield "core"
    cp.arrived(W.at[:, :, 1 - p.c, :, :, cs], s_c.at[n], r_c.at[n], p.at())
    cp.pending.append((True, lambda: pltpu.make_async_remote_copy(
        src_ref=W.at[:, :, p.c, :, :, cs], dst_ref=W.at[:, :, p.c, :, :, cs], send_sem=s_c.at[n],
        recv_sem=r_c.at[n], device_id=p.at(i=p.member(1)), device_id_type=MESH)))


def sum_sems(nz, count):
    D = pltpu.SemaphoreType.DMA
    return [D((count,)), D((count,)), D((count, nz)), D((count, nz)), D((count, nz)), D((count, nz)),
            D((count, nz)), D((count, nz))]


def sum_scratch(nz, shard, pieces):
    return dict(
        one=[pltpu.VMEM((2, nz, shard, q[2]), BF) for q in pieces],
        two=[pltpu.VMEM((nz if q[3][0] == "z" else 1, shard, q[2]), BF) for q in pieces],
        path=[pltpu.VMEM((nz, 1 if q[3][0] == "z" else 2, shard, q[2]), BF) for q in pieces],
    )


def sum_flow(p, cp, n, piece, G, LC, L1, L2, LZ, out, sems):
    s_c, r_c, s_1, r_1, s_2, r_2, s_z, r_z = sems
    _, c0, cn, order = piece
    cs = slice(c0, c0 + cn)
    z = p.z
    targets = p.others[::-1] + (z,)
    zlast = order[0] == "z"
    b_is_y = order.index("x") < order.index("y")
    b, a = (p.y, p.x) if b_is_y else (p.x, p.y)
    dev_x, dev_y = p.at(i=p.member(2)), p.at(y=1 - p.y)
    dev_b, dev_a = (dev_y, dev_x) if b_is_y else (dev_x, dev_y)

    def g(bb, aa, zz):
        y, x = (bb, aa) if b_is_y else (aa, bb)
        return (y, x, p.c, zz, slice(None), cs)

    def f(v):
        return v.astype(F32)

    def lc(bb, aa, zz):
        y, x = (bb, aa) if b_is_y else (aa, bb)
        return (y, x, zz)

    def row(bb, zz, aa=None):
        aa = slice(None) if aa is None else pl.ds(aa, 1)
        y, x = (bb, aa) if b_is_y else (aa, bb)
        return G.at[y, x, p.c, zz, :, cs]
    cp.send(G.at[:, :, 1 - p.c, :, :, cs], LC, s_c.at[n], r_c.at[n], p.at(i=p.member(1)))
    LZ[z] = jnp.zeros(LZ.shape[1:], BF)
    yield
    cp.arrived(LC, s_c.at[n], r_c.at[n], p.at())
    for zz in targets:
        for aa in range(2):
            i = g(1 - b, aa, zz)
            G[i] = (f(G[i]) + f(LC[lc(1 - b, aa, zz)])).astype(BF)
        cp.send(row(1 - b, zz), L1.at[:, zz], s_1.at[n, zz], r_1.at[n, zz], dev_b)
    for zz in targets:
        for aa in range(2):
            i = g(b, aa, zz)
            G[i] = (f(G[i]) + f(LC[lc(b, aa, zz)])).astype(BF)
    if zlast:
        yield
        for zz in targets:
            cp.arrived(L1.at[:, zz], s_1.at[n, zz], r_1.at[n, zz], p.at())
            i = g(b, 1 - a, zz)
            G[i] = (f(G[i]) + f(L1[1 - a, zz])).astype(BF)
            cp.send(G.at[i], L2.at[zz], s_2.at[n, zz], r_2.at[n, zz], dev_a)

    def own(zz, k):
        if zlast:
            return f(G[g(b, a, zz)]) + f(L1[a, zz]) + f(L2[zz])
        return f(G[g(b, k, zz)]) + f(L1[k, zz])
    yield
    for zz in targets:
        if zlast:
            cp.arrived(L2.at[zz], s_2.at[n, zz], r_2.at[n, zz], p.at())
        else:
            cp.arrived(L1.at[:, zz], s_1.at[n, zz], r_1.at[n, zz], p.at())
        if zz is z:
            continue
        for k in range(1 if zlast else 2):
            G[g(b, a if zlast else k, zz)] = own(zz, k).astype(BF)
        cp.send(row(b, zz, a if zlast else None), LZ.at[z], s_z.at[n, zz], r_z.at[n, z], p.at(z=zz))
    yield
    for zz in p.others:
        cp.arrived(LZ.at[zz], s_z.at[n, zz], r_z.at[n, zz], p.at())

    def total(k):
        v = own(z, k)
        for zz in range(p.nz):
            v = v + f(LZ[zz, k])
        return v
    if zlast:
        out[:, cs] = total(0)
        return
    G[g(b, 1 - a, z)] = total(1 - a).astype(BF)
    cp.send(G.at[g(b, 1 - a, z)], L2.at[0], s_2.at[n, 0], r_2.at[n, 0], dev_a)
    out[:, cs] = total(a)
    yield
    cp.arrived(L2.at[0], s_2.at[n, 0], r_2.at[n, 0], p.at())
    out[:, cs] += f(L2[0])


def slot(ref, t):
    return ref.at[t // 2, t % 2]


def block_body(parts, nz, x_in, df_in, masks, b0, b1, b2, b3, b4, gus, ds,
               out_o, gx_o, ogu_o, od_o, m012, m3, m4, W0, W1, W2, W3, W4, SV32, SV16, s):
    p = Place(nz)
    z = p.z
    rows, width = x_in.shape
    shard = gus.shape[2]
    npos = 2 * nz
    count = rows // 2
    half = width // 2
    low = rows // (2 * nz)
    offs = [sum(parts[:k]) for k in range(len(parts))]
    CH = [(offs[k] * npos, parts[k] * npos) for k in range(len(parts))]
    K = len(parts)
    cp, cx, ct = Copies(), Copies(), Copies()
    cg = [Copies() for _ in range(K)]
    first, last = z == 0, z == nz - 1
    inner_l, inner_r = z > 0, z < nz - 1
    H, dF, WGU, WD, dHa, Zb, dAb, dGb = (s[k] for k in ("H", "dF", "WGU", "WD", "dHa", "Zb", "dAb", "dGb"))
    GGU = WGU
    GD, RY, ZGU, ZD, YD, LX, SX = (s[k] for k in ("GD", "RY", "ZGU", "ZD", "YD", "LX", "SX"))
    sem_h, s_p0, r_p0, s_z, r_z, s_y, r_y, s_dz, r_dz, s_dy, r_dy = (
        s[k] for k in ("sem_h", "s_p0", "r_p0", "s_z", "r_z", "s_y", "r_y", "s_dz", "r_dz", "s_dy", "r_dy"))
    s_gy, r_gy, s_gz, r_gz, s_gt, r_gt, s_ez, r_ez, s_ey, r_ey, s_x, r_x = (
        s[k] for k in ("s_gy", "r_gy", "s_gz", "r_gz", "s_gt", "r_gt", "s_ez", "r_ez", "s_ey", "r_ey", "s_x", "r_x"))
    sem = s["sem"]
    GN, SG, SM, PV, NX = (s[k] for k in ("GN", "SG", "SM", "PV", "NX"))
    GS = SM
    W = (W0, W1, W2, W3, W4)
    sums = tuple(m012.at[:, q * width:(q + 1) * width] for q in range(3)) + (m3, m4)

    def cols(k):
        return slice(CH[k][0], CH[k][0] + CH[k][1])

    def rws(k):
        return slice(offs[k], offs[k] + parts[k])

    class Load:
        def __init__(self, n, *pairs):
            self.copies = [pltpu.make_async_copy(a, b, sem.at[n + k]) for k, (a, b) in enumerate(pairs)]

        def start(self):
            for c in self.copies:
                c.start()
            return self

        def wait(self):
            for c in self.copies:
                c.wait()

    own_w = Load(0, *[(b, w.at[p.y, p.x, p.c, z]) for b, w in zip((b0, b1, b2, b3, b4), W)]).start()
    own_x = Load(5, (x_in, SX.at[0])).start()
    df_blocks = df_in
    own_df = Load(6, (df_blocks, slot(dF, 0))).start()
    own_gu = Load(7, (gus.at[p.i], WGU.at[p.y, p.i, z])).start()
    own_d = Load(8, *[(ds.at[rws(k)], WD[k].at[p.y, z]) for k in range(K)]).start()
    entry_barrier(p)

    ZGU[z] = jnp.zeros(ZGU.shape[1:], BF)
    for k in range(K):
        ZD[k][z] = jnp.zeros(ZD[k].shape[1:], BF)

    @pl.when(first)
    def _():
        PV[...] = jnp.zeros(PV.shape, BF)

    @pl.when(last)
    def _():
        NX[...] = jnp.zeros(NX.shape, BF)

    def p0(k):
        for t in (2, 3, 1):
            m = p.member(t)
            cg[k].send(gus.at[m, :, :, cols(k)], WGU.at[p.y, p.i, z, :, :, cols(k)],
                       s_p0.at[k, t - 1], r_p0.at[k, t - 1], p.at(i=m))

    def acts(dst, q):
        for t in (2, 1):
            cp.send(slot(dst, 0), slot(dst, t), sem_h.at[q, 0, t - 1], sem_h.at[q, 1, t - 1], p.at(i=p.member(t)))

    def acts_wait(dst, q, t):
        cp.arrived(slot(dst, t), sem_h.at[q, 0, t - 1], sem_h.at[q, 1, t - 1], p.at(i=p.member(t)))

    def acts_forward(dst, q):
        acts_wait(dst, q, 2)
        cp.send(slot(dst, 2), slot(dst, 3), sem_h.at[q, 0, 2], sem_h.at[q, 1, 2], p.at(i=p.member(1)))

    def gu_blk(k, y, zz):
        return WGU.at[y, :, zz, :, :, cols(k)]

    def ysend(k, zz):
        b = gu_blk(k, p.y, zz)
        cg[k].send(b, b, s_y.at[k, zz], r_y.at[k, zz], p.at(y=1 - p.y))

    def flow_ag(k):
        W = WD[k]
        for t in (1, 2, 3):
            m = p.member(t)
            cp.arrived(WGU.at[p.y, m, z, :, :, cols(k)], s_p0.at[k, t - 1], r_p0.at[k, t - 1], p.at(i=m))
        p.to_both_sides(cg[k], gu_blk(k, p.y, z), lambda to: s_z.at[k, to], r_z.at[k, z])
        b = W.at[p.y, z]
        cg[k].send(b, b, s_dy.at[k], r_dy.at[k], p.at(y=1 - p.y))
        p.to_both_sides(cg[k], b, lambda to: s_dz.at[k, p.y, to], r_dz.at[k, p.y, z])
        yield
        ysend(k, z)
        b = W.at[1 - p.y, z]
        cp.arrived(b, s_dy.at[k], r_dy.at[k], p.at())
        p.to_both_sides(cg[k], b, lambda to: s_dz.at[k, 1 - p.y, to], r_dz.at[k, 1 - p.y, z])
        for zz in p.others:
            yield
            b = gu_blk(k, p.y, zz)
            cp.arrived(b, s_z.at[k, zz], r_z.at[k, zz], p.at())
            p.relay(cg[k], b, zz, s_z.at[k, nz + zz], r_z.at[k, zz])
            ysend(k, zz)
            for y in (p.y, 1 - p.y):
                b = W.at[y, zz]
                cp.arrived(b, s_dz.at[k, y, zz], r_dz.at[k, y, zz], p.at())
                p.relay(cg[k], b, zz, s_dz.at[k, y, nz + zz], r_dz.at[k, y, zz])
        yield
        for zz in (z,) + p.others:
            cp.arrived(gu_blk(k, 1 - p.y, zz), s_y.at[k, zz], r_y.at[k, zz], p.at())

    targets = p.others[::-1] + (z,)

    def flow_rs_gu(k, w):
        c = cols(k)
        for zz in targets:
            cp.send(GGU.at[1 - p.y, :, zz, w, :, c], RY.at[:, zz, w, :, c],
                    s_gy.at[k, w, zz], r_gy.at[k, w, zz], p.at(y=1 - p.y))
        for zz in p.others[::-1]:
            yield
            cp.arrived(RY.at[:, zz, w, :, c], s_gy.at[k, w, zz], r_gy.at[k, w, zz], p.at())
            for j in range(TP):
                GGU[p.y, j, zz, w, :, c] = (
                    GGU[p.y, j, zz, w, :, c].astype(F32) + RY[j, zz, w, :, c].astype(F32)).astype(BF)
            cp.send(GGU.at[p.y, :, zz, w, :, c], ZGU.at[z, :, w, :, c], s_gz.at[k, w, zz], r_gz.at[k, w, z],
                    p.at(z=zz))
        yield
        cp.arrived(RY.at[:, z, w, :, c], s_gy.at[k, w, z], r_gy.at[k, w, z], p.at())
        for zz in p.others:
            cp.arrived(ZGU.at[zz, :, w, :, c], s_gz.at[k, w, zz], r_gz.at[k, w, zz], p.at())
        for j in range(TP):
            v = GGU[p.y, j, z, w, :, c].astype(F32) + RY[j, z, w, :, c].astype(F32)
            for zz in range(nz):
                v = v + ZGU[zz, j, w, :, c].astype(F32)
            GGU[p.y, j, z, w, :, c] = v.astype(BF)
        for t in (2, 3, 1):
            m = p.member(t)
            cp.send(GGU.at[p.y, m, z, w, :, c], ogu_o.at[p.i, w, :, c], s_gt.at[k, w, t - 1], r_gt.at[k, w, t - 1],
                    p.at(i=m))
        own_out.append(Load(11 + 2 * k + w, (GGU.at[p.y, p.i, z, w, :, c], ogu_o.at[p.i, w, :, c])).start())
        yield
        for t in (1, 2, 3):
            m = p.member(t)
            cp.arrived(ogu_o.at[m, w, :, c], s_gt.at[k, w, t - 1], r_gt.at[k, w, t - 1], p.at(i=m))

    def flow_rs_d(k):
        G, L, Y = GD[k], ZD[k], YD[k]
        for zz in targets:
            cp.send(G.at[1 - p.y, zz], Y.at[zz], s_ey.at[k, zz], r_ey.at[k, zz], p.at(y=1 - p.y))
        for zz in p.others[::-1]:
            yield
            cp.arrived(Y.at[zz], s_ey.at[k, zz], r_ey.at[k, zz], p.at())
            G[p.y, zz] = (G[p.y, zz].astype(F32) + Y[zz].astype(F32)).astype(BF)
            cp.send(G.at[p.y, zz], L.at[z], s_ez.at[k, zz], r_ez.at[k, z], p.at(z=zz))
        yield
        cp.arrived(Y.at[z], s_ey.at[k, z], r_ey.at[k, z], p.at())
        for zz in p.others:
            cp.arrived(L.at[zz], s_ez.at[k, zz], r_ez.at[k, zz], p.at())
        v = G[p.y, z].astype(F32) + Y[z].astype(F32)
        for zz in range(nz):
            v = v + L[zz].astype(F32)
        od_o[rws(k), :] = v

    live, own_out = [], []

    def pump(n=1, which=None):
        for _ in range(n):
            for f in list(live if which is None else which):
                if f in live and next(f, "end") == "end":
                    live.remove(f)

    def run(*gens):
        for g in gens:
            for _ in g:
                pass
            if g in live:
                live.remove(g)

    own_w.wait()
    gp = gather_pieces(width)
    gather = [gather_flow(p, cp, n, q, W[q[0]], s["gather"]) for n, q in enumerate(gp)]
    states = {}

    def gather_to(*stops):
        left = list(gather)
        while left:
            for f in list(left):
                if states.get(f) in stops:
                    left.remove(f)
                else:
                    states[f] = next(f)
    gather_to("first")
    own_gu.wait()
    own_d.wait()
    own_df.wait()
    gather_to("z")
    for k in range(K):
        p0(k)
    gather_to("last axis")
    acts(dF, 1)
    ag = [flow_ag(k) for k in range(K)]
    for g in ag:
        next(g)
    for g in ag:
        next(g)
    gather_to("core")

    def need(*panels):
        for f, q in zip(gather, gp):
            if q[0] in panels:
                next(f, None)

    def panel(q, buf, n):
        return Load(n, *[(W[q].at[:, :, :, :, :, h * half:(h + 1) * half], buf.at[:, h, :, :, :, :, pl.ds(0, half)]) for h in range(2)])

    def half_panel(buf, h):
        return buf[:, h, :, :, :, :, :half].reshape(width, half)

    need(4)
    Load(20, (W4, SM)).start().wait()
    GN[...] = SM[...].reshape(width, LANES).astype(F32).T[:8]
    need(0)
    wb = panel(0, dAb, 21).start()
    own_x.wait()

    def norm(v):
        inv = lax.rsqrt(jnp.mean(v * v, axis=-1, keepdims=True) + eps)
        return inv, v * inv

    def tiles(size):
        return [slice(t * size, (t + 1) * size) for t in range(rows // size)]

    def norm_one(m, _):
        rs = pl.ds(pl.multiple_of(m * 128, 128), 128)
        _, n1 = norm(SX[0, rs].astype(F32))
        SX[1, rs] = (n1 * GN[0:1]).astype(BF)
        return 0
    lax.fori_loop(0, rows // 128, norm_one, 0)
    save_h1 = Load(30, (SX.at[1], SV16.at[0])).start()

    def project(buf, dst):
        for h in range(2):
            dHa[dst, :, h * half:(h + 1) * half] = mm(SX[1], half_panel(buf, h), NN)
    need(2)
    wu = panel(2, dGb, 23).start()
    wb.wait()
    project(dAb, 0)
    need(1)
    wc = panel(1, dAb, 21).start()
    wu.wait()
    project(dGb, 2)
    save_bu = Load(31, (dHa.at[0], SV32.at[0]), (dHa.at[2], SV32.at[2])).start()

    def make_bx(m, _):
        rs = pl.ds(pl.multiple_of(m * 128, 128), 128)
        SX[2, rs] = (dHa[0, rs] * dHa[2, rs]).astype(BF)
        return 0
    lax.fori_loop(0, rows // 128, make_bx, 0)
    s_h, r_h = s["s_h"], s["r_h"]
    for m in range(2):
        cp.send(SX.at[2, pl.ds((m + 1) * count - 16, 16)], PV.at[m], s_h.at[0, m], r_h.at[0, m],
                p.at(z=z + 1), inner_r)
    save_bx = Load(33, (SX.at[2], SV16.at[1])).start()
    live.extend(ag)
    pump(1, ag[:1])
    need(3)
    wo = panel(3, dGb, 23).start()
    wc.wait()
    project(dAb, 1)
    save_c = Load(34, (dHa.at[1], SV32.at[1])).start()
    for m in range(2):
        cp.arrived(PV.at[m], s_h.at[0, m], r_h.at[0, m], p.at(), inner_l)

    def earlier(v, prev, back):
        r = lax.broadcasted_iota(jnp.int32, v.shape, 0)
        n = prev.shape[0]
        moved = pltpu.roll(v, back, 0)
        moved = jnp.where(r == back - 1, prev[n - 1:n], moved)
        return jnp.where(r == 0, prev[n - back:n - back + 1], moved)

    def later(v, after, ahead):
        r = lax.broadcasted_iota(jnp.int32, v.shape, 0)
        n = v.shape[0]
        moved = pltpu.roll(v, n - ahead, 0)
        moved = jnp.where(r == n - ahead, after[0:1], moved)
        return jnp.where(r == n - 1, after[ahead - 1:ahead], moved)

    lanes = 256
    nl = width // lanes

    def conv(q, _):
        m, c = q // nl, q % nl
        ls = pl.ds(pl.multiple_of(c * lanes, lanes), lanes)
        rs = pl.ds(pl.multiple_of(m * count, count), count)
        v = SX[2, rs, ls].astype(F32)
        prev = PV[m, :, ls].astype(F32)
        mk = masks[m]
        total = GN[2:3, ls] * earlier(v, prev, 2) * mk[:count, 0:1]
        total = total + GN[3:4, ls] * earlier(v, prev, 1) * mk[:count, 1:2]
        total = total + GN[4:5, ls] * v * mk[:count, 2:3]
        dHa[3, rs, ls] = total
        LX[0, rs, ls] = (dHa[1, rs, ls] * total).astype(BF)
        return 0
    lax.fori_loop(0, 2 * nl, conv, 0)
    save_cv = Load(35, (dHa.at[3], SV32.at[3]), (LX.at[0], SV16.at[2])).start()
    save_bu.wait()
    pump(1, ag)
    wo.wait()
    for h in range(2):
        hs = slice(h * half, (h + 1) * half)
        dHa[0, :, hs] = SX[0, :, hs].astype(F32) + mm(LX[0], half_panel(dGb, h), NN)

    def norm_two(m, _):
        rs = pl.ds(pl.multiple_of(m * nz * shard, nz * shard), nz * shard)
        _, n2 = norm(dHa[0, rs])
        H[0, 0, m // 2, m % 2] = (n2 * GN[1:2]).astype(BF).reshape(nz, shard, width)
        return 0
    lax.fori_loop(0, 4, norm_two, 0)
    save_r = Load(37, (dHa.at[0], SV32.at[4])).start()
    save_cv.wait()
    acts(H, 0)
    save_h1.wait()
    save_bx.wait()
    save_c.wait()
    save_r.wait()
    pump(1, ag)

    def half_blocks(v):
        return v.reshape(2, nz, shard, v.shape[-1])

    def fwd_mid(k, t):
        c0, cn = CH[k]
        c = cols(k)
        wg = WGU[:, :, :, 0, :, c].reshape(width, cn)
        wu = WGU[:, :, :, 1, :, c].reshape(width, cn)
        wd = WD[k][...].reshape(cn, width)

        def some(r, _):
            rs = pl.ds(pl.multiple_of(r * count, count), count)
            h = H[t // 2, t % 2, r].reshape(count, width)
            a = mm(h, wg, NN)
            g = mm(h, wu, NN)
            dz = mm(dF[t // 2, t % 2, r].reshape(count, width), wd, NT)
            sg = 1.0 / (1.0 + jnp.exp(-a))
            act = a * sg
            Zb[t, r, :, :, :, c] = half_blocks((act * g).astype(BF))
            da = (dz * g * sg * (1.0 + a * (1.0 - sg))).astype(BF)
            dg = (dz * act).astype(BF)
            dAb[t // 2, t % 2, r, :, :, :, :cn] = half_blocks(da)
            dGb[t // 2, t % 2, r, :, :, :, :cn] = half_blocks(dg)
            d = mm(da, wg, NT) + mm(dg, wu, NT)
            if k == 0:
                dHa[t, rs] = d
            else:
                dHa[t, rs] += d
            return 0
        lax.fori_loop(0, 2, some, 0)

    def ffn_out(t, put):
        def some(r, _):
            f = None
            for k in range(K):
                v = mm(Zb[t, r, :, :, :, cols(k)].reshape(count, CH[k][1]), WD[k][...].reshape(CH[k][1], width), NN)
                f = v if f is None else f + v
            put(pl.ds(pl.multiple_of(r * count, count), count), f)
            return 0
        lax.fori_loop(0, 2, some, 0)

    tok = TP * rows

    def grads(k):
        c0, cn = CH[k]
        c = cols(k)
        for w, src in ((0, dAb), (1, dGb)):
            def body(m, _, w=w, src=src):
                y, j = m // 2, (m % 2) * 2
                f = 2 * nz * shard
                ms = pl.ds(pl.multiple_of(m * f, f), f)
                v = mm(H[:, :, :, :, :, :, ms].reshape(tok, f), src[:, :, :, :, :, :, :cn].reshape(tok, cn), TN)
                GGU[y, pl.ds(j, 2), :, w, :, c] = v.astype(BF).reshape(2, nz, shard, cn)
                return 0
            lax.fori_loop(0, TP, body, 0)
            begin((k, w), flow_rs_gu(k, w))
            if k == K - 1:
                advance(*(((0, 0), (0, 1)) if w == 0 else ((0, 0), (0, 1), (0, 2))))
        r = parts[k]
        for b in range(cn // 128):
            zb = Zb[:, :, :, :, :, c0 + b * 128:c0 + (b + 1) * 128].reshape(tok, 128)
            v = mm(zb, dF[...].reshape(tok, width), TN).astype(BF)
            lo = b * 128
            while lo < (b + 1) * 128:
                pos, q = lo // r, lo % r
                n = min(r - q, (b + 1) * 128 - lo)
                GD[k][pos // nz, pos % nz, q:q + n] = v[lo - b * 128:lo - b * 128 + n]
                lo += n
        begin((k, 2), flow_rs_d(k))

    rs_flows = {}

    def begin(key, flow):
        next(flow)
        rs_flows[key] = flow
        live.append(flow)

    def advance(*keys):
        for key in keys:
            if rs_flows[key] in live:
                pump(1, [rs_flows[key]])

    def x_land(q, e):
        return LX.at[2 + q] if e == 2 else LX.at[e]

    def x_send1(q, e, value=None):
        if value is not None:
            SX[e] = value.astype(BF)
        cx.send(SX.at[e], x_land(q, e), s_x.at[q, e], r_x.at[q, e], p.at(i=p.member(1)))

    def x_wait(q, e):
        cx.arrived(x_land(q, e), s_x.at[q, e], r_x.at[q, e], p.at(i=p.member(2 if e == 2 else 1)))

    def x_send2(q, acc):
        x_wait(q, 1)
        SX[2] = (acc[...] + LX[1].astype(F32)).astype(BF)
        cx.send(SX.at[2], x_land(q, 2), s_x.at[q, 2], r_x.at[q, 2], p.at(i=p.member(2)))

    def x_add(q, acc, e):
        x_wait(q, e)
        acc[...] += x_land(q, e)[...].astype(F32)

    acts_forward(dF, 1)
    before = 0
    for k in range(K):
        run(ag[k])
        if k == K - 1:
            cp.drain(before)
        if k == 0:
            acts_wait(H, 0, 1)
            acts_wait(dF, 1, 1)
            fwd_mid(0, 0)
            fwd_mid(0, 1)
            acts_forward(H, 0)
            acts_wait(dF, 1, 3)
            fwd_mid(0, 2)
            acts_wait(H, 0, 3)
            fwd_mid(0, 3)
            pump(1, ag[1:2])
        else:
            for t in (3, 2, 1, 0):
                fwd_mid(k, t)
                if k == K - 1 and t == 3:
                    x_send1(0, 1, dHa[3])
                if k == K - 1 and t == 2:
                    x_send2(0, dHa.at[2])
                if k == K - 1 and t == 1:
                    x_send1(0, 0, dHa[1])
                if k == 1:
                    advance(*{3: (), 2: ((0, 0),), 1: ((0, 0),), 0: ((0, 0), (0, 1))}[t])
        cg[k].drain()
        before = len(cp.pending)
        grads(k)
    wo = panel(3, dAb, 21).start()
    x_add(0, dHa.at[0], 0)
    pl.semaphore_signal(s["ready"], inc=1, device_id=p.at(i=p.member(1)), device_id_type=MESH)
    pr = Load(40, (SV32.at[4], dHa.at[2])).start()
    advance((0, 1), (0, 2), (0, 2))

    def keep(n):
        def put(rs, v):
            dHa[n, rs] = v
        return put

    def stage(e):
        def put(rs, v):
            SX[e, rs] = v.astype(BF)
        return put
    ffn_out(2, keep(1))
    ffn_out(0, keep(3))
    advance((0, 1), (0, 2), (1, 0))
    cx.drain(1)
    cx.pending.append(cx.pending.pop(0))
    cx.drain(1)
    ffn_out(1, stage(0))
    ffn_out(3, stage(1))
    pl.semaphore_wait(s["ready"], 1)
    x_send1(1, 0)
    x_send1(1, 1)
    advance((1, 0))
    x_add(0, dHa.at[0], 2)
    cx.drain(1)
    x_send2(1, dHa.at[1])
    x_add(1, dHa.at[3], 0)

    pc = Load(41, (SV32.at[1], dHa.at[1])).start()
    cx.drain(2)
    py = Load(42, (SV16.at[2], SX.at[0]), (SV16.at[0], SX.at[1])).start()
    pr.wait()
    SG[...] = jnp.zeros(SG.shape, F32)

    def back_two(m, _):
        n = nz * shard
        rs = pl.ds(pl.multiple_of(m * n, n), n)
        r = dHa[2, rs]
        dHa[3, rs] += r
        inv, n2 = norm(r)
        d = dHa[0, rs]
        SG[1:2] += jnp.sum(d * n2, axis=0, keepdims=True)
        dn = d * GN[1:2]
        df = dF[0, 0, m // 2, m % 2].reshape(n, width).astype(F32)
        dr = df + inv * (dn - n2 * jnp.mean(dn * n2, axis=-1, keepdims=True))
        dHa[0, rs] = dr
        WD[0][m // 2, pl.ds((m % 2) * (nz // 2), nz // 2), :low] = dr.astype(BF).reshape(nz // 2, low, width)
        return 0
    lax.fori_loop(0, 4, back_two, 0)
    pcv = Load(44, (SV32.at[3], dHa.at[2])).start()
    advance((1, 0), (1, 1))
    wo.wait()
    pc.wait()
    pcv.wait()
    wbk = panel(0, dGb, 23).start()

    def back_y(m, _):
        rs = pl.ds(pl.multiple_of(m * count, count), count)
        do = WD[0][m, :, :low].reshape(count, width)
        dy = mm(do[:, :half], half_panel(dAb, 0), NT) + mm(do[:, half:], half_panel(dAb, 1), NT)
        LX[1, rs] = (dy * dHa[2, rs]).astype(BF)
        WD[1][m, :, :low] = (dy * dHa[1, rs]).astype(BF).reshape(nz, low, width)
        return 0
    lax.fori_loop(0, 2, back_y, 0)
    advance((1, 0), (1, 1))
    wck = panel(1, dAb, 21).start()
    for m in range(2):
        cp.send(WD[1].at[m, 0, pl.ds(0, 16)], NX.at[m], s_h.at[1, m], r_h.at[1, m], p.at(z=z - 1), inner_l)
    pu = Load(41, (SV32.at[2], dHa.at[1])).start()
    pb = Load(44, (SV32.at[0], dHa.at[2])).start()

    panels = (H.at[0], H.at[1], dF.at[0], dF.at[1], GS)
    sp = sum_pieces(width)

    mix = {}

    def start_sums(q):
        for n, piece in enumerate(sp):
            if piece[0] != q:
                continue
            _, c0, cn, _ = piece
            lc = Zb.at[q, :, :, :, :, pl.ds(c0, cn)] if q < 4 else Zb.at[3, :, :, :, :, pl.ds(width, LANES)]
            g = sum_flow(p, ct, n, piece, panels[q], lc, s["land"]["one"][n], s["land"]["two"][n],
                         s["land"]["path"][n], sums[q], s["sum"])
            next(g)
            live.append(g)
            mix.setdefault(q, []).append(g)

    def weight_grad(q, left, right):
        def body(m, _):
            f = 2 * nz * shard
            ms = pl.ds(pl.multiple_of(m * f, f), f)
            v = mm(left(ms), right(), TN)
            panels[q][m // 2, m % 2] = v.astype(BF).reshape(2, nz, shard, width)
            return 0
        lax.fori_loop(0, width // (2 * nz * shard), body, 0)
        start_sums(q)

    py.wait()
    weight_grad(3, lambda ms: SX[0, :, ms], lambda: WD[0][:, :, :low].reshape(rows, width))
    advance((1, 0), (1, 1))
    weight_grad(1, lambda ms: SX[1, :, ms], lambda: LX[1])
    pbx = Load(42, (SV16.at[1], SX.at[0])).start()
    advance((1, 1), (1, 2))
    pump(1, mix[3])
    for m in range(2):
        cp.arrived(NX.at[m], s_h.at[1, m], r_h.at[1, m], p.at(), inner_r)
    pu.wait()
    pb.wait()
    pbx.wait()

    def back_conv(q, _):
        m, c = q // nl, q % nl
        ls = pl.ds(pl.multiple_of(c * lanes, lanes), lanes)
        rs = pl.ds(pl.multiple_of(m * count, count), count)
        v = SX[0, rs, ls].astype(F32)
        prev = PV[m, :, ls].astype(F32)
        dcv = WD[1][m, :, :low, ls].reshape(count, lanes).astype(F32)
        after = NX[m, :, ls].astype(F32)
        mk = masks[m]
        w0, w1, w2 = (dcv * mk[:count, t:t + 1] for t in range(3))
        SG[2:3, ls] += jnp.sum(w0 * earlier(v, prev, 2), axis=0, keepdims=True)
        SG[3:4, ls] += jnp.sum(w1 * earlier(v, prev, 1), axis=0, keepdims=True)
        SG[4:5, ls] += jnp.sum(w2 * v, axis=0, keepdims=True)
        tail = mk[count:count + 8]
        d = GN[2:3, ls] * later(w0, after[:8] * tail[:, 0:1], 2)
        d = d + GN[3:4, ls] * later(w1, after[:8] * tail[:, 1:2], 1)
        d = d + GN[4:5, ls] * w2
        LX[0, rs, ls] = (d * dHa[1, rs, ls]).astype(BF)
        LX[2, rs, ls] = (d * dHa[2, rs, ls]).astype(BF)
        return 0
    lax.fori_loop(0, 2 * nl, back_conv, 0)
    advance((1, 1), (1, 2), (1, 2))
    pump(1, mix[1])
    weight_grad(0, lambda ms: SX[1, :, ms], lambda: LX[0])
    advance((1, 2))
    weight_grad(2, lambda ms: SX[1, :, ms], lambda: LX[2])
    pump(1, mix[0])
    pump(1, mix[3])
    px = Load(42, (x_in, SX.at[1])).start()
    for e, buf, w in ((0, dGb, wbk), (1, dAb, wck)):
        w.wait()
        v = mm(LX[e, :, :half], half_panel(buf, 0), NT) + mm(LX[e, :, half:], half_panel(buf, 1), NT)
        if e == 0:
            dHa[1] = v
            wuk = panel(2, dGb, 23).start()
            pump(1, mix[2])
            pump(1, mix[1])
        else:
            dHa[1] += v
            pump(1, mix[3])
            pump(1, mix[0])
    wuk.wait()
    dHa[1] += mm(LX[2, :, :half], half_panel(dGb, 0), NT) + mm(LX[2, :, half:], half_panel(dGb, 1), NT)
    px.wait()

    def back_one(m, _):
        rs = pl.ds(pl.multiple_of(m * 128, 128), 128)
        inv, n1 = norm(SX[1, rs].astype(F32))
        d = dHa[1, rs]
        SG[0:1] += jnp.sum(d * n1, axis=0, keepdims=True)
        dn = d * GN[0:1]
        SX[0, rs] = (dHa[0, rs] + inv * (dn - n1 * jnp.mean(dn * n1, axis=-1, keepdims=True))).astype(BF)
        return 0
    lax.fori_loop(0, rows // 128, back_one, 0)
    save_gx = Load(30, (SX.at[0], gx_o)).start()
    rest = jnp.zeros((LANES - 8, width), F32)
    GS[...] = jnp.concatenate([SG[...], rest], axis=0).T.astype(BF).reshape(GS.shape)
    start_sums(4)
    pump(1)
    x_add(1, dHa.at[3], 2)

    def finish(m, _):
        rs = pl.ds(pl.multiple_of(m * 128, 128), 128)
        SX[1, rs] = dHa[3, rs].astype(BF)
        return 0
    lax.fori_loop(0, rows // 128, finish, 0)
    save_out = Load(31, (SX.at[1], out_o)).start()
    while live:
        pump(1)
    save_gx.wait()
    save_out.wait()
    for c in own_out:
        c.wait()
    cp.drain()
    ct.drain()
    cx.drain()


def block_call(x, df, masks, blocks, gus, ds, parts, nz, cid):
    rows, width = x.shape
    shard, cols = gus.shape[2], gus.shape[3]
    K = len(parts)
    dr = ds.shape[0]
    V = pl.BlockSpec(memory_space=pltpu.VMEM)
    A = pl.BlockSpec(memory_space=pl.ANY)
    D = pltpu.SemaphoreType.DMA
    M = pltpu.VMEM
    maxc = max(parts) * 2 * nz
    sp = sum_pieces(width)
    ngather = len(gather_pieces(width))
    scratch = dict(
        H=M((2, 2, 2, 2, nz, shard, width), BF),
        dF=M((2, 2, 2, 2, nz, shard, width), BF),
        WGU=M((2, TP, nz, 2, shard, cols), BF),
        WD=[M((2, nz, r, width), BF) for r in parts],
        dHa=M((TP, rows, width), F32),
        Zb=M((TP, 2, 2, nz, shard, cols), BF),
        dAb=M((2, 2, 2, 2, nz, shard, maxc), BF),
        dGb=M((2, 2, 2, 2, nz, shard, maxc), BF),
        GD=[M((2, nz, r, width), BF) for r in parts],
        RY=M((TP, nz, 2, shard, cols), BF),
        ZGU=M((nz, TP, 2, shard, cols), BF),
        ZD=[M((nz, r, width), BF) for r in parts],
        YD=[M((nz, r, width), BF) for r in parts],
        LX=M((4, rows, width), BF),
        SX=M((3, rows, width), BF),
        GN=M((8, width), F32),
        SG=M((8, width), F32),
        SM=M((2, 2, 2, nz, shard, LANES), BF),
        PV=M((2, 16, width), BF),
        NX=M((2, 16, width), BF),
        land=sum_scratch(nz, shard, sp),
        gather=gather_sems(nz, ngather),
        sum=sum_sems(nz, len(sp)),
        sem=D((48,)), sem_h=D((2, 2, 3)), s_h=D((2, 2)), r_h=D((2, 2)),
        s_p0=D((K, 3)), r_p0=D((K, 3)),
        s_z=D((K, 2 * nz)), r_z=D((K, nz)), s_y=D((K, nz)), r_y=D((K, nz)),
        s_dz=D((K, 2, 2 * nz)), r_dz=D((K, 2, nz)), s_dy=D((K,)), r_dy=D((K,)),
        s_gy=D((K, 2, nz)), r_gy=D((K, 2, nz)), s_gz=D((K, 2, nz)), r_gz=D((K, 2, nz)),
        s_gt=D((K, 2, 3)), r_gt=D((K, 2, 3)),
        s_ez=D((K, nz)), r_ez=D((K, nz)), s_ey=D((K, nz)), r_ey=D((K, nz)),
        s_x=D((2, 3)), r_x=D((2, 3)), ready=pltpu.SemaphoreType.REGULAR,
    )
    S = jax.ShapeDtypeStruct
    wide = [width] * 4 + [LANES]
    outs = pl.pallas_call(
        functools.partial(block_body, parts, nz),
        name="block",
        out_shape=[
            S((rows, width), BF), S((rows, width), BF),
            S((TP, 2, shard, cols), BF), S((dr, width), F32),
            *[S((shard, w), F32) for w in (3 * width, width, LANES)],
            *[S((2, 2, 2, nz, shard, w), BF) for w in wide],
            S((5, rows, width), F32), S((3, rows, width), BF),
        ],
        in_specs=[A, A] + [V] * 6 + [A, A],
        out_specs=[A, A, A] + [V] * 4 + [A] * 7,
        scratch_shapes=[scratch],
        compiler_params=pltpu.CompilerParams(
            collective_id=cid, has_side_effects=True, vmem_limit_bytes=67_000_000),
    )(x, df.reshape(2, 2, nz, shard, width), masks, *blocks, gus, ds)
    return outs[:7]


def shifted(block, axis, distance):
    devices = range(lax.axis_size(axis))
    route = [(i - distance, i) for i in devices if i - distance in devices]
    return lax.ppermute(block, axis, route)


def matmul(left, right):
    return jnp.dot(left, right, preferred_element_type=jnp.float32)


def norm_parts(values):
    inverse = lax.rsqrt(jnp.mean(values * values, axis=-1, keepdims=True) + eps)
    return (inverse, values * inverse)


def norm_back(grad_hidden, normed, inverse, gain):
    grad_normed = grad_hidden * gain
    inner_mean = jnp.mean(grad_normed * normed, axis=-1, keepdims=True)
    return inverse * (grad_normed - normed * inner_mean)


def plain_device(
    tokens,
    segments,
    ln1_gain,
    in_weight,
    conv_kernel,
    out_weight,
    ln2_gain,
    gate_weight,
    up_weight,
    down_weight,
    cotangent,
):
    micro_count = tokens.shape[0]
    row_count = tokens.shape[2]
    width = tokens.shape[3]
    taps = conv_kernel.shape[0]
    offset = lax.axis_index("seq") * row_count
    low_gain1 = ln1_gain.astype(jnp.bfloat16)
    low_in = in_weight.astype(jnp.bfloat16)
    low_kernel = conv_kernel.astype(jnp.bfloat16)
    low_out = out_weight.astype(jnp.bfloat16)
    low_gain2 = ln2_gain.astype(jnp.bfloat16)
    low_gate = gate_weight.astype(jnp.bfloat16)
    low_up = up_weight.astype(jnp.bfloat16)
    low_down = down_weight.astype(jnp.bfloat16)
    shard_totals = None
    full_totals = None
    out_list = []
    grad_list = []
    for micro_index in range(micro_count):
        weights = (
            lax.all_gather(low_gain1, ("dp", "seq"), axis=0, tiled=True),
            lax.all_gather(low_in, ("dp", "seq"), axis=0, tiled=True),
            lax.all_gather(low_kernel, ("dp", "seq"), axis=1, tiled=True),
            lax.all_gather(low_out, ("dp", "seq"), axis=0, tiled=True),
            lax.all_gather(low_gain2, ("dp", "seq"), axis=0, tiled=True),
            lax.all_gather(low_gate, ("dp", "seq"), axis=0, tiled=True),
            lax.all_gather(low_up, ("dp", "seq"), axis=0, tiled=True),
            lax.all_gather(low_down, ("dp", "seq"), axis=0, tiled=True),
        )
        gain_one = weights[0].astype(jnp.float32)
        kernel = weights[2].astype(jnp.float32)
        gain_two = weights[4].astype(jnp.float32)
        seg_line = segments[micro_index, 0]
        fill = jnp.full((2,), -1, jnp.int32)
        seg_pad = jnp.concatenate([fill, seg_line, fill])
        window = lax.dynamic_slice_in_dim(seg_pad, offset, row_count + 4)
        masks = [
            (window[tap : tap + row_count + 2] == window[2 : row_count + 4]).astype(jnp.float32)
            for tap in range(taps)
        ]
        tokens_f = tokens[micro_index, 0].astype(jnp.float32)
        inverse_one, normed_one = norm_parts(tokens_f)
        hidden_one = (normed_one * gain_one).astype(jnp.bfloat16)
        projected = matmul(hidden_one, weights[1])
        b_part = projected[:, :width]
        c_part = projected[:, width : 2 * width]
        x_part = projected[:, 2 * width :]
        mixed = (b_part * x_part).astype(jnp.bfloat16)
        prev_rows = shifted(mixed[row_count - 2 :], "seq", 1)
        extended = jnp.concatenate([prev_rows, mixed], axis=0).astype(jnp.float32)
        conv_out = jnp.zeros((row_count, width), jnp.float32)
        for tap in range(taps):
            conv_out = (
                conv_out
                + kernel[tap] * extended[tap : tap + row_count] * masks[tap][:row_count, None]
            )
        gated = (c_part * conv_out).astype(jnp.bfloat16)
        resid = tokens_f + matmul(gated, weights[3])
        inverse_two, normed_two = norm_parts(resid)
        hidden_two = (normed_two * gain_two).astype(jnp.bfloat16)
        gate_pre = matmul(hidden_two, weights[5])
        up_pre = matmul(hidden_two, weights[6])
        sigmoid_gate = jax.nn.sigmoid(gate_pre)
        activated = gate_pre * sigmoid_gate
        inner = (activated * up_pre).astype(jnp.bfloat16)
        ffn_out = matmul(inner, weights[7])
        out_list.append((resid + ffn_out).astype(jnp.bfloat16))
        back_weights = (
            lax.all_gather(low_gain1, ("dp", "seq"), axis=0, tiled=True),
            lax.all_gather(low_in, ("dp", "seq"), axis=0, tiled=True),
            lax.all_gather(low_kernel, ("dp", "seq"), axis=1, tiled=True),
            lax.all_gather(low_out, ("dp", "seq"), axis=0, tiled=True),
            lax.all_gather(low_gain2, ("dp", "seq"), axis=0, tiled=True),
            lax.all_gather(low_gate, ("dp", "seq"), axis=0, tiled=True),
            lax.all_gather(low_up, ("dp", "seq"), axis=0, tiled=True),
            lax.all_gather(low_down, ("dp", "seq"), axis=0, tiled=True),
        )
        grad_final = cotangent[micro_index, 0]
        grad_inner = matmul(grad_final, back_weights[7].T)
        part_down = matmul(inner.T, grad_final)
        grad_gate_pre = (
            grad_inner * up_pre * sigmoid_gate * (1.0 + gate_pre * (1.0 - sigmoid_gate))
        ).astype(jnp.bfloat16)
        grad_up_pre = (grad_inner * activated).astype(jnp.bfloat16)
        grad_hidden_two = matmul(grad_gate_pre, back_weights[5].T) + matmul(
            grad_up_pre, back_weights[6].T
        )
        part_gate = matmul(hidden_two.T, grad_gate_pre)
        part_up = matmul(hidden_two.T, grad_up_pre)
        part_gain2 = jnp.sum(grad_hidden_two * normed_two, axis=0)
        grad_resid = grad_final.astype(jnp.float32) + norm_back(
            grad_hidden_two, normed_two, inverse_two, gain_two
        )
        grad_branch = grad_resid.astype(jnp.bfloat16)
        grad_gated = matmul(grad_branch, back_weights[3].T)
        part_out = matmul(gated.T, grad_branch)
        grad_c = grad_gated * conv_out
        grad_conv = (grad_gated * c_part).astype(jnp.bfloat16)
        next_rows = shifted(grad_conv[:2], "seq", -1)
        grad_extended = jnp.concatenate([grad_conv, next_rows], axis=0).astype(jnp.float32)
        grad_mixed = jnp.zeros((row_count, width), jnp.float32)
        kernel_terms = []
        for tap in range(taps):
            weighted = grad_extended * masks[tap][:, None]
            grad_mixed = grad_mixed + kernel[tap] * weighted[2 - tap : 2 - tap + row_count]
            kernel_terms.append(
                jnp.sum(weighted[:row_count] * extended[tap : tap + row_count], axis=0)
            )
        part_kernel = jnp.stack(kernel_terms, axis=0)
        grad_proj = jnp.concatenate(
            [grad_mixed * x_part, grad_c, grad_mixed * b_part], axis=1
        ).astype(jnp.bfloat16)
        grad_hidden_one = matmul(grad_proj, back_weights[1].T)
        part_in = matmul(hidden_one.T, grad_proj)
        part_gain1 = jnp.sum(grad_hidden_one * normed_one, axis=0)
        grad_input = grad_resid + norm_back(grad_hidden_one, normed_one, inverse_one, gain_one)
        grad_list.append(grad_input.astype(jnp.bfloat16))
        parts = (
            part_gain1,
            part_in,
            part_kernel,
            part_out,
            part_gain2,
            part_gate,
            part_up,
            part_down,
        )
        full_totals = (
            parts
            if full_totals is None
            else tuple((first + second for first, second in zip(full_totals, parts)))
        )
    shard_totals = (
        lax.psum_scatter(full_totals[0], ("dp", "seq"), scatter_dimension=0, tiled=True),
        lax.psum_scatter(full_totals[1], ("dp", "seq"), scatter_dimension=0, tiled=True),
        lax.psum_scatter(full_totals[2], ("dp", "seq"), scatter_dimension=1, tiled=True),
        lax.psum_scatter(full_totals[3], ("dp", "seq"), scatter_dimension=0, tiled=True),
        lax.psum_scatter(full_totals[4], ("dp", "seq"), scatter_dimension=0, tiled=True),
        lax.psum_scatter(full_totals[5], ("dp", "seq"), scatter_dimension=0, tiled=True),
        lax.psum_scatter(full_totals[6], ("dp", "seq"), scatter_dimension=0, tiled=True),
        lax.psum_scatter(full_totals[7], ("dp", "seq"), scatter_dimension=0, tiled=True),
    )
    output = jnp.stack(out_list, axis=0)[:, None]
    grad_tokens = jnp.stack(grad_list, axis=0)[:, None]
    return (
        output,
        grad_tokens,
        shard_totals[0],
        shard_totals[1],
        shard_totals[2],
        shard_totals[3],
        shard_totals[4],
        shard_totals[5],
        shard_totals[6],
        shard_totals[7],
    )


def cut_columns(w, parts, ny, nz):
    rows, shard = w.shape[0], w.shape[1] // (ny * TP * nz)
    cut = w.astype(BF).reshape(rows, ny, TP, nz, shard)
    pieces, start = [], 0
    for size in parts:
        piece = cut[..., start : start + size].transpose(2, 0, 1, 3, 4)
        pieces.append(piece.reshape(TP, rows, ny * nz * size))
        start += size
    return jnp.concatenate(pieces, axis=-1)


def join_columns(g, parts, ny, nz):
    rows = g.shape[1]
    pieces, start, npos = [], 0, ny * nz
    for size in parts:
        piece = g[:, :, npos * start : npos * (start + size)].reshape(TP, rows, ny, nz, size)
        pieces.append(piece.transpose(1, 2, 0, 3, 4))
        start += size
    return jnp.concatenate(pieces, axis=-1).reshape(rows, -1).astype(F32)


def fast_device(
    parts,
    tokens,
    segments,
    ln1_gain,
    in_weight,
    conv_kernel,
    out_weight,
    ln2_gain,
    gate_weight,
    up_weight,
    down_weight,
    cotangent,
):
    micro, _, count, width = tokens.shape
    taps = conv_kernel.shape[0]
    nz = lax.axis_size("seq")
    ny = lax.axis_size("dp") // TP
    rows = micro * count
    low_in = in_weight.astype(BF)
    small = jnp.concatenate([ln1_gain[None], ln2_gain[None], conv_kernel], axis=0).astype(BF)
    small = jnp.pad(small.T, ((0, 0), (0, LANES - taps - 2)))
    blocks = [low_in[:, q * width : (q + 1) * width] for q in range(3)]
    blocks += [out_weight.astype(BF), small]
    offset = lax.axis_index("seq") * count
    fill = jnp.full((micro, 2), -1, jnp.int32)
    seg_pad = jnp.concatenate([fill, segments[:, 0], fill, fill, fill, fill], axis=1)
    window = lax.dynamic_slice_in_dim(seg_pad, offset, count + 10, axis=1)
    masks = jnp.stack(
        [window[:, tap : tap + count + 8] == window[:, 2 : count + 10] for tap in range(taps)], axis=-1
    ).astype(F32)
    masks = jnp.pad(masks, ((0, 0), (0, 0), (0, LANES - taps)))
    gus = jnp.stack([cut_columns(w, parts, ny, nz) for w in (gate_weight, up_weight)], axis=1)
    output, gx, gu, gd, g_in, g_out, g_small = block_call(
        tokens.reshape(rows, width), cotangent.reshape(rows, width), masks, blocks, gus,
        down_weight.astype(BF), parts, nz, 0
    )
    g_gate = join_columns(gu[:, 0], parts, ny, nz)
    g_up = join_columns(gu[:, 1], parts, ny, nz)
    g_small = g_small[:, : taps + 2].T
    shape = tokens.shape
    return (
        output.reshape(shape), gx.reshape(shape), g_small[0], g_in, g_small[2:], g_out,
        g_small[1], g_gate, g_up, gd,
    )


def row_parts(mesh, token_shape, down_shape):
    nd, nz = mesh.shape["dp"], mesh.shape["seq"]
    if nd != 2 * TP:
        return None
    per = down_shape[0] // (nd * nz)
    shard = token_shape[3] // (nd * nz)
    rows = token_shape[0] * (token_shape[2] // nz)
    if per <= 64 or per % 16 or shard % 16 or token_shape[1] != nd or token_shape[0] != 2:
        return None
    if rows != 4 * nz * shard or token_shape[3] != 2 * rows or 128 * nz != rows:
        return None
    return (per - 64, 64)


def solution(mesh):
    in_specs = (
        P(None, "dp", "seq", None),
        P(None, "dp", None),
        P(("dp", "seq")),
        P(("dp", "seq"), None),
        P(None, ("dp", "seq")),
        P(("dp", "seq"), None),
        P(("dp", "seq")),
        P(("dp", "seq"), None),
        P(("dp", "seq"), None),
        P(("dp", "seq"), None),
        P(None, "dp", "seq", None),
    )
    out_specs = (
        P(None, "dp", "seq", None),
        P(None, "dp", "seq", None),
        P(("dp", "seq")),
        P(("dp", "seq"), None),
        P(None, ("dp", "seq")),
        P(("dp", "seq"), None),
        P(("dp", "seq")),
        P(("dp", "seq"), None),
        P(("dp", "seq"), None),
        P(("dp", "seq"), None),
    )

    def run(*arrays):
        parts = row_parts(mesh, arrays[0].shape, arrays[9].shape)
        device = plain_device if parts is None else functools.partial(fast_device, parts)
        return jax.shard_map(
            device, mesh=mesh, in_specs=in_specs, out_specs=out_specs, check_vma=False
        )(*arrays)

    return run
```

```python
import functools
import jax
import jax.numpy as jnp
from jax import lax
from jax.experimental import pallas as pl
from jax.experimental.pallas import tpu as pltpu
from jax.sharding import PartitionSpec as P

BF = jnp.bfloat16
F32 = jnp.float32
eps = 1e-05
MESH = pl.DeviceIdType.MESH
NN = (((1,), (0,)), ((), ()))
NT = (((1,), (1,)), ((), ()))
TN = (((0,), (0,)), ((), ()))
TP = 4
LANES = 128


def mm(left, right, dims):
    return lax.dot_general(left, right, dims, preferred_element_type=F32)


def when(pred, body):
    if pred is True:
        body()
    else:
        pl.when(pred)(body)


class Place:
    def __init__(self, nz):
        dp = lax.axis_index("dp")
        self.y = dp // TP
        self.i = dp % TP
        self.z = lax.axis_index("seq")
        self.nz = nz
        self.x = self.i // 2
        self.c = self.i % 2
        self.others = tuple(self._near(k) for k in range(nz - 1))

    def _near(self, k):
        ranks = [sorted((q for q in range(self.nz) if q != z), key=lambda q: abs(q - z)) for z in range(self.nz)]
        place = jnp.int32(ranks[0][k])
        for z in range(1, self.nz):
            place = jnp.where(self.z == z, ranks[z][k], place)
        return place

    def to_both_sides(self, cp, block, ssem, rsem):
        for to, there in ((self.z - 1, self.z > 0), (self.z + 1, self.z < self.nz - 1)):
            cp.send(block, block, ssem(to), rsem, self.at(z=to), there)

    def relay(self, cp, block, source, ssem, rsem):
        to = jnp.where(source < self.z, self.z + 1, self.z - 1)
        cp.send(block, block, ssem, rsem, self.at(z=to), (to >= 0) & (to < self.nz))

    def member(self, t):
        x = 1 - self.x if t // 2 else self.x
        c = 1 - self.c if t % 2 else self.c
        return x * 2 + c

    def at(self, y=None, i=None, z=None):
        y = self.y if y is None else y
        i = self.i if i is None else i
        z = self.z if z is None else z
        return (y * TP + i, z)


class Copies:
    def __init__(self):
        self.pending = []

    def send(self, src, dst, ssem, rsem, device, pred=True, group=None):
        def make():
            return pltpu.make_async_remote_copy(
                src_ref=src, dst_ref=dst, send_sem=ssem, recv_sem=rsem,
                device_id=device, device_id_type=MESH)
        when(pred, lambda: make().start())
        if group is None:
            self.pending.append((pred, make))

    def local(self, src, dst, sem):
        pltpu.make_async_copy(src, dst, sem).start()

    def arrived(self, ref, ssem, rsem, device, pred=True):
        when(pred, lambda: pltpu.make_async_remote_copy(
            src_ref=ref, dst_ref=ref, send_sem=ssem, recv_sem=rsem,
            device_id=device, device_id_type=MESH).wait_recv())

    def drain(self, count=None):
        done = self.pending[:count]
        self.pending = self.pending[len(done):]
        for pred, make in done:
            when(pred, lambda make=make: make().wait_send())


def entry_barrier(p):
    bar = pltpu.get_barrier_semaphore()
    there = [p.at(i=p.member(t)) for t in range(1, TP)] + [p.at(y=1 - p.y)] + [p.at(z=q) for q in p.others]
    for device in there:
        pl.semaphore_signal(bar, inc=1, device_id=device, device_id_type=MESH)
    return lambda: pl.semaphore_wait(bar, len(there))


def gather_pieces(width):
    half = width // 2
    return (
        (4, 0, LANES, "zyx"),
        (0, 0, half, "zyx"), (0, half, half, "zxy"),
        (2, 0, half, "xzy"), (2, half, half, "yzx"),
        (1, 0, half, "zyx"), (1, half, half, "zxy"),
        (3, 0, half, "xzy"), (3, half, half, "yzx"),
    )


def sum_pieces(width):
    half = width // 2
    return (
        (3, 0, half, "zyx"), (3, half, half, "zxy"),
        (1, 0, half, "zyx"), (1, half, half, "zxy"),
        (0, 0, half, "zyx"), (0, half, half, "zxy"),
        (2, 0, half, "zyx"), (2, half, half, "zxy"),
        (4, 0, LANES, "zyx"),
    )


def gather_sems(nz, count):
    D = pltpu.SemaphoreType.DMA
    return [D((count, 2, 2 * nz)), D((count, 2, nz)), D((count, nz)), D((count, nz)), D((count, 2, nz)),
            D((count, 2, nz)), D((count,)), D((count,))]


def gather_flow(p, cp, n, piece, W, sems):
    s_z, r_z, s_1, r_1, s_2, r_2, s_c, r_c = sems
    _, c0, cn, order = piece
    cs = slice(c0, c0 + cn)
    z, nz = p.z, p.nz
    a_is_x = order.index("x") < order.index("y")
    zfirst = order[0] == "z"

    def blk(a, b, zz):
        y, x = (b, a) if a_is_x else (a, b)
        return W.at[y, x, p.c, zz, :, cs]
    a, b = (p.x, p.y) if a_is_x else (p.y, p.x)
    dev_x, dev_y = p.at(i=p.member(2)), p.at(y=1 - p.y)
    dev_a, dev_b = (dev_x, dev_y) if a_is_x else (dev_y, dev_x)

    def core(aa, bb, zz):
        r = blk(aa, bb, zz)
        cp.send(r, r, s_c.at[n], r_c.at[n], p.at(i=p.member(1)), group=True)

    def zsend(aa):
        p.to_both_sides(cp, blk(aa, b, z), lambda to: s_z.at[n, aa, to], r_z.at[n, aa, z])

    def asend(zz):
        r = blk(a, b, zz)
        cp.send(r, r, s_1.at[n, zz], r_1.at[n, zz], dev_a)

    def bsend(aa, zz):
        r = blk(aa, b, zz)
        cp.send(r, r, s_2.at[n, aa, zz], r_2.at[n, aa, zz], dev_b)

    asend(z)
    zsend(a)
    bsend(a, z)
    core(a, b, z)
    yield "first"
    if not zfirst:
        cp.arrived(blk(1 - a, b, z), s_1.at[n, z], r_1.at[n, z], p.at())
        zsend(1 - a)
        bsend(1 - a, z)
        core(1 - a, b, z)
    for zz in p.others:
        yield "z"
        for aa in ((a,) if zfirst else (a, 1 - a)):
            cp.arrived(blk(aa, b, zz), s_z.at[n, aa, zz], r_z.at[n, aa, zz], p.at())
            p.relay(cp, blk(aa, b, zz), zz, s_z.at[n, aa, nz + zz], r_z.at[n, aa, zz])
            if zfirst:
                asend(zz)
            bsend(aa, zz)
            core(aa, b, zz)
    if zfirst:
        yield "second"
        for zz in (z,) + p.others:
            cp.arrived(blk(1 - a, b, zz), s_1.at[n, zz], r_1.at[n, zz], p.at())
            bsend(1 - a, zz)
            core(1 - a, b, zz)
    for zz in (z,) + p.others:
        yield "last axis"
        for aa in (a, 1 - a):
            cp.arrived(blk(aa, 1 - b, zz), s_2.at[n, aa, zz], r_2.at[n, aa, zz], p.at())
            core(aa, 1 - b, zz)
    yield "core"
    cp.arrived(W.at[:, :, 1 - p.c, :, :, cs], s_c.at[n], r_c.at[n], p.at())
    cp.pending.append((True, lambda: pltpu.make_async_remote_copy(
        src_ref=W.at[:, :, p.c, :, :, cs], dst_ref=W.at[:, :, p.c, :, :, cs], send_sem=s_c.at[n],
        recv_sem=r_c.at[n], device_id=p.at(i=p.member(1)), device_id_type=MESH)))


def sum_sems(nz, count):
    D = pltpu.SemaphoreType.DMA
    return [D((count,)), D((count,)), D((count, nz)), D((count, nz)), D((count, nz)), D((count, nz)),
            D((count, nz)), D((count, nz))]


def sum_scratch(nz, shard, pieces):
    return dict(
        one=[pltpu.VMEM((2, nz, shard, q[2]), BF) for q in pieces],
        two=[pltpu.VMEM((nz if q[3][0] == "z" else 1, shard, q[2]), BF) for q in pieces],
        path=[pltpu.VMEM((nz, 1 if q[3][0] == "z" else 2, shard, q[2]), BF) for q in pieces],
    )


def sum_flow(p, cp, n, piece, G, LC, L1, L2, LZ, out, sems):
    s_c, r_c, s_1, r_1, s_2, r_2, s_z, r_z = sems
    _, c0, cn, order = piece
    cs = slice(c0, c0 + cn)
    z = p.z
    targets = p.others[::-1] + (z,)
    zlast = order[0] == "z"
    b_is_y = order.index("x") < order.index("y")
    b, a = (p.y, p.x) if b_is_y else (p.x, p.y)
    dev_x, dev_y = p.at(i=p.member(2)), p.at(y=1 - p.y)
    dev_b, dev_a = (dev_y, dev_x) if b_is_y else (dev_x, dev_y)

    def g(bb, aa, zz):
        y, x = (bb, aa) if b_is_y else (aa, bb)
        return (y, x, p.c, zz, slice(None), cs)

    def f(v):
        return v.astype(F32)

    def lc(bb, aa, zz):
        y, x = (bb, aa) if b_is_y else (aa, bb)
        return (y, x, zz)

    def row(bb, zz, aa=None):
        aa = slice(None) if aa is None else pl.ds(aa, 1)
        y, x = (bb, aa) if b_is_y else (aa, bb)
        return G.at[y, x, p.c, zz, :, cs]
    cp.send(G.at[:, :, 1 - p.c, :, :, cs], LC, s_c.at[n], r_c.at[n], p.at(i=p.member(1)))
    LZ[z] = jnp.zeros(LZ.shape[1:], BF)
    yield
    cp.arrived(LC, s_c.at[n], r_c.at[n], p.at())
    def add_core(bb):
        def one(zz, _):
            for aa in range(2):
                i = g(bb, aa, zz)
                G[i] = (f(G[i]) + f(LC[lc(bb, aa, zz)])).astype(BF)
            return 0
        lax.fori_loop(0, p.nz, one, 0)
    add_core(1 - b)
    for zz in targets:
        cp.send(row(1 - b, zz), L1.at[:, zz], s_1.at[n, zz], r_1.at[n, zz], dev_b)
    add_core(b)
    if zlast:
        yield
        for zz in targets:
            cp.arrived(L1.at[:, zz], s_1.at[n, zz], r_1.at[n, zz], p.at())
            i = g(b, 1 - a, zz)
            G[i] = (f(G[i]) + f(L1[1 - a, zz])).astype(BF)
            cp.send(G.at[i], L2.at[zz], s_2.at[n, zz], r_2.at[n, zz], dev_a)

    def own(zz, k):
        if zlast:
            return f(G[g(b, a, zz)]) + f(L1[a, zz]) + f(L2[zz])
        return f(G[g(b, k, zz)]) + f(L1[k, zz])
    yield
    for zz in targets:
        if zlast:
            cp.arrived(L2.at[zz], s_2.at[n, zz], r_2.at[n, zz], p.at())
        else:
            cp.arrived(L1.at[:, zz], s_1.at[n, zz], r_1.at[n, zz], p.at())
        if zz is z:
            continue
        for k in range(1 if zlast else 2):
            G[g(b, a if zlast else k, zz)] = own(zz, k).astype(BF)
        cp.send(row(b, zz, a if zlast else None), LZ.at[z], s_z.at[n, zz], r_z.at[n, z], p.at(z=zz))
    yield
    for zz in p.others:
        cp.arrived(LZ.at[zz], s_z.at[n, zz], r_z.at[n, zz], p.at())

    def total(k):
        v = own(z, k)
        for zz in range(p.nz):
            v = v + f(LZ[zz, k])
        return v
    if zlast:
        out[:, cs] = total(0)
        return
    G[g(b, 1 - a, z)] = total(1 - a).astype(BF)
    cp.send(G.at[g(b, 1 - a, z)], L2.at[0], s_2.at[n, 0], r_2.at[n, 0], dev_a)
    out[:, cs] = total(a)
    yield
    cp.arrived(L2.at[0], s_2.at[n, 0], r_2.at[n, 0], p.at())
    out[:, cs] += f(L2[0])


def slot(ref, t):
    return ref.at[t // 2, t % 2]


def block_body(parts, nz, x_in, df_in, masks, b0, b1, b2, b3, b4, gus, ds,
               out_o, gx_o, ogu_o, od_o, m012, m3, m4, W0, W1, W2, W3, W4, SV32, SV16, s):
    p = Place(nz)
    z = p.z
    rows, width = x_in.shape
    shard = gus.shape[2]
    npos = 2 * nz
    count = rows // 2
    half = width // 2
    low = rows // (2 * nz)
    offs = [sum(parts[:k]) for k in range(len(parts))]
    CH = [(offs[k] * npos, parts[k] * npos) for k in range(len(parts))]
    K = len(parts)
    cp, cx, ct = Copies(), Copies(), Copies()
    cg = [Copies() for _ in range(K)]
    first, last = z == 0, z == nz - 1
    inner_l, inner_r = z > 0, z < nz - 1
    H, dF, WGU, WD, dHa, Zb, dAb, dGb = (s[k] for k in ("H", "dF", "WGU", "WD", "dHa", "Zb", "dAb", "dGb"))
    GGU = WGU
    GD, RY, ZGU, ZD, YD, LX, SX = (s[k] for k in ("GD", "RY", "ZGU", "ZD", "YD", "LX", "SX"))
    sem_h, s_p0, r_p0, s_z, r_z, s_y, r_y, s_dz, r_dz, s_dy, r_dy = (
        s[k] for k in ("sem_h", "s_p0", "r_p0", "s_z", "r_z", "s_y", "r_y", "s_dz", "r_dz", "s_dy", "r_dy"))
    s_gy, r_gy, s_gz, r_gz, s_gt, r_gt, s_ez, r_ez, s_ey, r_ey, s_x, r_x = (
        s[k] for k in ("s_gy", "r_gy", "s_gz", "r_gz", "s_gt", "r_gt", "s_ez", "r_ez", "s_ey", "r_ey", "s_x", "r_x"))
    sem = s["sem"]
    GN, SG, SM, PV, NX = (s[k] for k in ("GN", "SG", "SM", "PV", "NX"))
    GS = SM
    W = (W0, W1, W2, W3, W4)
    sums = tuple(m012.at[:, q * width:(q + 1) * width] for q in range(3)) + (m3, m4)

    def cols(k):
        return slice(CH[k][0], CH[k][0] + CH[k][1])

    def rws(k):
        return slice(offs[k], offs[k] + parts[k])

    class Load:
        def __init__(self, n, *pairs):
            self.copies = [pltpu.make_async_copy(a, b, sem.at[n + k]) for k, (a, b) in enumerate(pairs)]

        def start(self):
            for c in self.copies:
                c.start()
            return self

        def wait(self):
            for c in self.copies:
                c.wait()

    all_here = entry_barrier(p)
    own_w = Load(0, *[(b, w.at[p.y, p.x, p.c, z]) for b, w in zip((b0, b1, b2, b3, b4), W)]).start()
    own_x = Load(5, (x_in, SX.at[0])).start()
    df_blocks = df_in
    own_df = Load(6, (df_blocks, slot(dF, 0))).start()
    own_gu = Load(7, (gus.at[p.i], WGU.at[p.y, p.i, z])).start()
    own_d = Load(8, *[(ds.at[rws(k)], WD[k].at[p.y, z]) for k in range(K)]).start()

    ZGU[z] = jnp.zeros(ZGU.shape[1:], BF)
    for k in range(K):
        ZD[k][z] = jnp.zeros(ZD[k].shape[1:], BF)

    @pl.when(first)
    def _():
        PV[...] = jnp.zeros(PV.shape, BF)

    @pl.when(last)
    def _():
        NX[...] = jnp.zeros(NX.shape, BF)

    def p0(k):
        for t in (2, 3, 1):
            m = p.member(t)
            cg[k].send(gus.at[m, :, :, cols(k)], WGU.at[p.y, p.i, z, :, :, cols(k)],
                       s_p0.at[k, t - 1], r_p0.at[k, t - 1], p.at(i=m))

    def acts(dst, q):
        for t in (2, 1):
            cp.send(slot(dst, 0), slot(dst, t), sem_h.at[q, 0, t - 1], sem_h.at[q, 1, t - 1], p.at(i=p.member(t)))

    def acts_wait(dst, q, t):
        cp.arrived(slot(dst, t), sem_h.at[q, 0, t - 1], sem_h.at[q, 1, t - 1], p.at(i=p.member(t)))

    def acts_forward(dst, q):
        acts_wait(dst, q, 2)
        cp.send(slot(dst, 2), slot(dst, 3), sem_h.at[q, 0, 2], sem_h.at[q, 1, 2], p.at(i=p.member(1)))

    def gu_blk(k, y, zz):
        return WGU.at[y, :, zz, :, :, cols(k)]

    def ysend(k, zz):
        b = gu_blk(k, p.y, zz)
        cg[k].send(b, b, s_y.at[k, zz], r_y.at[k, zz], p.at(y=1 - p.y))

    def flow_ag(k):
        W = WD[k]
        for t in (1, 2, 3):
            m = p.member(t)
            cp.arrived(WGU.at[p.y, m, z, :, :, cols(k)], s_p0.at[k, t - 1], r_p0.at[k, t - 1], p.at(i=m))
        p.to_both_sides(cg[k], gu_blk(k, p.y, z), lambda to: s_z.at[k, to], r_z.at[k, z])
        b = W.at[p.y, z]
        cg[k].send(b, b, s_dy.at[k], r_dy.at[k], p.at(y=1 - p.y))
        p.to_both_sides(cg[k], b, lambda to: s_dz.at[k, p.y, to], r_dz.at[k, p.y, z])
        yield
        ysend(k, z)
        b = W.at[1 - p.y, z]
        cp.arrived(b, s_dy.at[k], r_dy.at[k], p.at())
        p.to_both_sides(cg[k], b, lambda to: s_dz.at[k, 1 - p.y, to], r_dz.at[k, 1 - p.y, z])
        for zz in p.others:
            yield
            b = gu_blk(k, p.y, zz)
            cp.arrived(b, s_z.at[k, zz], r_z.at[k, zz], p.at())
            p.relay(cg[k], b, zz, s_z.at[k, nz + zz], r_z.at[k, zz])
            ysend(k, zz)
            for y in (p.y, 1 - p.y):
                b = W.at[y, zz]
                cp.arrived(b, s_dz.at[k, y, zz], r_dz.at[k, y, zz], p.at())
                p.relay(cg[k], b, zz, s_dz.at[k, y, nz + zz], r_dz.at[k, y, zz])
        yield
        for zz in (z,) + p.others:
            cp.arrived(gu_blk(k, 1 - p.y, zz), s_y.at[k, zz], r_y.at[k, zz], p.at())

    targets = p.others[::-1] + (z,)

    def flow_rs_gu(k, w):
        c = cols(k)
        for zz in targets:
            cp.send(GGU.at[1 - p.y, :, zz, w, :, c], RY.at[:, zz, w, :, c],
                    s_gy.at[k, w, zz], r_gy.at[k, w, zz], p.at(y=1 - p.y))
        for zz in p.others[::-1]:
            yield
            cp.arrived(RY.at[:, zz, w, :, c], s_gy.at[k, w, zz], r_gy.at[k, w, zz], p.at())

            def add(j, _, zz=zz):
                GGU[p.y, j, zz, w, :, c] = (
                    GGU[p.y, j, zz, w, :, c].astype(F32) + RY[j, zz, w, :, c].astype(F32)).astype(BF)
                return 0
            lax.fori_loop(0, TP, add, 0)
            cp.send(GGU.at[p.y, :, zz, w, :, c], ZGU.at[z, :, w, :, c], s_gz.at[k, w, zz], r_gz.at[k, w, z],
                    p.at(z=zz))
        yield
        cp.arrived(RY.at[:, z, w, :, c], s_gy.at[k, w, z], r_gy.at[k, w, z], p.at())
        for zz in p.others:
            cp.arrived(ZGU.at[zz, :, w, :, c], s_gz.at[k, w, zz], r_gz.at[k, w, zz], p.at())

        def add_all(j, _):
            v = GGU[p.y, j, z, w, :, c].astype(F32) + RY[j, z, w, :, c].astype(F32)
            for zz in range(nz):
                v = v + ZGU[zz, j, w, :, c].astype(F32)
            GGU[p.y, j, z, w, :, c] = v.astype(BF)
            return 0
        lax.fori_loop(0, TP, add_all, 0)
        for t in (2, 3, 1):
            m = p.member(t)
            cp.send(GGU.at[p.y, m, z, w, :, c], ogu_o.at[p.i, w, :, c], s_gt.at[k, w, t - 1], r_gt.at[k, w, t - 1],
                    p.at(i=m))
        own_out.append(Load(11 + 2 * k + w, (GGU.at[p.y, p.i, z, w, :, c], ogu_o.at[p.i, w, :, c])).start())
        yield
        for t in (1, 2, 3):
            m = p.member(t)
            cp.arrived(ogu_o.at[m, w, :, c], s_gt.at[k, w, t - 1], r_gt.at[k, w, t - 1], p.at(i=m))

    def flow_rs_d(k):
        G, L, Y = GD[k], ZD[k], YD[k]
        for zz in targets:
            cp.send(G.at[1 - p.y, zz], Y.at[zz], s_ey.at[k, zz], r_ey.at[k, zz], p.at(y=1 - p.y))
        for zz in p.others[::-1]:
            yield
            cp.arrived(Y.at[zz], s_ey.at[k, zz], r_ey.at[k, zz], p.at())
            G[p.y, zz] = (G[p.y, zz].astype(F32) + Y[zz].astype(F32)).astype(BF)
            cp.send(G.at[p.y, zz], L.at[z], s_ez.at[k, zz], r_ez.at[k, z], p.at(z=zz))
        yield
        cp.arrived(Y.at[z], s_ey.at[k, z], r_ey.at[k, z], p.at())
        for zz in p.others:
            cp.arrived(L.at[zz], s_ez.at[k, zz], r_ez.at[k, zz], p.at())
        v = G[p.y, z].astype(F32) + Y[z].astype(F32)
        for zz in range(nz):
            v = v + L[zz].astype(F32)
        od_o[rws(k), :] = v

    live, own_out = [], []

    def pump(n=1, which=None):
        for _ in range(n):
            for f in list(live if which is None else which):
                if f in live and next(f, "end") == "end":
                    live.remove(f)

    def run(*gens):
        for g in gens:
            for _ in g:
                pass
            if g in live:
                live.remove(g)

    own_w.wait()
    all_here()
    gp = gather_pieces(width)
    gather = [gather_flow(p, cp, n, q, W[q[0]], s["gather"]) for n, q in enumerate(gp)]
    states = {}

    def gather_to(*stops):
        left = list(gather)
        while left:
            for f in list(left):
                if states.get(f) in stops:
                    left.remove(f)
                else:
                    states[f] = next(f)
    gather_to("first")
    own_gu.wait()
    own_d.wait()
    own_df.wait()
    gather_to("z")
    for k in range(K):
        p0(k)
    gather_to("last axis")
    acts(dF, 1)
    ag = [flow_ag(k) for k in range(K)]
    for g in ag:
        next(g)
    for g in ag:
        next(g)
    gather_to("core")

    def need(*panels):
        for f, q in zip(gather, gp):
            if q[0] in panels:
                next(f, None)

    def panel(q, buf, n):
        return Load(n, *[(W[q].at[:, :, :, :, :, h * half:(h + 1) * half], buf.at[:, h, :, :, :, :, pl.ds(0, half)]) for h in range(2)])

    def half_panel(buf, h):
        return buf[:, h, :, :, :, :, :half].reshape(width, half)

    need(4)
    Load(20, (W4, SM)).start().wait()
    GN[...] = SM[...].reshape(width, LANES).astype(F32).T[:8]
    need(0)
    wb = panel(0, dAb, 21).start()
    own_x.wait()

    def norm(v):
        inv = lax.rsqrt(jnp.mean(v * v, axis=-1, keepdims=True) + eps)
        return inv, v * inv

    def tiles(size):
        return [slice(t * size, (t + 1) * size) for t in range(rows // size)]

    def norm_one(m, _):
        rs = pl.ds(pl.multiple_of(m * 128, 128), 128)
        _, n1 = norm(SX[0, rs].astype(F32))
        SX[1, rs] = (n1 * GN[0:1]).astype(BF)
        return 0
    lax.fori_loop(0, rows // 128, norm_one, 0)
    save_h1 = Load(30, (SX.at[1], SV16.at[0])).start()

    def project(buf, dst):
        for h in range(2):
            dHa[dst, :, h * half:(h + 1) * half] = mm(SX[1], half_panel(buf, h), NN)
    need(2)
    wu = panel(2, dGb, 23).start()
    wb.wait()
    project(dAb, 0)
    need(1)
    wc = panel(1, dAb, 21).start()
    wu.wait()
    project(dGb, 2)
    save_bu = Load(31, (dHa.at[0], SV32.at[0]), (dHa.at[2], SV32.at[2])).start()

    def make_bx(m, _):
        rs = pl.ds(pl.multiple_of(m * 128, 128), 128)
        SX[2, rs] = (dHa[0, rs] * dHa[2, rs]).astype(BF)
        return 0
    lax.fori_loop(0, rows // 128, make_bx, 0)
    s_h, r_h = s["s_h"], s["r_h"]
    for m in range(2):
        cp.send(SX.at[2, pl.ds((m + 1) * count - 16, 16)], PV.at[m], s_h.at[0, m], r_h.at[0, m],
                p.at(z=z + 1), inner_r)
    save_bx = Load(33, (SX.at[2], SV16.at[1])).start()
    live.extend(ag)
    pump(1, ag[:1])
    need(3)
    wo = panel(3, dGb, 23).start()
    wc.wait()
    project(dAb, 1)
    save_c = Load(34, (dHa.at[1], SV32.at[1])).start()
    for m in range(2):
        cp.arrived(PV.at[m], s_h.at[0, m], r_h.at[0, m], p.at(), inner_l)

    def earlier(v, prev, back):
        r = lax.broadcasted_iota(jnp.int32, v.shape, 0)
        n = prev.shape[0]
        moved = pltpu.roll(v, back, 0)
        moved = jnp.where(r == back - 1, prev[n - 1:n], moved)
        return jnp.where(r == 0, prev[n - back:n - back + 1], moved)

    def later(v, after, ahead):
        r = lax.broadcasted_iota(jnp.int32, v.shape, 0)
        n = v.shape[0]
        moved = pltpu.roll(v, n - ahead, 0)
        moved = jnp.where(r == n - ahead, after[0:1], moved)
        return jnp.where(r == n - 1, after[ahead - 1:ahead], moved)

    lanes = 256
    nl = width // lanes

    def conv(q, _):
        m, c = q // nl, q % nl
        ls = pl.ds(pl.multiple_of(c * lanes, lanes), lanes)
        rs = pl.ds(pl.multiple_of(m * count, count), count)
        v = SX[2, rs, ls].astype(F32)
        prev = PV[m, :, ls].astype(F32)
        mk = masks[m]
        total = GN[2:3, ls] * earlier(v, prev, 2) * mk[:count, 0:1]
        total = total + GN[3:4, ls] * earlier(v, prev, 1) * mk[:count, 1:2]
        total = total + GN[4:5, ls] * v * mk[:count, 2:3]
        dHa[3, rs, ls] = total
        LX[0, rs, ls] = (dHa[1, rs, ls] * total).astype(BF)
        return 0
    lax.fori_loop(0, 2 * nl, conv, 0)
    save_cv = Load(35, (dHa.at[3], SV32.at[3]), (LX.at[0], SV16.at[2])).start()
    save_bu.wait()
    pump(1, ag)
    wo.wait()
    for h in range(2):
        hs = slice(h * half, (h + 1) * half)
        dHa[0, :, hs] = SX[0, :, hs].astype(F32) + mm(LX[0], half_panel(dGb, h), NN)

    def norm_two(m, _):
        rs = pl.ds(pl.multiple_of(m * nz * shard, nz * shard), nz * shard)
        _, n2 = norm(dHa[0, rs])
        H[0, 0, m // 2, m % 2] = (n2 * GN[1:2]).astype(BF).reshape(nz, shard, width)
        return 0
    lax.fori_loop(0, 4, norm_two, 0)
    save_r = Load(37, (dHa.at[0], SV32.at[4])).start()
    save_cv.wait()
    acts(H, 0)
    save_h1.wait()
    save_bx.wait()
    save_c.wait()
    save_r.wait()
    pump(1, ag)

    def half_blocks(v):
        return v.reshape(2, nz, shard, v.shape[-1])

    def fwd_mid(k, t):
        c0, cn = CH[k]
        c = cols(k)
        wg = WGU[:, :, :, 0, :, c].reshape(width, cn)
        wu = WGU[:, :, :, 1, :, c].reshape(width, cn)
        wd = WD[k][...].reshape(cn, width)

        def some(r, _):
            rs = pl.ds(pl.multiple_of(r * count, count), count)
            h = H[t // 2, t % 2, r].reshape(count, width)
            a = mm(h, wg, NN)
            g = mm(h, wu, NN)
            dz = mm(dF[t // 2, t % 2, r].reshape(count, width), wd, NT)
            sg = 1.0 / (1.0 + jnp.exp(-a))
            act = a * sg
            Zb[t, r, :, :, :, c] = half_blocks((act * g).astype(BF))
            da = (dz * g * sg * (1.0 + a * (1.0 - sg))).astype(BF)
            dg = (dz * act).astype(BF)
            dAb[t // 2, t % 2, r, :, :, :, :cn] = half_blocks(da)
            dGb[t // 2, t % 2, r, :, :, :, :cn] = half_blocks(dg)
            d = mm(da, wg, NT) + mm(dg, wu, NT)
            if k == 0:
                dHa[t, rs] = d
            else:
                dHa[t, rs] += d
            return 0
        lax.fori_loop(0, 2, some, 0)

    def slots(k, start, step):
        def one(n, _):
            fwd_mid(k, start + step * n)
            return 0
        lax.fori_loop(0, 2, one, 0)

    def ffn_out(slot_of, put):
        def some(q, _):
            n, r = q // 2, q % 2
            t = slot_of(n)
            f = None
            for k in range(K):
                v = mm(Zb[t, r, :, :, :, cols(k)].reshape(count, CH[k][1]), WD[k][...].reshape(CH[k][1], width), NN)
                f = v if f is None else f + v
            put(n, pl.ds(pl.multiple_of(r * count, count), count), f)
            return 0
        lax.fori_loop(0, 4, some, 0)

    tok = TP * rows

    def grads(k):
        c0, cn = CH[k]
        c = cols(k)
        for w, src in ((0, dAb), (1, dGb)):
            def body(m, _, w=w, src=src):
                y, j = m // 2, (m % 2) * 2
                f = 2 * nz * shard
                ms = pl.ds(pl.multiple_of(m * f, f), f)
                v = mm(H[:, :, :, :, :, :, ms].reshape(tok, f), src[:, :, :, :, :, :, :cn].reshape(tok, cn), TN)
                GGU[y, pl.ds(j, 2), :, w, :, c] = v.astype(BF).reshape(2, nz, shard, cn)
                return 0
            lax.fori_loop(0, TP, body, 0)
            begin((k, w), flow_rs_gu(k, w))
            if k == K - 1:
                advance(*(((0, 0), (0, 1)) if w == 0 else ((0, 0), (0, 1), (0, 2))))
        r = parts[k]
        for b in range(cn // 128):
            zb = Zb[:, :, :, :, :, c0 + b * 128:c0 + (b + 1) * 128].reshape(tok, 128)
            v = mm(zb, dF[...].reshape(tok, width), TN).astype(BF)
            lo = b * 128
            while lo < (b + 1) * 128:
                pos, q = lo // r, lo % r
                n = min(r - q, (b + 1) * 128 - lo)
                GD[k][pos // nz, pos % nz, q:q + n] = v[lo - b * 128:lo - b * 128 + n]
                lo += n
        begin((k, 2), flow_rs_d(k))

    rs_flows = {}

    def begin(key, flow):
        next(flow)
        rs_flows[key] = flow
        live.append(flow)

    def advance(*keys):
        for key in keys:
            if rs_flows[key] in live:
                pump(1, [rs_flows[key]])

    def x_land(q, e):
        return LX.at[2 + q] if e == 2 else LX.at[e]

    def x_send1(q, e, value=None):
        if value is not None:
            SX[e] = value.astype(BF)
        cx.send(SX.at[e], x_land(q, e), s_x.at[q, e], r_x.at[q, e], p.at(i=p.member(1)))

    def x_wait(q, e):
        cx.arrived(x_land(q, e), s_x.at[q, e], r_x.at[q, e], p.at(i=p.member(2 if e == 2 else 1)))

    def x_send2(q, acc):
        x_wait(q, 1)
        SX[2] = (acc[...] + LX[1].astype(F32)).astype(BF)
        cx.send(SX.at[2], x_land(q, 2), s_x.at[q, 2], r_x.at[q, 2], p.at(i=p.member(2)))

    def x_add(q, acc, e):
        x_wait(q, e)
        acc[...] += x_land(q, e)[...].astype(F32)

    acts_forward(dF, 1)
    before = 0
    for k in range(K):
        run(ag[k])
        if k == K - 1:
            cp.drain(before)
        if k == 0:
            acts_wait(H, 0, 1)
            acts_wait(dF, 1, 1)
            slots(0, 0, 1)
            acts_forward(H, 0)
            acts_wait(dF, 1, 3)
            acts_wait(H, 0, 3)
            slots(0, 2, 1)
            pump(1, ag[1:2])
        else:
            slots(k, 3, -1)
            if k == K - 1:
                x_send1(0, 1, dHa[3])
                advance((0, 0))
                x_send2(0, dHa.at[2])
                advance((0, 0))
            slots(k, 1, -1)
            if k == K - 1:
                x_send1(0, 0, dHa[1])
                advance((0, 0), (0, 1))
        cg[k].drain()
        before = len(cp.pending)
        grads(k)
    wo = panel(3, dAb, 21).start()
    x_add(0, dHa.at[0], 0)
    pl.semaphore_signal(s["ready"], inc=1, device_id=p.at(i=p.member(1)), device_id_type=MESH)
    pr = Load(40, (SV32.at[4], dHa.at[2])).start()

    def keep(n, rs, v):
        dHa[1 + 2 * n, rs] = v

    def stage(n, rs, v):
        SX[n, rs] = v.astype(BF)
    ffn_out(lambda n: 2 - 2 * n, keep)
    cx.drain(1)
    cx.pending.append(cx.pending.pop(0))
    cx.drain(1)
    ffn_out(lambda n: 1 + 2 * n, stage)
    pl.semaphore_wait(s["ready"], 1)
    x_send1(1, 0)
    x_send1(1, 1)
    x_add(0, dHa.at[0], 2)
    cx.drain(1)
    x_send2(1, dHa.at[1])
    x_add(1, dHa.at[3], 0)

    pc = Load(41, (SV32.at[1], dHa.at[1])).start()
    cx.drain(2)
    py = Load(42, (SV16.at[2], SX.at[0]), (SV16.at[0], SX.at[1])).start()
    pr.wait()
    SG[...] = jnp.zeros(SG.shape, F32)

    def back_two(m, _):
        n = nz * shard
        rs = pl.ds(pl.multiple_of(m * n, n), n)
        r = dHa[2, rs]
        dHa[3, rs] += r
        inv, n2 = norm(r)
        d = dHa[0, rs]
        SG[1:2] += jnp.sum(d * n2, axis=0, keepdims=True)
        dn = d * GN[1:2]
        df = dF[0, 0, m // 2, m % 2].reshape(n, width).astype(F32)
        dr = df + inv * (dn - n2 * jnp.mean(dn * n2, axis=-1, keepdims=True))
        dHa[0, rs] = dr
        WD[0][m // 2, pl.ds((m % 2) * (nz // 2), nz // 2), :low] = dr.astype(BF).reshape(nz // 2, low, width)
        return 0
    lax.fori_loop(0, 4, back_two, 0)
    pcv = Load(44, (SV32.at[3], dHa.at[2])).start()
    advance((1, 0))
    wo.wait()
    pc.wait()
    pcv.wait()
    wbk = panel(0, dGb, 23).start()

    def back_y(m, _):
        rs = pl.ds(pl.multiple_of(m * count, count), count)
        do = WD[0][m, :, :low].reshape(count, width)
        dy = mm(do[:, :half], half_panel(dAb, 0), NT) + mm(do[:, half:], half_panel(dAb, 1), NT)
        LX[1, rs] = (dy * dHa[2, rs]).astype(BF)
        WD[1][m, :, :low] = (dy * dHa[1, rs]).astype(BF).reshape(nz, low, width)
        return 0
    lax.fori_loop(0, 2, back_y, 0)
    advance((1, 0))
    wck = panel(1, dAb, 21).start()
    for m in range(2):
        cp.send(WD[1].at[m, 0, pl.ds(0, 16)], NX.at[m], s_h.at[1, m], r_h.at[1, m], p.at(z=z - 1), inner_l)
    pu = Load(41, (SV32.at[2], dHa.at[1])).start()
    pb = Load(44, (SV32.at[0], dHa.at[2])).start()

    panels = (H.at[0], H.at[1], dF.at[0], dF.at[1], GS)
    sp = sum_pieces(width)

    mix = {}

    def start_sums(q):
        for n, piece in enumerate(sp):
            if piece[0] != q:
                continue
            _, c0, cn, _ = piece
            lc = Zb.at[q, :, :, :, :, pl.ds(c0, cn)] if q < 4 else Zb.at[3, :, :, :, :, pl.ds(width, LANES)]
            g = sum_flow(p, ct, n, piece, panels[q], lc, s["land"]["one"][n], s["land"]["two"][n],
                         s["land"]["path"][n], sums[q], s["sum"])
            next(g)
            live.append(g)
            mix.setdefault(q, []).append(g)

    def weight_grad(q, left, right):
        def body(m, _):
            f = 2 * nz * shard
            ms = pl.ds(pl.multiple_of(m * f, f), f)
            v = mm(left(ms), right(), TN)
            panels[q][m // 2, m % 2] = v.astype(BF).reshape(2, nz, shard, width)
            return 0
        lax.fori_loop(0, width // (2 * nz * shard), body, 0)
        start_sums(q)

    py.wait()
    weight_grad(3, lambda ms: SX[0, :, ms], lambda: WD[0][:, :, :low].reshape(rows, width))
    advance((1, 0), (1, 1))
    weight_grad(1, lambda ms: SX[1, :, ms], lambda: LX[1])
    pbx = Load(42, (SV16.at[1], SX.at[0])).start()
    advance((1, 1))
    pump(1, mix[3])
    for m in range(2):
        cp.arrived(NX.at[m], s_h.at[1, m], r_h.at[1, m], p.at(), inner_r)
    pu.wait()
    pb.wait()
    pbx.wait()

    def back_conv(q, _):
        m, c = q // nl, q % nl
        ls = pl.ds(pl.multiple_of(c * lanes, lanes), lanes)
        rs = pl.ds(pl.multiple_of(m * count, count), count)
        v = SX[0, rs, ls].astype(F32)
        prev = PV[m, :, ls].astype(F32)
        dcv = WD[1][m, :, :low, ls].reshape(count, lanes).astype(F32)
        after = NX[m, :, ls].astype(F32)
        mk = masks[m]
        w0, w1, w2 = (dcv * mk[:count, t:t + 1] for t in range(3))
        SG[2:3, ls] += jnp.sum(w0 * earlier(v, prev, 2), axis=0, keepdims=True)
        SG[3:4, ls] += jnp.sum(w1 * earlier(v, prev, 1), axis=0, keepdims=True)
        SG[4:5, ls] += jnp.sum(w2 * v, axis=0, keepdims=True)
        tail = mk[count:count + 8]
        d = GN[2:3, ls] * later(w0, after[:8] * tail[:, 0:1], 2)
        d = d + GN[3:4, ls] * later(w1, after[:8] * tail[:, 1:2], 1)
        d = d + GN[4:5, ls] * w2
        LX[0, rs, ls] = (d * dHa[1, rs, ls]).astype(BF)
        LX[2, rs, ls] = (d * dHa[2, rs, ls]).astype(BF)
        return 0
    lax.fori_loop(0, 2 * nl, back_conv, 0)
    advance((1, 1), (1, 2), (1, 2))
    pump(1, mix[1])
    weight_grad(0, lambda ms: SX[1, :, ms], lambda: LX[0])
    advance((1, 2), (0, 2), (0, 2))
    weight_grad(2, lambda ms: SX[1, :, ms], lambda: LX[2])
    pump(1, mix[0])
    pump(1, mix[3])
    px = Load(42, (x_in, SX.at[1])).start()
    for e, buf, w in ((0, dGb, wbk), (1, dAb, wck)):
        w.wait()
        v = mm(LX[e, :, :half], half_panel(buf, 0), NT) + mm(LX[e, :, half:], half_panel(buf, 1), NT)
        if e == 0:
            dHa[1] = v
            wuk = panel(2, dGb, 23).start()
            pump(1, mix[2])
            pump(1, mix[1])
        else:
            dHa[1] += v
            pump(1, mix[3])
            pump(1, mix[0])
    wuk.wait()
    dHa[1] += mm(LX[2, :, :half], half_panel(dGb, 0), NT) + mm(LX[2, :, half:], half_panel(dGb, 1), NT)
    px.wait()

    def back_one(m, _):
        rs = pl.ds(pl.multiple_of(m * 128, 128), 128)
        inv, n1 = norm(SX[1, rs].astype(F32))
        d = dHa[1, rs]
        SG[0:1] += jnp.sum(d * n1, axis=0, keepdims=True)
        dn = d * GN[0:1]
        SX[0, rs] = (dHa[0, rs] + inv * (dn - n1 * jnp.mean(dn * n1, axis=-1, keepdims=True))).astype(BF)
        return 0
    lax.fori_loop(0, rows // 128, back_one, 0)
    save_gx = Load(30, (SX.at[0], gx_o)).start()
    rest = jnp.zeros((LANES - 8, width), F32)
    GS[...] = jnp.concatenate([SG[...], rest], axis=0).T.astype(BF).reshape(GS.shape)
    start_sums(4)
    pump(1)
    x_add(1, dHa.at[3], 2)

    def finish(m, _):
        rs = pl.ds(pl.multiple_of(m * 128, 128), 128)
        SX[1, rs] = dHa[3, rs].astype(BF)
        return 0
    lax.fori_loop(0, rows // 128, finish, 0)
    save_out = Load(31, (SX.at[1], out_o)).start()
    while live:
        pump(1)
    save_gx.wait()
    save_out.wait()
    for c in own_out:
        c.wait()
    cp.drain()
    ct.drain()
    cx.drain()


def block_call(x, df, masks, blocks, gus, ds, parts, nz, cid):
    rows, width = x.shape
    shard, cols = gus.shape[2], gus.shape[3]
    K = len(parts)
    dr = ds.shape[0]
    V = pl.BlockSpec(memory_space=pltpu.VMEM)
    A = pl.BlockSpec(memory_space=pl.ANY)
    D = pltpu.SemaphoreType.DMA
    M = pltpu.VMEM
    maxc = max(parts) * 2 * nz
    sp = sum_pieces(width)
    ngather = len(gather_pieces(width))
    scratch = dict(
        H=M((2, 2, 2, 2, nz, shard, width), BF),
        dF=M((2, 2, 2, 2, nz, shard, width), BF),
        WGU=M((2, TP, nz, 2, shard, cols), BF),
        WD=[M((2, nz, r, width), BF) for r in parts],
        dHa=M((TP, rows, width), F32),
        Zb=M((TP, 2, 2, nz, shard, cols), BF),
        dAb=M((2, 2, 2, 2, nz, shard, maxc), BF),
        dGb=M((2, 2, 2, 2, nz, shard, maxc), BF),
        GD=[M((2, nz, r, width), BF) for r in parts],
        RY=M((TP, nz, 2, shard, cols), BF),
        ZGU=M((nz, TP, 2, shard, cols), BF),
        ZD=[M((nz, r, width), BF) for r in parts],
        YD=[M((nz, r, width), BF) for r in parts],
        LX=M((4, rows, width), BF),
        SX=M((3, rows, width), BF),
        GN=M((8, width), F32),
        SG=M((8, width), F32),
        SM=M((2, 2, 2, nz, shard, LANES), BF),
        PV=M((2, 16, width), BF),
        NX=M((2, 16, width), BF),
        land=sum_scratch(nz, shard, sp),
        gather=gather_sems(nz, ngather),
        sum=sum_sems(nz, len(sp)),
        sem=D((48,)), sem_h=D((2, 2, 3)), s_h=D((2, 2)), r_h=D((2, 2)),
        s_p0=D((K, 3)), r_p0=D((K, 3)),
        s_z=D((K, 2 * nz)), r_z=D((K, nz)), s_y=D((K, nz)), r_y=D((K, nz)),
        s_dz=D((K, 2, 2 * nz)), r_dz=D((K, 2, nz)), s_dy=D((K,)), r_dy=D((K,)),
        s_gy=D((K, 2, nz)), r_gy=D((K, 2, nz)), s_gz=D((K, 2, nz)), r_gz=D((K, 2, nz)),
        s_gt=D((K, 2, 3)), r_gt=D((K, 2, 3)),
        s_ez=D((K, nz)), r_ez=D((K, nz)), s_ey=D((K, nz)), r_ey=D((K, nz)),
        s_x=D((2, 3)), r_x=D((2, 3)), ready=pltpu.SemaphoreType.REGULAR,
    )
    S = jax.ShapeDtypeStruct
    wide = [width] * 4 + [LANES]
    outs = pl.pallas_call(
        functools.partial(block_body, parts, nz),
        name="block",
        out_shape=[
            S((rows, width), BF), S((rows, width), BF),
            S((TP, 2, shard, cols), BF), S((dr, width), F32),
            *[S((shard, w), F32) for w in (3 * width, width, LANES)],
            *[S((2, 2, 2, nz, shard, w), BF) for w in wide],
            S((5, rows, width), F32), S((3, rows, width), BF),
        ],
        in_specs=[A, A] + [V] * 6 + [A, A],
        out_specs=[A, A, A] + [V] * 4 + [A] * 7,
        scratch_shapes=[scratch],
        compiler_params=pltpu.CompilerParams(
            collective_id=cid, has_side_effects=True, vmem_limit_bytes=67_000_000),
    )(x, df.reshape(2, 2, nz, shard, width), masks, *blocks, gus, ds)
    return outs[:7]


def shifted(block, axis, distance):
    devices = range(lax.axis_size(axis))
    route = [(i - distance, i) for i in devices if i - distance in devices]
    return lax.ppermute(block, axis, route)


def matmul(left, right):
    return jnp.dot(left, right, preferred_element_type=jnp.float32)


def norm_parts(values):
    inverse = lax.rsqrt(jnp.mean(values * values, axis=-1, keepdims=True) + eps)
    return (inverse, values * inverse)


def norm_back(grad_hidden, normed, inverse, gain):
    grad_normed = grad_hidden * gain
    inner_mean = jnp.mean(grad_normed * normed, axis=-1, keepdims=True)
    return inverse * (grad_normed - normed * inner_mean)


def plain_device(
    tokens,
    segments,
    ln1_gain,
    in_weight,
    conv_kernel,
    out_weight,
    ln2_gain,
    gate_weight,
    up_weight,
    down_weight,
    cotangent,
):
    micro_count = tokens.shape[0]
    row_count = tokens.shape[2]
    width = tokens.shape[3]
    taps = conv_kernel.shape[0]
    offset = lax.axis_index("seq") * row_count
    low_gain1 = ln1_gain.astype(jnp.bfloat16)
    low_in = in_weight.astype(jnp.bfloat16)
    low_kernel = conv_kernel.astype(jnp.bfloat16)
    low_out = out_weight.astype(jnp.bfloat16)
    low_gain2 = ln2_gain.astype(jnp.bfloat16)
    low_gate = gate_weight.astype(jnp.bfloat16)
    low_up = up_weight.astype(jnp.bfloat16)
    low_down = down_weight.astype(jnp.bfloat16)
    shard_totals = None
    full_totals = None
    out_list = []
    grad_list = []
    for micro_index in range(micro_count):
        weights = (
            lax.all_gather(low_gain1, ("dp", "seq"), axis=0, tiled=True),
            lax.all_gather(low_in, ("dp", "seq"), axis=0, tiled=True),
            lax.all_gather(low_kernel, ("dp", "seq"), axis=1, tiled=True),
            lax.all_gather(low_out, ("dp", "seq"), axis=0, tiled=True),
            lax.all_gather(low_gain2, ("dp", "seq"), axis=0, tiled=True),
            lax.all_gather(low_gate, ("dp", "seq"), axis=0, tiled=True),
            lax.all_gather(low_up, ("dp", "seq"), axis=0, tiled=True),
            lax.all_gather(low_down, ("dp", "seq"), axis=0, tiled=True),
        )
        gain_one = weights[0].astype(jnp.float32)
        kernel = weights[2].astype(jnp.float32)
        gain_two = weights[4].astype(jnp.float32)
        seg_line = segments[micro_index, 0]
        fill = jnp.full((2,), -1, jnp.int32)
        seg_pad = jnp.concatenate([fill, seg_line, fill])
        window = lax.dynamic_slice_in_dim(seg_pad, offset, row_count + 4)
        masks = [
            (window[tap : tap + row_count + 2] == window[2 : row_count + 4]).astype(jnp.float32)
            for tap in range(taps)
        ]
        tokens_f = tokens[micro_index, 0].astype(jnp.float32)
        inverse_one, normed_one = norm_parts(tokens_f)
        hidden_one = (normed_one * gain_one).astype(jnp.bfloat16)
        projected = matmul(hidden_one, weights[1])
        b_part = projected[:, :width]
        c_part = projected[:, width : 2 * width]
        x_part = projected[:, 2 * width :]
        mixed = (b_part * x_part).astype(jnp.bfloat16)
        prev_rows = shifted(mixed[row_count - 2 :], "seq", 1)
        extended = jnp.concatenate([prev_rows, mixed], axis=0).astype(jnp.float32)
        conv_out = jnp.zeros((row_count, width), jnp.float32)
        for tap in range(taps):
            conv_out = (
                conv_out
                + kernel[tap] * extended[tap : tap + row_count] * masks[tap][:row_count, None]
            )
        gated = (c_part * conv_out).astype(jnp.bfloat16)
        resid = tokens_f + matmul(gated, weights[3])
        inverse_two, normed_two = norm_parts(resid)
        hidden_two = (normed_two * gain_two).astype(jnp.bfloat16)
        gate_pre = matmul(hidden_two, weights[5])
        up_pre = matmul(hidden_two, weights[6])
        sigmoid_gate = jax.nn.sigmoid(gate_pre)
        activated = gate_pre * sigmoid_gate
        inner = (activated * up_pre).astype(jnp.bfloat16)
        ffn_out = matmul(inner, weights[7])
        out_list.append((resid + ffn_out).astype(jnp.bfloat16))
        back_weights = (
            lax.all_gather(low_gain1, ("dp", "seq"), axis=0, tiled=True),
            lax.all_gather(low_in, ("dp", "seq"), axis=0, tiled=True),
            lax.all_gather(low_kernel, ("dp", "seq"), axis=1, tiled=True),
            lax.all_gather(low_out, ("dp", "seq"), axis=0, tiled=True),
            lax.all_gather(low_gain2, ("dp", "seq"), axis=0, tiled=True),
            lax.all_gather(low_gate, ("dp", "seq"), axis=0, tiled=True),
            lax.all_gather(low_up, ("dp", "seq"), axis=0, tiled=True),
            lax.all_gather(low_down, ("dp", "seq"), axis=0, tiled=True),
        )
        grad_final = cotangent[micro_index, 0]
        grad_inner = matmul(grad_final, back_weights[7].T)
        part_down = matmul(inner.T, grad_final)
        grad_gate_pre = (
            grad_inner * up_pre * sigmoid_gate * (1.0 + gate_pre * (1.0 - sigmoid_gate))
        ).astype(jnp.bfloat16)
        grad_up_pre = (grad_inner * activated).astype(jnp.bfloat16)
        grad_hidden_two = matmul(grad_gate_pre, back_weights[5].T) + matmul(
            grad_up_pre, back_weights[6].T
        )
        part_gate = matmul(hidden_two.T, grad_gate_pre)
        part_up = matmul(hidden_two.T, grad_up_pre)
        part_gain2 = jnp.sum(grad_hidden_two * normed_two, axis=0)
        grad_resid = grad_final.astype(jnp.float32) + norm_back(
            grad_hidden_two, normed_two, inverse_two, gain_two
        )
        grad_branch = grad_resid.astype(jnp.bfloat16)
        grad_gated = matmul(grad_branch, back_weights[3].T)
        part_out = matmul(gated.T, grad_branch)
        grad_c = grad_gated * conv_out
        grad_conv = (grad_gated * c_part).astype(jnp.bfloat16)
        next_rows = shifted(grad_conv[:2], "seq", -1)
        grad_extended = jnp.concatenate([grad_conv, next_rows], axis=0).astype(jnp.float32)
        grad_mixed = jnp.zeros((row_count, width), jnp.float32)
        kernel_terms = []
        for tap in range(taps):
            weighted = grad_extended * masks[tap][:, None]
            grad_mixed = grad_mixed + kernel[tap] * weighted[2 - tap : 2 - tap + row_count]
            kernel_terms.append(
                jnp.sum(weighted[:row_count] * extended[tap : tap + row_count], axis=0)
            )
        part_kernel = jnp.stack(kernel_terms, axis=0)
        grad_proj = jnp.concatenate(
            [grad_mixed * x_part, grad_c, grad_mixed * b_part], axis=1
        ).astype(jnp.bfloat16)
        grad_hidden_one = matmul(grad_proj, back_weights[1].T)
        part_in = matmul(hidden_one.T, grad_proj)
        part_gain1 = jnp.sum(grad_hidden_one * normed_one, axis=0)
        grad_input = grad_resid + norm_back(grad_hidden_one, normed_one, inverse_one, gain_one)
        grad_list.append(grad_input.astype(jnp.bfloat16))
        parts = (
            part_gain1,
            part_in,
            part_kernel,
            part_out,
            part_gain2,
            part_gate,
            part_up,
            part_down,
        )
        full_totals = (
            parts
            if full_totals is None
            else tuple((first + second for first, second in zip(full_totals, parts)))
        )
    shard_totals = (
        lax.psum_scatter(full_totals[0], ("dp", "seq"), scatter_dimension=0, tiled=True),
        lax.psum_scatter(full_totals[1], ("dp", "seq"), scatter_dimension=0, tiled=True),
        lax.psum_scatter(full_totals[2], ("dp", "seq"), scatter_dimension=1, tiled=True),
        lax.psum_scatter(full_totals[3], ("dp", "seq"), scatter_dimension=0, tiled=True),
        lax.psum_scatter(full_totals[4], ("dp", "seq"), scatter_dimension=0, tiled=True),
        lax.psum_scatter(full_totals[5], ("dp", "seq"), scatter_dimension=0, tiled=True),
        lax.psum_scatter(full_totals[6], ("dp", "seq"), scatter_dimension=0, tiled=True),
        lax.psum_scatter(full_totals[7], ("dp", "seq"), scatter_dimension=0, tiled=True),
    )
    output = jnp.stack(out_list, axis=0)[:, None]
    grad_tokens = jnp.stack(grad_list, axis=0)[:, None]
    return (
        output,
        grad_tokens,
        shard_totals[0],
        shard_totals[1],
        shard_totals[2],
        shard_totals[3],
        shard_totals[4],
        shard_totals[5],
        shard_totals[6],
        shard_totals[7],
    )


def cut_columns(w, parts, ny, nz):
    rows, shard = w.shape[0], w.shape[1] // (ny * TP * nz)
    cut = w.astype(BF).reshape(rows, ny, TP, nz, shard)
    pieces, start = [], 0
    for size in parts:
        piece = cut[..., start : start + size].transpose(2, 0, 1, 3, 4)
        pieces.append(piece.reshape(TP, rows, ny * nz * size))
        start += size
    return jnp.concatenate(pieces, axis=-1)


def join_columns(g, parts, ny, nz):
    rows = g.shape[1]
    pieces, start, npos = [], 0, ny * nz
    for size in parts:
        piece = g[:, :, npos * start : npos * (start + size)].reshape(TP, rows, ny, nz, size)
        pieces.append(piece.transpose(1, 2, 0, 3, 4))
        start += size
    return jnp.concatenate(pieces, axis=-1).reshape(rows, -1).astype(F32)


def fast_device(
    parts,
    tokens,
    segments,
    ln1_gain,
    in_weight,
    conv_kernel,
    out_weight,
    ln2_gain,
    gate_weight,
    up_weight,
    down_weight,
    cotangent,
):
    micro, _, count, width = tokens.shape
    taps = conv_kernel.shape[0]
    nz = lax.axis_size("seq")
    ny = lax.axis_size("dp") // TP
    rows = micro * count
    low_in = in_weight.astype(BF)
    small = jnp.concatenate([ln1_gain[None], ln2_gain[None], conv_kernel], axis=0).astype(BF)
    small = jnp.pad(small.T, ((0, 0), (0, LANES - taps - 2)))
    blocks = [low_in[:, q * width : (q + 1) * width] for q in range(3)]
    blocks += [out_weight.astype(BF), small]
    offset = lax.axis_index("seq") * count
    fill = jnp.full((micro, 2), -1, jnp.int32)
    seg_pad = jnp.concatenate([fill, segments[:, 0], fill, fill, fill, fill], axis=1)
    window = lax.dynamic_slice_in_dim(seg_pad, offset, count + 10, axis=1)
    masks = jnp.stack(
        [window[:, tap : tap + count + 8] == window[:, 2 : count + 10] for tap in range(taps)], axis=-1
    ).astype(F32)
    masks = jnp.pad(masks, ((0, 0), (0, 0), (0, LANES - taps)))
    gus = jnp.stack([cut_columns(w, parts, ny, nz) for w in (gate_weight, up_weight)], axis=1)
    output, gx, gu, gd, g_in, g_out, g_small = block_call(
        tokens.reshape(rows, width), cotangent.reshape(rows, width), masks, blocks, gus,
        down_weight.astype(BF), parts, nz, 0
    )
    g_gate = join_columns(gu[:, 0], parts, ny, nz)
    g_up = join_columns(gu[:, 1], parts, ny, nz)
    g_small = g_small[:, : taps + 2].T
    shape = tokens.shape
    return (
        output.reshape(shape), gx.reshape(shape), g_small[0], g_in, g_small[2:], g_out,
        g_small[1], g_gate, g_up, gd,
    )


def row_parts(mesh, token_shape, down_shape):
    nd, nz = mesh.shape["dp"], mesh.shape["seq"]
    if nd != 2 * TP:
        return None
    per = down_shape[0] // (nd * nz)
    shard = token_shape[3] // (nd * nz)
    rows = token_shape[0] * (token_shape[2] // nz)
    if per <= 64 or per % 16 or shard % 16 or token_shape[1] != nd or token_shape[0] != 2:
        return None
    if rows != 4 * nz * shard or token_shape[3] != 2 * rows or 128 * nz != rows:
        return None
    return (per - 64, 64)


def solution(mesh):
    in_specs = (
        P(None, "dp", "seq", None),
        P(None, "dp", None),
        P(("dp", "seq")),
        P(("dp", "seq"), None),
        P(None, ("dp", "seq")),
        P(("dp", "seq"), None),
        P(("dp", "seq")),
        P(("dp", "seq"), None),
        P(("dp", "seq"), None),
        P(("dp", "seq"), None),
        P(None, "dp", "seq", None),
    )
    out_specs = (
        P(None, "dp", "seq", None),
        P(None, "dp", "seq", None),
        P(("dp", "seq")),
        P(("dp", "seq"), None),
        P(None, ("dp", "seq")),
        P(("dp", "seq"), None),
        P(("dp", "seq")),
        P(("dp", "seq"), None),
        P(("dp", "seq"), None),
        P(("dp", "seq"), None),
    )

    def run(*arrays):
        parts = row_parts(mesh, arrays[0].shape, arrays[9].shape)
        device = plain_device if parts is None else functools.partial(fast_device, parts)
        return jax.shard_map(
            device, mesh=mesh, in_specs=in_specs, out_specs=out_specs, check_vma=False
        )(*arrays)

    return run
```

```python
import functools
import jax
import jax.numpy as jnp
from jax import lax
from jax.experimental import pallas as pl
from jax.experimental.pallas import tpu as pltpu
from jax.sharding import PartitionSpec as P

BF = jnp.bfloat16
F32 = jnp.float32
eps = 1e-05
MESH = pl.DeviceIdType.MESH
NN = (((1,), (0,)), ((), ()))
NT = (((1,), (1,)), ((), ()))
TN = (((0,), (0,)), ((), ()))
TP = 4
LANES = 128


def mm(left, right, dims):
    return lax.dot_general(left, right, dims, preferred_element_type=F32)


def when(pred, body):
    if pred is True:
        body()
    else:
        pl.when(pred)(body)


class Place:
    def __init__(self, nz):
        dp = lax.axis_index("dp")
        self.dp = dp
        self.y = dp // TP
        self.i = dp % TP
        self.z = lax.axis_index("seq")
        self.nz = nz
        self.x = self.i // 2
        self.c = self.i % 2
        self.others = tuple(self._near(k) for k in range(nz - 1))

    def _near(self, k):
        ranks = [sorted((q for q in range(self.nz) if q != z), key=lambda q: abs(q - z)) for z in range(self.nz)]
        place = jnp.int32(ranks[0][k])
        for z in range(1, self.nz):
            place = jnp.where(self.z == z, ranks[z][k], place)
        return place

    def to_both_sides(self, cp, block, ssem, rsem):
        for to, there in ((self.z - 1, self.z > 0), (self.z + 1, self.z < self.nz - 1)):
            cp.send(block, block, ssem(to), rsem, self.at(z=to), there)

    def relay(self, cp, block, source, ssem, rsem):
        to = jnp.where(source < self.z, self.z + 1, self.z - 1)
        cp.send(block, block, ssem, rsem, self.at(z=to), (to >= 0) & (to < self.nz))

    def member(self, t):
        x = 1 - self.x if t // 2 else self.x
        c = 1 - self.c if t % 2 else self.c
        return x * 2 + c

    def at(self, y=None, i=None, z=None):
        z = self.z if z is None else z
        if y is None and i is None:
            return (self.dp, z)
        y = self.y if y is None else y
        i = self.i if i is None else i
        return (y * TP + i, z)


class Copies:
    def __init__(self):
        self.pending = []

    def send(self, src, dst, ssem, rsem, device, pred=True, group=None):
        def make():
            return pltpu.make_async_remote_copy(
                src_ref=src, dst_ref=dst, send_sem=ssem, recv_sem=rsem,
                device_id=device, device_id_type=MESH)
        when(pred, lambda: make().start())
        if group is None:
            self.pending.append((pred, make))

    def local(self, src, dst, sem):
        pltpu.make_async_copy(src, dst, sem).start()

    def arrived(self, ref, ssem, rsem, device, pred=True):
        when(pred, lambda: pltpu.make_async_remote_copy(
            src_ref=ref, dst_ref=ref, send_sem=ssem, recv_sem=rsem,
            device_id=device, device_id_type=MESH).wait_recv())

    def drain(self, count=None):
        done = self.pending[:count]
        self.pending = self.pending[len(done):]
        for pred, make in done:
            when(pred, lambda make=make: make().wait_send())


def entry_barrier(p):
    bar = pltpu.get_barrier_semaphore()
    there = [p.at(i=p.member(t)) for t in range(1, TP)] + [p.at(y=1 - p.y)] + [p.at(z=q) for q in p.others]
    for device in there:
        pl.semaphore_signal(bar, inc=1, device_id=device, device_id_type=MESH)
    return lambda: pl.semaphore_wait(bar, len(there))


def gather_pieces(width):
    return (
        (4, 0, LANES, "zyx"),
        (0, 0, width, "zyx"),
        (2, 0, width, "xzy"),
        (1, 0, width, "zxy"),
        (3, 0, width, "yzx"),
    )


def sum_pieces(width):
    half = width // 2
    return (
        (3, 0, half, "zyx"), (3, half, half, "zxy"),
        (1, 0, half, "zyx"), (1, half, half, "zxy"),
        (0, 0, half, "zyx"), (0, half, half, "zxy"),
        (2, 0, half, "zyx"), (2, half, half, "zxy"),
        (4, 0, LANES, "zyx"),
    )


def gather_sems(nz, count):
    D = pltpu.SemaphoreType.DMA
    return [D((count, 2, 2 * nz)), D((count, 2, nz)), D((count, nz)), D((count, nz)), D((count, 2, nz)),
            D((count, 2, nz)), D((count,)), D((count,))]


def gather_flow(p, cp, n, piece, W, sems):
    s_z, r_z, s_1, r_1, s_2, r_2, s_c, r_c = sems
    _, c0, cn, order = piece
    cs = slice(c0, c0 + cn)
    z, nz = p.z, p.nz
    a_is_x = order.index("x") < order.index("y")
    zfirst = order[0] == "z"

    def blk(a, b, zz):
        y, x = (b, a) if a_is_x else (a, b)
        return W.at[y, x, p.c, zz, :, cs]
    a, b = (p.x, p.y) if a_is_x else (p.y, p.x)
    dev_x, dev_y = p.at(i=p.member(2)), p.at(y=1 - p.y)
    dev_a, dev_b = (dev_x, dev_y) if a_is_x else (dev_y, dev_x)

    def core(aa, bb, zz):
        r = blk(aa, bb, zz)
        cp.send(r, r, s_c.at[n], r_c.at[n], p.at(i=p.member(1)), group=True)

    def zsend(aa):
        p.to_both_sides(cp, blk(aa, b, z), lambda to: s_z.at[n, aa, to], r_z.at[n, aa, z])

    def asend(zz):
        r = blk(a, b, zz)
        cp.send(r, r, s_1.at[n, zz], r_1.at[n, zz], dev_a)

    def bsend(aa, zz):
        r = blk(aa, b, zz)
        cp.send(r, r, s_2.at[n, aa, zz], r_2.at[n, aa, zz], dev_b)

    asend(z)
    zsend(a)
    bsend(a, z)
    core(a, b, z)
    yield "first"
    if not zfirst:
        cp.arrived(blk(1 - a, b, z), s_1.at[n, z], r_1.at[n, z], p.at())
        zsend(1 - a)
        bsend(1 - a, z)
        core(1 - a, b, z)
    for zz in p.others:
        yield "z"
        for aa in ((a,) if zfirst else (a, 1 - a)):
            cp.arrived(blk(aa, b, zz), s_z.at[n, aa, zz], r_z.at[n, aa, zz], p.at())
            p.relay(cp, blk(aa, b, zz), zz, s_z.at[n, aa, nz + zz], r_z.at[n, aa, zz])
            if zfirst:
                asend(zz)
            bsend(aa, zz)
            core(aa, b, zz)
    if zfirst:
        yield "second"
        for zz in (z,) + p.others:
            cp.arrived(blk(1 - a, b, zz), s_1.at[n, zz], r_1.at[n, zz], p.at())
            bsend(1 - a, zz)
            core(1 - a, b, zz)
    for zz in (z,) + p.others:
        yield "last axis"
        for aa in (a, 1 - a):
            cp.arrived(blk(aa, 1 - b, zz), s_2.at[n, aa, zz], r_2.at[n, aa, zz], p.at())
            core(aa, 1 - b, zz)
    yield "core"
    cp.arrived(W.at[:, :, 1 - p.c, :, :, cs], s_c.at[n], r_c.at[n], p.at())
    cp.pending.append((True, lambda: pltpu.make_async_remote_copy(
        src_ref=W.at[:, :, p.c, :, :, cs], dst_ref=W.at[:, :, p.c, :, :, cs], send_sem=s_c.at[n],
        recv_sem=r_c.at[n], device_id=p.at(i=p.member(1)), device_id_type=MESH)))


def sum_sems(nz, count):
    D = pltpu.SemaphoreType.DMA
    return [D((count,)), D((count,)), D((count, nz)), D((count, nz)), D((count, nz)), D((count, nz)),
            D((count, nz)), D((count, nz))]


def sum_scratch(nz, shard, pieces):
    return dict(
        one=[pltpu.VMEM((2, nz, shard, q[2]), BF) for q in pieces],
        two=[pltpu.VMEM((nz if q[3][0] == "z" else 1, shard, q[2]), BF) for q in pieces],
        path=[pltpu.VMEM((nz, 1 if q[3][0] == "z" else 2, shard, q[2]), BF) for q in pieces],
    )


def sum_flow(p, cp, n, piece, G, LC, L1, L2, LZ, out, sems):
    s_c, r_c, s_1, r_1, s_2, r_2, s_z, r_z = sems
    _, c0, cn, order = piece
    cs = slice(c0, c0 + cn)
    z = p.z
    targets = p.others[::-1] + (z,)
    zlast = order[0] == "z"
    b_is_y = order.index("x") < order.index("y")
    b, a = (p.y, p.x) if b_is_y else (p.x, p.y)
    dev_x, dev_y = p.at(i=p.member(2)), p.at(y=1 - p.y)
    dev_b, dev_a = (dev_y, dev_x) if b_is_y else (dev_x, dev_y)

    def g(bb, aa, zz):
        y, x = (bb, aa) if b_is_y else (aa, bb)
        return (y, x, p.c, zz, slice(None), cs)

    def f(v):
        return v.astype(F32)

    def lc(bb, aa, zz):
        y, x = (bb, aa) if b_is_y else (aa, bb)
        return (y, x, zz)

    def row(bb, zz, aa=None):
        aa = slice(None) if aa is None else pl.ds(aa, 1)
        y, x = (bb, aa) if b_is_y else (aa, bb)
        return G.at[y, x, p.c, zz, :, cs]
    cp.send(G.at[:, :, 1 - p.c, :, :, cs], LC, s_c.at[n], r_c.at[n], p.at(i=p.member(1)))
    LZ[z] = jnp.zeros(LZ.shape[1:], BF)
    yield
    cp.arrived(LC, s_c.at[n], r_c.at[n], p.at())
    def add_core(bb):
        def one(zz, _):
            for aa in range(2):
                i = g(bb, aa, zz)
                G[i] = (f(G[i]) + f(LC[lc(bb, aa, zz)])).astype(BF)
            return 0
        lax.fori_loop(0, p.nz, one, 0)
    add_core(1 - b)
    for zz in targets:
        cp.send(row(1 - b, zz), L1.at[:, zz], s_1.at[n, zz], r_1.at[n, zz], dev_b)
    add_core(b)
    if zlast:
        yield
        for zz in targets:
            cp.arrived(L1.at[:, zz], s_1.at[n, zz], r_1.at[n, zz], p.at())
            i = g(b, 1 - a, zz)
            G[i] = (f(G[i]) + f(L1[1 - a, zz])).astype(BF)
            cp.send(G.at[i], L2.at[zz], s_2.at[n, zz], r_2.at[n, zz], dev_a)

    def own(zz, k):
        if zlast:
            return f(G[g(b, a, zz)]) + f(L1[a, zz]) + f(L2[zz])
        return f(G[g(b, k, zz)]) + f(L1[k, zz])
    yield
    for zz in targets:
        if zlast:
            cp.arrived(L2.at[zz], s_2.at[n, zz], r_2.at[n, zz], p.at())
        else:
            cp.arrived(L1.at[:, zz], s_1.at[n, zz], r_1.at[n, zz], p.at())
        if zz is z:
            continue
        for k in range(1 if zlast else 2):
            G[g(b, a if zlast else k, zz)] = own(zz, k).astype(BF)
        cp.send(row(b, zz, a if zlast else None), LZ.at[z], s_z.at[n, zz], r_z.at[n, z], p.at(z=zz))
    yield
    for zz in p.others:
        cp.arrived(LZ.at[zz], s_z.at[n, zz], r_z.at[n, zz], p.at())

    def total(k):
        v = own(z, k)
        for zz in range(p.nz):
            v = v + f(LZ[zz, k])
        return v
    if zlast:
        out[:, cs] = total(0)
        return
    G[g(b, 1 - a, z)] = total(1 - a).astype(BF)
    cp.send(G.at[g(b, 1 - a, z)], L2.at[0], s_2.at[n, 0], r_2.at[n, 0], dev_a)
    out[:, cs] = total(a)
    yield
    cp.arrived(L2.at[0], s_2.at[n, 0], r_2.at[n, 0], p.at())
    out[:, cs] += f(L2[0])


def slot(ref, t):
    return ref.at[t // 2, t % 2]


def block_body(parts, nz, x_in, df_in, masks, b0, b1, b2, b3, b4, gus, ds,
               out_o, gx_o, ogu_o, od_o, m012, m3, m4, W0, W1, W2, W3, W4, SV32, SV16, s):
    p = Place(nz)
    z = p.z
    rows, width = x_in.shape
    shard = gus.shape[2]
    npos = 2 * nz
    count = rows // 2
    half = width // 2
    low = rows // (2 * nz)
    offs = [sum(parts[:k]) for k in range(len(parts))]
    CH = [(offs[k] * npos, parts[k] * npos) for k in range(len(parts))]
    K = len(parts)
    cp, cx, ct = Copies(), Copies(), Copies()
    cg = [Copies() for _ in range(K)]
    core_dev, x_dev = p.at(i=p.member(1)), p.at(i=p.member(2))
    first, last = z == 0, z == nz - 1
    inner_l, inner_r = z > 0, z < nz - 1
    H, dF, WGU, WD, dHa, Zb, dAb, dGb = (s[k] for k in ("H", "dF", "WGU", "WD", "dHa", "Zb", "dAb", "dGb"))
    GGU = WGU
    GD, RY, ZGU, ZD, YD, LX, SX = (s[k] for k in ("GD", "RY", "ZGU", "ZD", "YD", "LX", "SX"))
    sem_h, s_p0, r_p0, s_z, r_z, s_y, r_y, s_dz, r_dz, s_dy, r_dy = (
        s[k] for k in ("sem_h", "s_p0", "r_p0", "s_z", "r_z", "s_y", "r_y", "s_dz", "r_dz", "s_dy", "r_dy"))
    s_gy, r_gy, s_gz, r_gz, s_gt, r_gt, s_ez, r_ez, s_ey, r_ey, s_x, r_x = (
        s[k] for k in ("s_gy", "r_gy", "s_gz", "r_gz", "s_gt", "r_gt", "s_ez", "r_ez", "s_ey", "r_ey", "s_x", "r_x"))
    sem = s["sem"]
    GN, SG, SM, PV, NX = (s[k] for k in ("GN", "SG", "SM", "PV", "NX"))
    GS = SM
    W = (W0, W1, W2, W3, W4)
    sums = tuple(m012.at[:, q * width:(q + 1) * width] for q in range(3)) + (m3, m4)

    def cols(k):
        return slice(CH[k][0], CH[k][0] + CH[k][1])

    def rws(k):
        return slice(offs[k], offs[k] + parts[k])

    class Load:
        def __init__(self, n, *pairs):
            self.copies = [pltpu.make_async_copy(a, b, sem.at[n + k]) for k, (a, b) in enumerate(pairs)]

        def start(self):
            for c in self.copies:
                c.start()
            return self

        def wait(self):
            for c in self.copies:
                c.wait()

    all_here = entry_barrier(p)
    own_w = Load(0, *[(b, w.at[p.y, p.x, p.c, z]) for b, w in zip((b0, b1, b2, b3, b4), W)]).start()
    own_x = Load(5, (x_in, SX.at[0])).start()
    df_blocks = df_in
    own_df = Load(6, (df_blocks, slot(dF, 0))).start()
    own_gu = Load(7, (gus.at[p.i], WGU.at[p.y, p.i, z])).start()
    own_d = Load(8, *[(ds.at[rws(k)], WD[k].at[p.y, z]) for k in range(K)]).start()

    ZGU[z] = jnp.zeros(ZGU.shape[1:], BF)
    for k in range(K):
        ZD[k][z] = jnp.zeros(ZD[k].shape[1:], BF)

    @pl.when(first)
    def _():
        PV[...] = jnp.zeros(PV.shape, BF)

    @pl.when(last)
    def _():
        NX[...] = jnp.zeros(NX.shape, BF)

    def p0(k):
        for t in (2, 3, 1):
            m = p.member(t)
            cg[k].send(gus.at[m, :, :, cols(k)], WGU.at[p.y, p.i, z, :, :, cols(k)],
                       s_p0.at[k, t - 1], r_p0.at[k, t - 1], p.at(i=m))

    def acts(dst, q):
        for t in (2, 1):
            cp.send(slot(dst, 0), slot(dst, t), sem_h.at[q, 0, t - 1], sem_h.at[q, 1, t - 1], p.at(i=p.member(t)))

    def acts_wait(dst, q, t):
        cp.arrived(slot(dst, t), sem_h.at[q, 0, t - 1], sem_h.at[q, 1, t - 1], p.at(i=p.member(t)))

    def acts_forward(dst, q):
        acts_wait(dst, q, 2)
        cp.send(slot(dst, 2), slot(dst, 3), sem_h.at[q, 0, 2], sem_h.at[q, 1, 2], core_dev, group=True)

    def acts_forwarded(dst, q):
        cp.pending.append((True, lambda: pltpu.make_async_remote_copy(
            src_ref=slot(dst, 2), dst_ref=slot(dst, 3), send_sem=sem_h.at[q, 0, 2], recv_sem=sem_h.at[q, 1, 2],
            device_id=core_dev, device_id_type=MESH)))

    def gu_blk(k, y, zz):
        return WGU.at[y, :, zz, :, :, cols(k)]

    def ysend(k, zz):
        b = gu_blk(k, p.y, zz)
        cg[k].send(b, b, s_y.at[k, zz], r_y.at[k, zz], p.at(y=1 - p.y))

    def flow_ag(k):
        W = WD[k]
        for t in (1, 2, 3):
            m = p.member(t)
            cp.arrived(WGU.at[p.y, m, z, :, :, cols(k)], s_p0.at[k, t - 1], r_p0.at[k, t - 1], p.at(i=m))
        p.to_both_sides(cg[k], gu_blk(k, p.y, z), lambda to: s_z.at[k, to], r_z.at[k, z])
        b = W.at[p.y, z]
        cg[k].send(b, b, s_dy.at[k], r_dy.at[k], p.at(y=1 - p.y))
        p.to_both_sides(cg[k], b, lambda to: s_dz.at[k, p.y, to], r_dz.at[k, p.y, z])
        yield
        ysend(k, z)
        b = W.at[1 - p.y, z]
        cp.arrived(b, s_dy.at[k], r_dy.at[k], p.at())
        p.to_both_sides(cg[k], b, lambda to: s_dz.at[k, 1 - p.y, to], r_dz.at[k, 1 - p.y, z])
        for zz in p.others:
            yield
            b = gu_blk(k, p.y, zz)
            cp.arrived(b, s_z.at[k, zz], r_z.at[k, zz], p.at())
            p.relay(cg[k], b, zz, s_z.at[k, nz + zz], r_z.at[k, zz])
            ysend(k, zz)
            for y in (p.y, 1 - p.y):
                b = W.at[y, zz]
                cp.arrived(b, s_dz.at[k, y, zz], r_dz.at[k, y, zz], p.at())
                p.relay(cg[k], b, zz, s_dz.at[k, y, nz + zz], r_dz.at[k, y, zz])
        yield
        for zz in (z,) + p.others:
            cp.arrived(gu_blk(k, 1 - p.y, zz), s_y.at[k, zz], r_y.at[k, zz], p.at())

    targets = p.others[::-1] + (z,)

    def flow_rs_gu(k, w):
        c = cols(k)
        for zz in targets:
            cp.send(GGU.at[1 - p.y, :, zz, w, :, c], RY.at[:, zz, w, :, c],
                    s_gy.at[k, w, zz], r_gy.at[k, w, zz], p.at(y=1 - p.y))
        for zz in p.others[::-1]:
            yield
            cp.arrived(RY.at[:, zz, w, :, c], s_gy.at[k, w, zz], r_gy.at[k, w, zz], p.at())

            def add(j, _, zz=zz):
                GGU[p.y, j, zz, w, :, c] = (
                    GGU[p.y, j, zz, w, :, c].astype(F32) + RY[j, zz, w, :, c].astype(F32)).astype(BF)
                return 0
            lax.fori_loop(0, TP, add, 0)
            cp.send(GGU.at[p.y, :, zz, w, :, c], ZGU.at[z, :, w, :, c], s_gz.at[k, w, zz], r_gz.at[k, w, z],
                    p.at(z=zz))
        yield
        cp.arrived(RY.at[:, z, w, :, c], s_gy.at[k, w, z], r_gy.at[k, w, z], p.at())
        for zz in p.others:
            cp.arrived(ZGU.at[zz, :, w, :, c], s_gz.at[k, w, zz], r_gz.at[k, w, zz], p.at())

        def add_all(j, _):
            v = GGU[p.y, j, z, w, :, c].astype(F32) + RY[j, z, w, :, c].astype(F32)
            for zz in range(nz):
                v = v + ZGU[zz, j, w, :, c].astype(F32)
            GGU[p.y, j, z, w, :, c] = v.astype(BF)
            return 0
        lax.fori_loop(0, TP, add_all, 0)
        for t in (2, 3, 1):
            m = p.member(t)
            cp.send(GGU.at[p.y, m, z, w, :, c], ogu_o.at[p.i, w, :, c], s_gt.at[k, w, t - 1], r_gt.at[k, w, t - 1],
                    p.at(i=m))
        own_out.append(Load(11 + 2 * k + w, (GGU.at[p.y, p.i, z, w, :, c], ogu_o.at[p.i, w, :, c])).start())
        yield
        for t in (1, 2, 3):
            m = p.member(t)
            cp.arrived(ogu_o.at[m, w, :, c], s_gt.at[k, w, t - 1], r_gt.at[k, w, t - 1], p.at(i=m))

    def flow_rs_d(k):
        G, L, Y = GD[k], ZD[k], YD[k]
        for zz in targets:
            cp.send(G.at[1 - p.y, zz], Y.at[zz], s_ey.at[k, zz], r_ey.at[k, zz], p.at(y=1 - p.y))
        for zz in p.others[::-1]:
            yield
            cp.arrived(Y.at[zz], s_ey.at[k, zz], r_ey.at[k, zz], p.at())
            G[p.y, zz] = (G[p.y, zz].astype(F32) + Y[zz].astype(F32)).astype(BF)
            cp.send(G.at[p.y, zz], L.at[z], s_ez.at[k, zz], r_ez.at[k, z], p.at(z=zz))
        yield
        cp.arrived(Y.at[z], s_ey.at[k, z], r_ey.at[k, z], p.at())
        for zz in p.others:
            cp.arrived(L.at[zz], s_ez.at[k, zz], r_ez.at[k, zz], p.at())
        v = G[p.y, z].astype(F32) + Y[z].astype(F32)
        for zz in range(nz):
            v = v + L[zz].astype(F32)
        od_o[rws(k), :] = v

    live, own_out = [], []

    def pump(n=1, which=None):
        for _ in range(n):
            for f in list(live if which is None else which):
                if f in live and next(f, "end") == "end":
                    live.remove(f)

    def run(*gens):
        for g in gens:
            for _ in g:
                pass
            if g in live:
                live.remove(g)

    own_w.wait()
    all_here()
    gp = gather_pieces(width)
    gather = [gather_flow(p, cp, n, q, W[q[0]], s["gather"]) for n, q in enumerate(gp)]
    states = {}

    def gather_to(*stops):
        left = list(gather)
        while left:
            for f in list(left):
                if states.get(f) in stops:
                    left.remove(f)
                else:
                    states[f] = next(f)
    gather_to("first")
    own_gu.wait()
    own_d.wait()
    own_df.wait()
    gather_to("z")
    for k in range(K):
        p0(k)
    gather_to("last axis")
    acts(dF, 1)
    ag = [flow_ag(k) for k in range(K)]
    for g in ag:
        next(g)
    for g in ag:
        next(g)
    gather_to("core")

    def need(*panels):
        for f, q in zip(gather, gp):
            if q[0] in panels:
                next(f, None)

    def panel(q, buf, n):
        return Load(n, *[(W[q].at[:, :, :, :, :, h * half:(h + 1) * half], buf.at[:, h, :, :, :, :, pl.ds(0, half)]) for h in range(2)])

    def half_panel(buf, h):
        return buf[:, h, :, :, :, :, :half].reshape(width, half)

    need(4)
    Load(20, (W4, SM)).start().wait()
    GN[...] = SM[...].reshape(width, LANES).astype(F32).T[:8]
    need(0)
    wb = panel(0, dAb, 21).start()
    own_x.wait()

    def norm(v):
        inv = lax.rsqrt(jnp.mean(v * v, axis=-1, keepdims=True) + eps)
        return inv, v * inv

    def tiles(size):
        return [slice(t * size, (t + 1) * size) for t in range(rows // size)]

    def norm_one(m, _):
        rs = pl.ds(pl.multiple_of(m * 128, 128), 128)
        _, n1 = norm(SX[0, rs].astype(F32))
        SX[1, rs] = (n1 * GN[0:1]).astype(BF)
        return 0
    lax.fori_loop(0, rows // 128, norm_one, 0)
    save_h1 = Load(30, (SX.at[1], SV16.at[0])).start()

    def project(buf, dst):
        def one(h, _):
            dHa[dst, :, pl.ds(pl.multiple_of(h * half, half), half)] = mm(SX[1], half_panel(buf, h), NN)
            return 0
        lax.fori_loop(0, 2, one, 0)
    need(2)
    wu = panel(2, dGb, 23).start()
    wb.wait()
    project(dAb, 0)
    need(1)
    wc = panel(1, dAb, 21).start()
    wu.wait()
    project(dGb, 2)
    save_bu = Load(31, (dHa.at[0], SV32.at[0]), (dHa.at[2], SV32.at[2])).start()

    def make_bx(m, _):
        rs = pl.ds(pl.multiple_of(m * 128, 128), 128)
        SX[2, rs] = (dHa[0, rs] * dHa[2, rs]).astype(BF)
        return 0
    lax.fori_loop(0, rows // 128, make_bx, 0)
    s_h, r_h = s["s_h"], s["r_h"]
    for m in range(2):
        cp.send(SX.at[2, pl.ds((m + 1) * count - 16, 16)], PV.at[m], s_h.at[0, m], r_h.at[0, m],
                p.at(z=z + 1), inner_r)
    save_bx = Load(33, (SX.at[2], SV16.at[1])).start()
    live.extend(ag)
    pump(1, ag[:1])
    need(3)
    wo = panel(3, dGb, 23).start()
    wc.wait()
    project(dAb, 1)
    save_c = Load(34, (dHa.at[1], SV32.at[1])).start()
    for m in range(2):
        cp.arrived(PV.at[m], s_h.at[0, m], r_h.at[0, m], p.at(), inner_l)

    def earlier(v, prev, back):
        r = lax.broadcasted_iota(jnp.int32, v.shape, 0)
        n = prev.shape[0]
        moved = pltpu.roll(v, back, 0)
        moved = jnp.where(r == back - 1, prev[n - 1:n], moved)
        return jnp.where(r == 0, prev[n - back:n - back + 1], moved)

    def later(v, after, ahead):
        r = lax.broadcasted_iota(jnp.int32, v.shape, 0)
        n = v.shape[0]
        moved = pltpu.roll(v, n - ahead, 0)
        moved = jnp.where(r == n - ahead, after[0:1], moved)
        return jnp.where(r == n - 1, after[ahead - 1:ahead], moved)

    lanes = 256
    nl = width // lanes

    def conv(q, _):
        m, c = q // nl, q % nl
        ls = pl.ds(pl.multiple_of(c * lanes, lanes), lanes)
        rs = pl.ds(pl.multiple_of(m * count, count), count)
        v = SX[2, rs, ls].astype(F32)
        prev = PV[m, :, ls].astype(F32)
        mk = masks[m]
        total = GN[2:3, ls] * earlier(v, prev, 2) * mk[:count, 0:1]
        total = total + GN[3:4, ls] * earlier(v, prev, 1) * mk[:count, 1:2]
        total = total + GN[4:5, ls] * v * mk[:count, 2:3]
        dHa[3, rs, ls] = total
        LX[0, rs, ls] = (dHa[1, rs, ls] * total).astype(BF)
        return 0
    lax.fori_loop(0, 2 * nl, conv, 0)
    save_cv = Load(35, (dHa.at[3], SV32.at[3]), (LX.at[0], SV16.at[2])).start()
    save_bu.wait()
    pump(1, ag)
    wo.wait()

    def residual(h, _):
        hs = pl.ds(pl.multiple_of(h * half, half), half)
        dHa[0, :, hs] = SX[0, :, hs].astype(F32) + mm(LX[0], half_panel(dGb, h), NN)
        return 0
    lax.fori_loop(0, 2, residual, 0)

    def norm_two(m, _):
        rs = pl.ds(pl.multiple_of(m * nz * shard, nz * shard), nz * shard)
        _, n2 = norm(dHa[0, rs])
        H[0, 0, m // 2, m % 2] = (n2 * GN[1:2]).astype(BF).reshape(nz, shard, width)
        return 0
    lax.fori_loop(0, 4, norm_two, 0)
    save_r = Load(37, (dHa.at[0], SV32.at[4])).start()
    save_cv.wait()
    acts(H, 0)
    save_h1.wait()
    save_bx.wait()
    save_c.wait()
    save_r.wait()
    pump(1, ag)

    def half_blocks(v):
        return v.reshape(2, nz, shard, v.shape[-1])

    def fwd_mid(k, t):
        c0, cn = CH[k]
        c = cols(k)
        wg = WGU[:, :, :, 0, :, c].reshape(width, cn)
        wu = WGU[:, :, :, 1, :, c].reshape(width, cn)
        wd = WD[k][...].reshape(cn, width)

        def some(r, _):
            rs = pl.ds(pl.multiple_of(r * count, count), count)
            h = H[t // 2, t % 2, r].reshape(count, width)
            a = mm(h, wg, NN)
            g = mm(h, wu, NN)
            dz = mm(dF[t // 2, t % 2, r].reshape(count, width), wd, NT)
            sg = 1.0 / (1.0 + jnp.exp(-a))
            act = a * sg
            Zb[t, r, :, :, :, c] = half_blocks((act * g).astype(BF))
            da = (dz * g * sg * (1.0 + a * (1.0 - sg))).astype(BF)
            dg = (dz * act).astype(BF)
            dAb[t // 2, t % 2, r, :, :, :, :cn] = half_blocks(da)
            dGb[t // 2, t % 2, r, :, :, :, :cn] = half_blocks(dg)
            d = mm(da, wg, NT) + mm(dg, wu, NT)
            if k == 0:
                dHa[t, rs] = d
            else:
                dHa[t, rs] += d
            return 0
        lax.fori_loop(0, 2, some, 0)

    def ffn_out(slot_of, put):
        def some(q, _):
            n, r = q // 2, q % 2
            t = slot_of(n)
            f = None
            for k in range(K):
                v = mm(Zb[t, r, :, :, :, cols(k)].reshape(count, CH[k][1]), WD[k][...].reshape(CH[k][1], width), NN)
                f = v if f is None else f + v
            put(n, pl.ds(pl.multiple_of(r * count, count), count), f)
            return 0
        lax.fori_loop(0, 4, some, 0)

    tok = TP * rows

    def grads(k):
        c0, cn = CH[k]
        c = cols(k)
        for w, src in ((0, dAb), (1, dGb)):
            def body(m, _, w=w, src=src):
                y, j = m // 2, (m % 2) * 2
                f = 2 * nz * shard
                ms = pl.ds(pl.multiple_of(m * f, f), f)
                v = mm(H[:, :, :, :, :, :, ms].reshape(tok, f), src[:, :, :, :, :, :, :cn].reshape(tok, cn), TN)
                GGU[y, pl.ds(j, 2), :, w, :, c] = v.astype(BF).reshape(2, nz, shard, cn)
                return 0
            lax.fori_loop(0, TP, body, 0)
            begin((k, w), flow_rs_gu(k, w))
            if k == K - 1:
                advance(*(((0, 0), (0, 1)) if w == 0 else ((0, 0), (0, 1), (0, 2))))
        r = parts[k]
        if 128 % r == 0 and (nz * r) % 128 == 0:
            def down(b, _):
                ls = pl.ds(pl.multiple_of(c0 + b * 128, 128), 128)
                v = mm(Zb[:, :, :, :, :, ls].reshape(tok, 128), dF[...].reshape(tok, width), TN).astype(BF)
                n, per = 128 // r, nz * r // 128
                GD[k][b // per, pl.ds((b % per) * n, n)] = v.reshape(n, r, width)
                return 0
            lax.fori_loop(0, cn // 128, down, 0)
            begin((k, 2), flow_rs_d(k))
            return
        for b in range(cn // 128):
            zb = Zb[:, :, :, :, :, c0 + b * 128:c0 + (b + 1) * 128].reshape(tok, 128)
            v = mm(zb, dF[...].reshape(tok, width), TN).astype(BF)
            lo = b * 128
            while lo < (b + 1) * 128:
                pos, q = lo // r, lo % r
                n = min(r - q, (b + 1) * 128 - lo)
                GD[k][pos // nz, pos % nz, q:q + n] = v[lo - b * 128:lo - b * 128 + n]
                lo += n
        begin((k, 2), flow_rs_d(k))

    rs_flows = {}

    def begin(key, flow):
        next(flow)
        rs_flows[key] = flow
        live.append(flow)

    def advance(*keys):
        for key in keys:
            if rs_flows[key] in live:
                pump(1, [rs_flows[key]])

    def x_land(q, e):
        return LX.at[2 + q] if e == 2 else LX.at[e]

    def x_send1(q, e, value=None):
        if value is not None:
            SX[e] = value.astype(BF)
        cx.send(SX.at[e], x_land(q, e), s_x.at[q, e], r_x.at[q, e], core_dev, group=True)

    def x_sent(q, e):
        cx.pending.append((True, lambda: pltpu.make_async_remote_copy(
            src_ref=SX.at[e], dst_ref=x_land(q, e), send_sem=s_x.at[q, e], recv_sem=r_x.at[q, e],
            device_id=x_dev if e == 2 else core_dev, device_id_type=MESH)))

    def x_wait(q, e):
        cx.arrived(x_land(q, e), s_x.at[q, e], r_x.at[q, e], p.at(i=p.member(2 if e == 2 else 1)))

    def x_send2(q, acc):
        x_wait(q, 1)
        SX[2] = (acc[...] + LX[1].astype(F32)).astype(BF)
        cx.send(SX.at[2], x_land(q, 2), s_x.at[q, 2], r_x.at[q, 2], x_dev, group=True)

    def x_add(q, acc, e):
        x_wait(q, e)
        acc[...] += x_land(q, e)[...].astype(F32)

    acts_forward(dF, 1)
    acts_forwarded(dF, 1)
    before = 0
    for k in range(K):
        run(ag[k])
        if k == K - 1:
            cp.drain(before)
        if k == 0:
            acts_wait(H, 0, 1)
            acts_wait(dF, 1, 1)
            def others_here():
                acts_forward(H, 0)
                acts_wait(dF, 1, 3)
                acts_wait(H, 0, 3)

            def one(t, _):
                pl.when(t == 2)(others_here)
                fwd_mid(0, t)
                return 0
            lax.fori_loop(0, TP, one, 0)
            acts_forwarded(H, 0)
            pump(1, ag[1:2])
        else:
            def sums_out():
                x_send1(0, 1, dHa[3])
                x_send2(0, dHa.at[2])

            def one(n, _, k=k):
                fwd_mid(k, TP - 1 - n)
                if k == K - 1:
                    pl.when(n == 1)(sums_out)
                return 0
            lax.fori_loop(0, TP, one, 0)
            if k == K - 1:
                x_send1(0, 0, dHa[1])
                for e in (1, 2, 0):
                    x_sent(0, e)
                advance((0, 0), (0, 0), (0, 0), (0, 1))
        cg[k].drain()
        before = len(cp.pending)
        grads(k)
    wo = panel(3, dAb, 21).start()
    x_add(0, dHa.at[0], 0)
    pl.semaphore_signal(s["ready"], inc=1, device_id=p.at(i=p.member(1)), device_id_type=MESH)
    pr = Load(40, (SV32.at[4], dHa.at[2])).start()

    def keep(n, rs, v):
        dHa[1 + 2 * n, rs] = v

    def stage(n, rs, v):
        SX[n, rs] = v.astype(BF)
    ffn_out(lambda n: 2 - 2 * n, keep)
    cx.drain(1)
    cx.pending.append(cx.pending.pop(0))
    cx.drain(1)
    ffn_out(lambda n: 1 + 2 * n, stage)
    pl.semaphore_wait(s["ready"], 1)
    x_send1(1, 0)
    x_send1(1, 1)
    x_sent(1, 0)
    x_sent(1, 1)
    x_add(0, dHa.at[0], 2)
    cx.drain(1)
    x_send2(1, dHa.at[1])
    x_sent(1, 2)
    x_add(1, dHa.at[3], 0)

    pc = Load(41, (SV32.at[1], dHa.at[1])).start()
    cx.drain(2)
    py = Load(42, (SV16.at[2], SX.at[0]), (SV16.at[0], SX.at[1])).start()
    pr.wait()
    SG[...] = jnp.zeros(SG.shape, F32)

    def back_two(m, _):
        n = nz * shard
        rs = pl.ds(pl.multiple_of(m * n, n), n)
        r = dHa[2, rs]
        dHa[3, rs] += r
        inv, n2 = norm(r)
        d = dHa[0, rs]
        SG[1:2] += jnp.sum(d * n2, axis=0, keepdims=True)
        dn = d * GN[1:2]
        df = dF[0, 0, m // 2, m % 2].reshape(n, width).astype(F32)
        dr = df + inv * (dn - n2 * jnp.mean(dn * n2, axis=-1, keepdims=True))
        dHa[0, rs] = dr
        WD[0][m // 2, pl.ds((m % 2) * (nz // 2), nz // 2), :low] = dr.astype(BF).reshape(nz // 2, low, width)
        return 0
    lax.fori_loop(0, 4, back_two, 0)
    pcv = Load(44, (SV32.at[3], dHa.at[2])).start()
    advance((1, 0))
    wo.wait()
    pc.wait()
    pcv.wait()
    wbk = panel(0, dGb, 23).start()

    def back_y(m, _):
        rs = pl.ds(pl.multiple_of(m * count, count), count)
        do = WD[0][m, :, :low].reshape(count, width)
        dy = mm(do[:, :half], half_panel(dAb, 0), NT) + mm(do[:, half:], half_panel(dAb, 1), NT)
        LX[1, rs] = (dy * dHa[2, rs]).astype(BF)
        WD[1][m, :, :low] = (dy * dHa[1, rs]).astype(BF).reshape(nz, low, width)
        return 0
    lax.fori_loop(0, 2, back_y, 0)
    advance((1, 0))
    wck = panel(1, dAb, 21).start()
    for m in range(2):
        cp.send(WD[1].at[m, 0, pl.ds(0, 16)], NX.at[m], s_h.at[1, m], r_h.at[1, m], p.at(z=z - 1), inner_l)
    pu = Load(41, (SV32.at[2], dHa.at[1])).start()
    pb = Load(44, (SV32.at[0], dHa.at[2])).start()

    panels = (H.at[0], H.at[1], dF.at[0], dF.at[1], GS)
    sp = sum_pieces(width)

    mix = {}

    def start_sums(q):
        for n, piece in enumerate(sp):
            if piece[0] != q:
                continue
            _, c0, cn, _ = piece
            lc = Zb.at[q, :, :, :, :, pl.ds(c0, cn)] if q < 4 else Zb.at[3, :, :, :, :, pl.ds(width, LANES)]
            g = sum_flow(p, ct, n, piece, panels[q], lc, s["land"]["one"][n], s["land"]["two"][n],
                         s["land"]["path"][n], sums[q], s["sum"])
            next(g)
            live.append(g)
            mix.setdefault(q, []).append(g)

    def weight_grad(q, left, right):
        def body(m, _):
            f = 2 * nz * shard
            ms = pl.ds(pl.multiple_of(m * f, f), f)
            v = mm(left(ms), right(), TN)
            panels[q][m // 2, m % 2] = v.astype(BF).reshape(2, nz, shard, width)
            return 0
        lax.fori_loop(0, width // (2 * nz * shard), body, 0)
        start_sums(q)

    py.wait()
    weight_grad(3, lambda ms: SX[0, :, ms], lambda: WD[0][:, :, :low].reshape(rows, width))
    advance((1, 0), (1, 1))
    weight_grad(1, lambda ms: SX[1, :, ms], lambda: LX[1])
    pbx = Load(42, (SV16.at[1], SX.at[0])).start()
    advance((1, 1))
    pump(1, mix[3])
    for m in range(2):
        cp.arrived(NX.at[m], s_h.at[1, m], r_h.at[1, m], p.at(), inner_r)
    pu.wait()
    pb.wait()
    pbx.wait()

    def back_conv(q, _):
        m, c = q // nl, q % nl
        ls = pl.ds(pl.multiple_of(c * lanes, lanes), lanes)
        rs = pl.ds(pl.multiple_of(m * count, count), count)
        v = SX[0, rs, ls].astype(F32)
        prev = PV[m, :, ls].astype(F32)
        dcv = WD[1][m, :, :low, ls].reshape(count, lanes).astype(F32)
        after = NX[m, :, ls].astype(F32)
        mk = masks[m]
        w0, w1, w2 = (dcv * mk[:count, t:t + 1] for t in range(3))
        SG[2:3, ls] += jnp.sum(w0 * earlier(v, prev, 2), axis=0, keepdims=True)
        SG[3:4, ls] += jnp.sum(w1 * earlier(v, prev, 1), axis=0, keepdims=True)
        SG[4:5, ls] += jnp.sum(w2 * v, axis=0, keepdims=True)
        tail = mk[count:count + 8]
        d = GN[2:3, ls] * later(w0, after[:8] * tail[:, 0:1], 2)
        d = d + GN[3:4, ls] * later(w1, after[:8] * tail[:, 1:2], 1)
        d = d + GN[4:5, ls] * w2
        LX[0, rs, ls] = (d * dHa[1, rs, ls]).astype(BF)
        LX[2, rs, ls] = (d * dHa[2, rs, ls]).astype(BF)
        return 0
    lax.fori_loop(0, 2 * nl, back_conv, 0)
    advance((1, 1), (1, 2), (1, 2))
    pump(1, mix[1])
    weight_grad(0, lambda ms: SX[1, :, ms], lambda: LX[0])
    advance((1, 2), (0, 2), (0, 2))
    weight_grad(2, lambda ms: SX[1, :, ms], lambda: LX[2])
    pump(1, mix[0])
    pump(1, mix[3])
    px = Load(42, (x_in, SX.at[1])).start()

    def back_in(e, buf):
        def one(m, _):
            rs = pl.ds(pl.multiple_of(m * count, count), count)
            v = mm(LX[e, rs, :half], half_panel(buf, 0), NT) + mm(LX[e, rs, half:], half_panel(buf, 1), NT)
            if e == 0:
                dHa[1, rs] = v
            else:
                dHa[1, rs] += v
            return 0
        lax.fori_loop(0, 2, one, 0)
    wbk.wait()
    back_in(0, dGb)
    wuk = panel(2, dGb, 23).start()
    pump(1, mix[2])
    pump(1, mix[1])
    wck.wait()
    back_in(1, dAb)
    pump(1, mix[3])
    pump(1, mix[0])
    wuk.wait()
    back_in(2, dGb)
    px.wait()

    def back_one(m, _):
        rs = pl.ds(pl.multiple_of(m * 128, 128), 128)
        inv, n1 = norm(SX[1, rs].astype(F32))
        d = dHa[1, rs]
        SG[0:1] += jnp.sum(d * n1, axis=0, keepdims=True)
        dn = d * GN[0:1]
        SX[0, rs] = (dHa[0, rs] + inv * (dn - n1 * jnp.mean(dn * n1, axis=-1, keepdims=True))).astype(BF)
        return 0
    lax.fori_loop(0, rows // 128, back_one, 0)
    save_gx = Load(30, (SX.at[0], gx_o)).start()
    rest = jnp.zeros((LANES - 8, width), F32)
    GS[...] = jnp.concatenate([SG[...], rest], axis=0).T.astype(BF).reshape(GS.shape)
    start_sums(4)
    pump(1)
    x_add(1, dHa.at[3], 2)

    def finish(m, _):
        rs = pl.ds(pl.multiple_of(m * 128, 128), 128)
        SX[1, rs] = dHa[3, rs].astype(BF)
        return 0
    lax.fori_loop(0, rows // 128, finish, 0)
    save_out = Load(31, (SX.at[1], out_o)).start()
    while live:
        pump(1)
    save_gx.wait()
    save_out.wait()
    for c in own_out:
        c.wait()
    cp.drain()
    ct.drain()
    cx.drain()


def block_call(x, df, masks, blocks, gus, ds, parts, nz, cid):
    rows, width = x.shape
    shard, cols = gus.shape[2], gus.shape[3]
    K = len(parts)
    dr = ds.shape[0]
    V = pl.BlockSpec(memory_space=pltpu.VMEM)
    A = pl.BlockSpec(memory_space=pl.ANY)
    D = pltpu.SemaphoreType.DMA
    M = pltpu.VMEM
    maxc = max(parts) * 2 * nz
    sp = sum_pieces(width)
    ngather = len(gather_pieces(width))
    scratch = dict(
        H=M((2, 2, 2, 2, nz, shard, width), BF),
        dF=M((2, 2, 2, 2, nz, shard, width), BF),
        WGU=M((2, TP, nz, 2, shard, cols), BF),
        WD=[M((2, nz, r, width), BF) for r in parts],
        dHa=M((TP, rows, width), F32),
        Zb=M((TP, 2, 2, nz, shard, cols), BF),
        dAb=M((2, 2, 2, 2, nz, shard, maxc), BF),
        dGb=M((2, 2, 2, 2, nz, shard, maxc), BF),
        GD=[M((2, nz, r, width), BF) for r in parts],
        RY=M((TP, nz, 2, shard, cols), BF),
        ZGU=M((nz, TP, 2, shard, cols), BF),
        ZD=[M((nz, r, width), BF) for r in parts],
        YD=[M((nz, r, width), BF) for r in parts],
        LX=M((4, rows, width), BF),
        SX=M((3, rows, width), BF),
        GN=M((8, width), F32),
        SG=M((8, width), F32),
        SM=M((2, 2, 2, nz, shard, LANES), BF),
        PV=M((2, 16, width), BF),
        NX=M((2, 16, width), BF),
        land=sum_scratch(nz, shard, sp),
        gather=gather_sems(nz, ngather),
        sum=sum_sems(nz, len(sp)),
        sem=D((48,)), sem_h=D((2, 2, 3)), s_h=D((2, 2)), r_h=D((2, 2)),
        s_p0=D((K, 3)), r_p0=D((K, 3)),
        s_z=D((K, 2 * nz)), r_z=D((K, nz)), s_y=D((K, nz)), r_y=D((K, nz)),
        s_dz=D((K, 2, 2 * nz)), r_dz=D((K, 2, nz)), s_dy=D((K,)), r_dy=D((K,)),
        s_gy=D((K, 2, nz)), r_gy=D((K, 2, nz)), s_gz=D((K, 2, nz)), r_gz=D((K, 2, nz)),
        s_gt=D((K, 2, 3)), r_gt=D((K, 2, 3)),
        s_ez=D((K, nz)), r_ez=D((K, nz)), s_ey=D((K, nz)), r_ey=D((K, nz)),
        s_x=D((2, 3)), r_x=D((2, 3)), ready=pltpu.SemaphoreType.REGULAR,
    )
    S = jax.ShapeDtypeStruct
    wide = [width] * 4 + [LANES]
    outs = pl.pallas_call(
        functools.partial(block_body, parts, nz),
        name="block",
        out_shape=[
            S((rows, width), BF), S((rows, width), BF),
            S((TP, 2, shard, cols), BF), S((dr, width), F32),
            *[S((shard, w), F32) for w in (3 * width, width, LANES)],
            *[S((2, 2, 2, nz, shard, w), BF) for w in wide],
            S((5, rows, width), F32), S((3, rows, width), BF),
        ],
        in_specs=[A, A] + [V] * 6 + [A, A],
        out_specs=[A, A, A] + [V] * 4 + [A] * 7,
        scratch_shapes=[scratch],
        compiler_params=pltpu.CompilerParams(
            collective_id=cid, has_side_effects=True, vmem_limit_bytes=67_000_000),
    )(x, df.reshape(2, 2, nz, shard, width), masks, *blocks, gus, ds)
    return outs[:7]


def shifted(block, axis, distance):
    devices = range(lax.axis_size(axis))
    route = [(i - distance, i) for i in devices if i - distance in devices]
    return lax.ppermute(block, axis, route)


def matmul(left, right):
    return jnp.dot(left, right, preferred_element_type=jnp.float32)


def norm_parts(values):
    inverse = lax.rsqrt(jnp.mean(values * values, axis=-1, keepdims=True) + eps)
    return (inverse, values * inverse)


def norm_back(grad_hidden, normed, inverse, gain):
    grad_normed = grad_hidden * gain
    inner_mean = jnp.mean(grad_normed * normed, axis=-1, keepdims=True)
    return inverse * (grad_normed - normed * inner_mean)


def plain_device(
    tokens,
    segments,
    ln1_gain,
    in_weight,
    conv_kernel,
    out_weight,
    ln2_gain,
    gate_weight,
    up_weight,
    down_weight,
    cotangent,
):
    micro_count = tokens.shape[0]
    row_count = tokens.shape[2]
    width = tokens.shape[3]
    taps = conv_kernel.shape[0]
    offset = lax.axis_index("seq") * row_count
    low_gain1 = ln1_gain.astype(jnp.bfloat16)
    low_in = in_weight.astype(jnp.bfloat16)
    low_kernel = conv_kernel.astype(jnp.bfloat16)
    low_out = out_weight.astype(jnp.bfloat16)
    low_gain2 = ln2_gain.astype(jnp.bfloat16)
    low_gate = gate_weight.astype(jnp.bfloat16)
    low_up = up_weight.astype(jnp.bfloat16)
    low_down = down_weight.astype(jnp.bfloat16)
    shard_totals = None
    full_totals = None
    out_list = []
    grad_list = []
    for micro_index in range(micro_count):
        weights = (
            lax.all_gather(low_gain1, ("dp", "seq"), axis=0, tiled=True),
            lax.all_gather(low_in, ("dp", "seq"), axis=0, tiled=True),
            lax.all_gather(low_kernel, ("dp", "seq"), axis=1, tiled=True),
            lax.all_gather(low_out, ("dp", "seq"), axis=0, tiled=True),
            lax.all_gather(low_gain2, ("dp", "seq"), axis=0, tiled=True),
            lax.all_gather(low_gate, ("dp", "seq"), axis=0, tiled=True),
            lax.all_gather(low_up, ("dp", "seq"), axis=0, tiled=True),
            lax.all_gather(low_down, ("dp", "seq"), axis=0, tiled=True),
        )
        gain_one = weights[0].astype(jnp.float32)
        kernel = weights[2].astype(jnp.float32)
        gain_two = weights[4].astype(jnp.float32)
        seg_line = segments[micro_index, 0]
        fill = jnp.full((2,), -1, jnp.int32)
        seg_pad = jnp.concatenate([fill, seg_line, fill])
        window = lax.dynamic_slice_in_dim(seg_pad, offset, row_count + 4)
        masks = [
            (window[tap : tap + row_count + 2] == window[2 : row_count + 4]).astype(jnp.float32)
            for tap in range(taps)
        ]
        tokens_f = tokens[micro_index, 0].astype(jnp.float32)
        inverse_one, normed_one = norm_parts(tokens_f)
        hidden_one = (normed_one * gain_one).astype(jnp.bfloat16)
        projected = matmul(hidden_one, weights[1])
        b_part = projected[:, :width]
        c_part = projected[:, width : 2 * width]
        x_part = projected[:, 2 * width :]
        mixed = (b_part * x_part).astype(jnp.bfloat16)
        prev_rows = shifted(mixed[row_count - 2 :], "seq", 1)
        extended = jnp.concatenate([prev_rows, mixed], axis=0).astype(jnp.float32)
        conv_out = jnp.zeros((row_count, width), jnp.float32)
        for tap in range(taps):
            conv_out = (
                conv_out
                + kernel[tap] * extended[tap : tap + row_count] * masks[tap][:row_count, None]
            )
        gated = (c_part * conv_out).astype(jnp.bfloat16)
        resid = tokens_f + matmul(gated, weights[3])
        inverse_two, normed_two = norm_parts(resid)
        hidden_two = (normed_two * gain_two).astype(jnp.bfloat16)
        gate_pre = matmul(hidden_two, weights[5])
        up_pre = matmul(hidden_two, weights[6])
        sigmoid_gate = jax.nn.sigmoid(gate_pre)
        activated = gate_pre * sigmoid_gate
        inner = (activated * up_pre).astype(jnp.bfloat16)
        ffn_out = matmul(inner, weights[7])
        out_list.append((resid + ffn_out).astype(jnp.bfloat16))
        back_weights = (
            lax.all_gather(low_gain1, ("dp", "seq"), axis=0, tiled=True),
            lax.all_gather(low_in, ("dp", "seq"), axis=0, tiled=True),
            lax.all_gather(low_kernel, ("dp", "seq"), axis=1, tiled=True),
            lax.all_gather(low_out, ("dp", "seq"), axis=0, tiled=True),
            lax.all_gather(low_gain2, ("dp", "seq"), axis=0, tiled=True),
            lax.all_gather(low_gate, ("dp", "seq"), axis=0, tiled=True),
            lax.all_gather(low_up, ("dp", "seq"), axis=0, tiled=True),
            lax.all_gather(low_down, ("dp", "seq"), axis=0, tiled=True),
        )
        grad_final = cotangent[micro_index, 0]
        grad_inner = matmul(grad_final, back_weights[7].T)
        part_down = matmul(inner.T, grad_final)
        grad_gate_pre = (
            grad_inner * up_pre * sigmoid_gate * (1.0 + gate_pre * (1.0 - sigmoid_gate))
        ).astype(jnp.bfloat16)
        grad_up_pre = (grad_inner * activated).astype(jnp.bfloat16)
        grad_hidden_two = matmul(grad_gate_pre, back_weights[5].T) + matmul(
            grad_up_pre, back_weights[6].T
        )
        part_gate = matmul(hidden_two.T, grad_gate_pre)
        part_up = matmul(hidden_two.T, grad_up_pre)
        part_gain2 = jnp.sum(grad_hidden_two * normed_two, axis=0)
        grad_resid = grad_final.astype(jnp.float32) + norm_back(
            grad_hidden_two, normed_two, inverse_two, gain_two
        )
        grad_branch = grad_resid.astype(jnp.bfloat16)
        grad_gated = matmul(grad_branch, back_weights[3].T)
        part_out = matmul(gated.T, grad_branch)
        grad_c = grad_gated * conv_out
        grad_conv = (grad_gated * c_part).astype(jnp.bfloat16)
        next_rows = shifted(grad_conv[:2], "seq", -1)
        grad_extended = jnp.concatenate([grad_conv, next_rows], axis=0).astype(jnp.float32)
        grad_mixed = jnp.zeros((row_count, width), jnp.float32)
        kernel_terms = []
        for tap in range(taps):
            weighted = grad_extended * masks[tap][:, None]
            grad_mixed = grad_mixed + kernel[tap] * weighted[2 - tap : 2 - tap + row_count]
            kernel_terms.append(
                jnp.sum(weighted[:row_count] * extended[tap : tap + row_count], axis=0)
            )
        part_kernel = jnp.stack(kernel_terms, axis=0)
        grad_proj = jnp.concatenate(
            [grad_mixed * x_part, grad_c, grad_mixed * b_part], axis=1
        ).astype(jnp.bfloat16)
        grad_hidden_one = matmul(grad_proj, back_weights[1].T)
        part_in = matmul(hidden_one.T, grad_proj)
        part_gain1 = jnp.sum(grad_hidden_one * normed_one, axis=0)
        grad_input = grad_resid + norm_back(grad_hidden_one, normed_one, inverse_one, gain_one)
        grad_list.append(grad_input.astype(jnp.bfloat16))
        parts = (
            part_gain1,
            part_in,
            part_kernel,
            part_out,
            part_gain2,
            part_gate,
            part_up,
            part_down,
        )
        full_totals = (
            parts
            if full_totals is None
            else tuple((first + second for first, second in zip(full_totals, parts)))
        )
    shard_totals = (
        lax.psum_scatter(full_totals[0], ("dp", "seq"), scatter_dimension=0, tiled=True),
        lax.psum_scatter(full_totals[1], ("dp", "seq"), scatter_dimension=0, tiled=True),
        lax.psum_scatter(full_totals[2], ("dp", "seq"), scatter_dimension=1, tiled=True),
        lax.psum_scatter(full_totals[3], ("dp", "seq"), scatter_dimension=0, tiled=True),
        lax.psum_scatter(full_totals[4], ("dp", "seq"), scatter_dimension=0, tiled=True),
        lax.psum_scatter(full_totals[5], ("dp", "seq"), scatter_dimension=0, tiled=True),
        lax.psum_scatter(full_totals[6], ("dp", "seq"), scatter_dimension=0, tiled=True),
        lax.psum_scatter(full_totals[7], ("dp", "seq"), scatter_dimension=0, tiled=True),
    )
    output = jnp.stack(out_list, axis=0)[:, None]
    grad_tokens = jnp.stack(grad_list, axis=0)[:, None]
    return (
        output,
        grad_tokens,
        shard_totals[0],
        shard_totals[1],
        shard_totals[2],
        shard_totals[3],
        shard_totals[4],
        shard_totals[5],
        shard_totals[6],
        shard_totals[7],
    )


def cut_columns(w, parts, ny, nz):
    rows, shard = w.shape[0], w.shape[1] // (ny * TP * nz)
    cut = w.astype(BF).reshape(rows, ny, TP, nz, shard)
    pieces, start = [], 0
    for size in parts:
        piece = cut[..., start : start + size].transpose(2, 0, 1, 3, 4)
        pieces.append(piece.reshape(TP, rows, ny * nz * size))
        start += size
    return jnp.concatenate(pieces, axis=-1)


def join_columns(g, parts, ny, nz):
    rows = g.shape[1]
    pieces, start, npos = [], 0, ny * nz
    for size in parts:
        piece = g[:, :, npos * start : npos * (start + size)].reshape(TP, rows, ny, nz, size)
        pieces.append(piece.transpose(1, 2, 0, 3, 4))
        start += size
    return jnp.concatenate(pieces, axis=-1).reshape(rows, -1).astype(F32)


def fast_device(
    parts,
    tokens,
    segments,
    ln1_gain,
    in_weight,
    conv_kernel,
    out_weight,
    ln2_gain,
    gate_weight,
    up_weight,
    down_weight,
    cotangent,
):
    micro, _, count, width = tokens.shape
    taps = conv_kernel.shape[0]
    nz = lax.axis_size("seq")
    ny = lax.axis_size("dp") // TP
    rows = micro * count
    low_in = in_weight.astype(BF)
    small = jnp.concatenate([ln1_gain[None], ln2_gain[None], conv_kernel], axis=0).astype(BF)
    small = jnp.pad(small.T, ((0, 0), (0, LANES - taps - 2)))
    blocks = [low_in[:, q * width : (q + 1) * width] for q in range(3)]
    blocks += [out_weight.astype(BF), small]
    offset = lax.axis_index("seq") * count
    fill = jnp.full((micro, 2), -1, jnp.int32)
    seg_pad = jnp.concatenate([fill, segments[:, 0], fill, fill, fill, fill], axis=1)
    window = lax.dynamic_slice_in_dim(seg_pad, offset, count + 10, axis=1)
    masks = jnp.stack(
        [window[:, tap : tap + count + 8] == window[:, 2 : count + 10] for tap in range(taps)], axis=-1
    ).astype(F32)
    masks = jnp.pad(masks, ((0, 0), (0, 0), (0, LANES - taps)))
    gus = jnp.stack([cut_columns(w, parts, ny, nz) for w in (gate_weight, up_weight)], axis=1)
    output, gx, gu, gd, g_in, g_out, g_small = block_call(
        tokens.reshape(rows, width), cotangent.reshape(rows, width), masks, blocks, gus,
        down_weight.astype(BF), parts, nz, 0
    )
    g_gate = join_columns(gu[:, 0], parts, ny, nz)
    g_up = join_columns(gu[:, 1], parts, ny, nz)
    g_small = g_small[:, : taps + 2].T
    shape = tokens.shape
    return (
        output.reshape(shape), gx.reshape(shape), g_small[0], g_in, g_small[2:], g_out,
        g_small[1], g_gate, g_up, gd,
    )


def row_parts(mesh, token_shape, down_shape):
    nd, nz = mesh.shape["dp"], mesh.shape["seq"]
    if nd != 2 * TP:
        return None
    per = down_shape[0] // (nd * nz)
    shard = token_shape[3] // (nd * nz)
    rows = token_shape[0] * (token_shape[2] // nz)
    if per <= 64 or per % 16 or shard % 16 or token_shape[1] != nd or token_shape[0] != 2:
        return None
    if rows != 4 * nz * shard or token_shape[3] != 2 * rows or 128 * nz != rows:
        return None
    return (per - 64, 64)


def solution(mesh):
    in_specs = (
        P(None, "dp", "seq", None),
        P(None, "dp", None),
        P(("dp", "seq")),
        P(("dp", "seq"), None),
        P(None, ("dp", "seq")),
        P(("dp", "seq"), None),
        P(("dp", "seq")),
        P(("dp", "seq"), None),
        P(("dp", "seq"), None),
        P(("dp", "seq"), None),
        P(None, "dp", "seq", None),
    )
    out_specs = (
        P(None, "dp", "seq", None),
        P(None, "dp", "seq", None),
        P(("dp", "seq")),
        P(("dp", "seq"), None),
        P(None, ("dp", "seq")),
        P(("dp", "seq"), None),
        P(("dp", "seq")),
        P(("dp", "seq"), None),
        P(("dp", "seq"), None),
        P(("dp", "seq"), None),
    )

    def run(*arrays):
        parts = row_parts(mesh, arrays[0].shape, arrays[9].shape)
        device = plain_device if parts is None else functools.partial(fast_device, parts)
        return jax.shard_map(
            device, mesh=mesh, in_specs=in_specs, out_specs=out_specs, check_vma=False
        )(*arrays)

    return run
```

```python
import functools
import jax
import jax.numpy as jnp
from jax import lax
from jax.experimental import pallas as pl
from jax.experimental.pallas import tpu as pltpu
from jax.sharding import PartitionSpec as P

BF = jnp.bfloat16
F32 = jnp.float32
eps = 1e-05
MESH = pl.DeviceIdType.MESH
NN = (((1,), (0,)), ((), ()))
NT = (((1,), (1,)), ((), ()))
TN = (((0,), (0,)), ((), ()))
TP = 4
LANES = 128


def mm(left, right, dims):
    return lax.dot_general(left, right, dims, preferred_element_type=F32)


def when(pred, body):
    if pred is True:
        body()
    else:
        pl.when(pred)(body)


class Place:
    def __init__(self, nz):
        dp = lax.axis_index("dp")
        self.dp = dp
        self.y = dp // TP
        self.i = dp % TP
        self.z = lax.axis_index("seq")
        self.nz = nz
        self.x = self.i // 2
        self.c = self.i % 2
        self.others = tuple(self._near(k) for k in range(nz - 1))

    def _near(self, k):
        ranks = [sorted((q for q in range(self.nz) if q != z), key=lambda q: abs(q - z)) for z in range(self.nz)]
        place = jnp.int32(ranks[0][k])
        for z in range(1, self.nz):
            place = jnp.where(self.z == z, ranks[z][k], place)
        return place

    def to_both_sides(self, cp, block, ssem, rsem):
        for to, there in ((self.z - 1, self.z > 0), (self.z + 1, self.z < self.nz - 1)):
            cp.send(block, block, ssem(to), rsem, self.at(z=to), there)

    def relay(self, cp, block, source, ssem, rsem):
        to = jnp.where(source < self.z, self.z + 1, self.z - 1)
        cp.send(block, block, ssem, rsem, self.at(z=to), (to >= 0) & (to < self.nz))

    def member(self, t):
        x = 1 - self.x if t // 2 else self.x
        c = 1 - self.c if t % 2 else self.c
        return x * 2 + c

    def at(self, y=None, i=None, z=None):
        z = self.z if z is None else z
        if y is None and i is None:
            return (self.dp, z)
        y = self.y if y is None else y
        i = self.i if i is None else i
        return (y * TP + i, z)


class Copies:
    def __init__(self):
        self.pending = []

    def send(self, src, dst, ssem, rsem, device, pred=True, group=None):
        def make():
            return pltpu.make_async_remote_copy(
                src_ref=src, dst_ref=dst, send_sem=ssem, recv_sem=rsem,
                device_id=device, device_id_type=MESH)
        when(pred, lambda: make().start())
        if group is None:
            self.pending.append((pred, make))

    def local(self, src, dst, sem):
        pltpu.make_async_copy(src, dst, sem).start()

    def arrived(self, ref, ssem, rsem, device, pred=True):
        when(pred, lambda: pltpu.make_async_remote_copy(
            src_ref=ref, dst_ref=ref, send_sem=ssem, recv_sem=rsem,
            device_id=device, device_id_type=MESH).wait_recv())

    def drain(self, count=None):
        done = self.pending[:count]
        self.pending = self.pending[len(done):]
        for pred, make in done:
            when(pred, lambda make=make: make().wait_send())


def entry_barrier(p):
    bar = pltpu.get_barrier_semaphore()
    there = [p.at(i=p.member(t)) for t in range(1, TP)] + [p.at(y=1 - p.y)] + [p.at(z=q) for q in p.others]
    for device in there:
        pl.semaphore_signal(bar, inc=1, device_id=device, device_id_type=MESH)
    return lambda: pl.semaphore_wait(bar, len(there))


def gather_pieces(width):
    return (
        (4, 0, LANES, "zyx"),
        (0, 0, width, "zyx"),
        (2, 0, width, "xzy"),
        (1, 0, width, "zxy"),
        (3, 0, width, "yzx"),
    )


def sum_pieces(width):
    half = width // 2
    return (
        (3, 0, half, "zyx"), (3, half, half, "zxy"),
        (1, 0, half, "zyx"), (1, half, half, "zxy"),
        (0, 0, half, "zyx"), (0, half, half, "zxy"),
        (2, 0, half, "zyx"), (2, half, half, "zxy"),
        (4, 0, LANES, "zyx"),
    )


def gather_sems(nz, count):
    D = pltpu.SemaphoreType.DMA
    return [D((count, 2, 2 * nz)), D((count, 2, nz)), D((count, nz)), D((count, nz)), D((count, 2, nz)),
            D((count, 2, nz)), D((count,)), D((count,))]


def gather_flow(p, cp, n, piece, W, sems):
    s_z, r_z, s_1, r_1, s_2, r_2, s_c, r_c = sems
    _, c0, cn, order = piece
    cs = slice(c0, c0 + cn)
    z, nz = p.z, p.nz
    a_is_x = order.index("x") < order.index("y")
    zfirst = order[0] == "z"

    def blk(a, b, zz):
        y, x = (b, a) if a_is_x else (a, b)
        return W.at[y, x, p.c, zz, :, cs]
    a, b = (p.x, p.y) if a_is_x else (p.y, p.x)
    dev_x, dev_y = p.at(i=p.member(2)), p.at(y=1 - p.y)
    dev_a, dev_b = (dev_x, dev_y) if a_is_x else (dev_y, dev_x)

    def core(aa, bb, zz):
        r = blk(aa, bb, zz)
        cp.send(r, r, s_c.at[n], r_c.at[n], p.at(i=p.member(1)), group=True)

    def zsend(aa):
        p.to_both_sides(cp, blk(aa, b, z), lambda to: s_z.at[n, aa, to], r_z.at[n, aa, z])

    def asend(zz):
        r = blk(a, b, zz)
        cp.send(r, r, s_1.at[n, zz], r_1.at[n, zz], dev_a)

    def bsend(aa, zz):
        r = blk(aa, b, zz)
        cp.send(r, r, s_2.at[n, aa, zz], r_2.at[n, aa, zz], dev_b)

    asend(z)
    zsend(a)
    bsend(a, z)
    core(a, b, z)
    yield "first"
    if not zfirst:
        cp.arrived(blk(1 - a, b, z), s_1.at[n, z], r_1.at[n, z], p.at())
        zsend(1 - a)
        bsend(1 - a, z)
        core(1 - a, b, z)
    for zz in p.others:
        yield "z"
        for aa in ((a,) if zfirst else (a, 1 - a)):
            cp.arrived(blk(aa, b, zz), s_z.at[n, aa, zz], r_z.at[n, aa, zz], p.at())
            p.relay(cp, blk(aa, b, zz), zz, s_z.at[n, aa, nz + zz], r_z.at[n, aa, zz])
            if zfirst:
                asend(zz)
            bsend(aa, zz)
            core(aa, b, zz)
    if zfirst:
        yield "second"
        for zz in (z,) + p.others:
            cp.arrived(blk(1 - a, b, zz), s_1.at[n, zz], r_1.at[n, zz], p.at())
            bsend(1 - a, zz)
            core(1 - a, b, zz)
    for zz in (z,) + p.others:
        yield "last axis"
        for aa in (a, 1 - a):
            cp.arrived(blk(aa, 1 - b, zz), s_2.at[n, aa, zz], r_2.at[n, aa, zz], p.at())
            core(aa, 1 - b, zz)
    yield "core"
    cp.arrived(W.at[:, :, 1 - p.c, :, :, cs], s_c.at[n], r_c.at[n], p.at())
    cp.pending.append((True, lambda: pltpu.make_async_remote_copy(
        src_ref=W.at[:, :, p.c, :, :, cs], dst_ref=W.at[:, :, p.c, :, :, cs], send_sem=s_c.at[n],
        recv_sem=r_c.at[n], device_id=p.at(i=p.member(1)), device_id_type=MESH)))


def sum_sems(nz, count):
    D = pltpu.SemaphoreType.DMA
    return [D((count,)), D((count,)), D((count, nz)), D((count, nz)), D((count, nz)), D((count, nz)),
            D((count, nz)), D((count, nz))]


def sum_scratch(nz, shard, pieces):
    return dict(
        one=[pltpu.VMEM((2, nz, shard, q[2]), BF) for q in pieces],
        two=[pltpu.VMEM((nz if q[3][0] == "z" else 1, shard, q[2]), BF) for q in pieces],
        path=[pltpu.VMEM((nz, 1 if q[3][0] == "z" else 2, shard, q[2]), BF) for q in pieces],
    )


def sum_flow(p, cp, n, piece, G, LC, L1, L2, LZ, out, sems):
    s_c, r_c, s_1, r_1, s_2, r_2, s_z, r_z = sems
    _, c0, cn, order = piece
    cs = slice(c0, c0 + cn)
    z = p.z
    targets = p.others[::-1] + (z,)
    zlast = order[0] == "z"
    b_is_y = order.index("x") < order.index("y")
    b, a = (p.y, p.x) if b_is_y else (p.x, p.y)
    dev_x, dev_y = p.at(i=p.member(2)), p.at(y=1 - p.y)
    dev_b, dev_a = (dev_y, dev_x) if b_is_y else (dev_x, dev_y)

    def g(bb, aa, zz):
        y, x = (bb, aa) if b_is_y else (aa, bb)
        return (y, x, p.c, zz, slice(None), cs)

    def f(v):
        return v.astype(F32)

    def lc(bb, aa, zz):
        y, x = (bb, aa) if b_is_y else (aa, bb)
        return (y, x, zz)

    def row(bb, zz, aa=None):
        aa = slice(None) if aa is None else pl.ds(aa, 1)
        y, x = (bb, aa) if b_is_y else (aa, bb)
        return G.at[y, x, p.c, zz, :, cs]
    cp.send(G.at[:, :, 1 - p.c, :, :, cs], LC, s_c.at[n], r_c.at[n], p.at(i=p.member(1)))
    LZ[z] = jnp.zeros(LZ.shape[1:], BF)
    yield
    cp.arrived(LC, s_c.at[n], r_c.at[n], p.at())
    def add_core(bb):
        def one(zz, _):
            for aa in range(2):
                i = g(bb, aa, zz)
                G[i] = (f(G[i]) + f(LC[lc(bb, aa, zz)])).astype(BF)
            return 0
        lax.fori_loop(0, p.nz, one, 0)
    add_core(1 - b)
    for zz in targets:
        cp.send(row(1 - b, zz), L1.at[:, zz], s_1.at[n, zz], r_1.at[n, zz], dev_b)
    add_core(b)
    if zlast:
        yield
        for zz in targets:
            cp.arrived(L1.at[:, zz], s_1.at[n, zz], r_1.at[n, zz], p.at())
            i = g(b, 1 - a, zz)
            G[i] = (f(G[i]) + f(L1[1 - a, zz])).astype(BF)
            cp.send(G.at[i], L2.at[zz], s_2.at[n, zz], r_2.at[n, zz], dev_a)

    def own(zz, k):
        if zlast:
            return f(G[g(b, a, zz)]) + f(L1[a, zz]) + f(L2[zz])
        return f(G[g(b, k, zz)]) + f(L1[k, zz])
    yield
    for zz in targets:
        if zlast:
            cp.arrived(L2.at[zz], s_2.at[n, zz], r_2.at[n, zz], p.at())
        else:
            cp.arrived(L1.at[:, zz], s_1.at[n, zz], r_1.at[n, zz], p.at())
        if zz is z:
            continue
        for k in range(1 if zlast else 2):
            G[g(b, a if zlast else k, zz)] = own(zz, k).astype(BF)
        cp.send(row(b, zz, a if zlast else None), LZ.at[z], s_z.at[n, zz], r_z.at[n, z], p.at(z=zz))
    yield
    for zz in p.others:
        cp.arrived(LZ.at[zz], s_z.at[n, zz], r_z.at[n, zz], p.at())

    def total(k):
        v = own(z, k)
        for zz in range(p.nz):
            v = v + f(LZ[zz, k])
        return v
    if zlast:
        out[:, cs] = total(0)
        return
    G[g(b, 1 - a, z)] = total(1 - a).astype(BF)
    cp.send(G.at[g(b, 1 - a, z)], L2.at[0], s_2.at[n, 0], r_2.at[n, 0], dev_a)
    out[:, cs] = total(a)
    yield
    cp.arrived(L2.at[0], s_2.at[n, 0], r_2.at[n, 0], p.at())
    out[:, cs] += f(L2[0])


def slot(ref, t):
    return ref.at[t // 2, t % 2]


def block_body(parts, nz, x_in, df_in, masks, b0, b1, b2, b3, b4, gus, ds,
               out_o, gx_o, ogu_o, od_o, m012, m3, m4, W0, W1, W2, W3, W4, SV32, SV16, s):
    p = Place(nz)
    z = p.z
    rows, width = x_in.shape
    shard = gus.shape[2]
    npos = 2 * nz
    count = rows // 2
    half = width // 2
    low = rows // (2 * nz)
    offs = [sum(parts[:k]) for k in range(len(parts))]
    CH = [(offs[k] * npos, parts[k] * npos) for k in range(len(parts))]
    K = len(parts)
    cp, cx, ct = Copies(), Copies(), Copies()
    cg = [Copies() for _ in range(K)]
    core_dev, x_dev = p.at(i=p.member(1)), p.at(i=p.member(2))
    first, last = z == 0, z == nz - 1
    inner_l, inner_r = z > 0, z < nz - 1
    H, dF, WGU, WD, dHa, Zb, dAb, dGb = (s[k] for k in ("H", "dF", "WGU", "WD", "dHa", "Zb", "dAb", "dGb"))
    GGU = WGU
    GD, RY, ZGU, ZD, YD, LX, SX = (s[k] for k in ("GD", "RY", "ZGU", "ZD", "YD", "LX", "SX"))
    sem_h, s_p0, r_p0, s_z, r_z, s_y, r_y, s_dz, r_dz, s_dy, r_dy = (
        s[k] for k in ("sem_h", "s_p0", "r_p0", "s_z", "r_z", "s_y", "r_y", "s_dz", "r_dz", "s_dy", "r_dy"))
    s_gy, r_gy, s_gz, r_gz, s_gt, r_gt, s_ez, r_ez, s_ey, r_ey, s_x, r_x = (
        s[k] for k in ("s_gy", "r_gy", "s_gz", "r_gz", "s_gt", "r_gt", "s_ez", "r_ez", "s_ey", "r_ey", "s_x", "r_x"))
    sem = s["sem"]
    GN, SG, SM, PV, NX = (s[k] for k in ("GN", "SG", "SM", "PV", "NX"))
    GS = SM
    W = (W0, W1, W2, W3, W4)
    sums = tuple(m012.at[:, q * width:(q + 1) * width] for q in range(3)) + (m3, m4)

    def cols(k):
        return slice(CH[k][0], CH[k][0] + CH[k][1])

    def rws(k):
        return slice(offs[k], offs[k] + parts[k])

    class Load:
        def __init__(self, n, *pairs):
            self.copies = [pltpu.make_async_copy(a, b, sem.at[n + k]) for k, (a, b) in enumerate(pairs)]

        def start(self):
            for c in self.copies:
                c.start()
            return self

        def wait(self):
            for c in self.copies:
                c.wait()

    all_here = entry_barrier(p)
    own_w = Load(0, *[(b, w.at[p.y, p.x, p.c, z]) for b, w in zip((b0, b1, b2, b3, b4), W)]).start()
    own_x = Load(5, (x_in, SX.at[0])).start()
    df_blocks = df_in
    own_df = Load(6, (df_blocks, slot(dF, 0))).start()
    own_gu = Load(7, (gus.at[p.i], WGU.at[p.y, p.i, z])).start()
    own_d = Load(8, *[(ds.at[rws(k)], WD[k].at[p.y, z]) for k in range(K)]).start()

    ZGU[z] = jnp.zeros(ZGU.shape[1:], BF)
    for k in range(K):
        ZD[k][z] = jnp.zeros(ZD[k].shape[1:], BF)

    @pl.when(first)
    def _():
        PV[...] = jnp.zeros(PV.shape, BF)

    @pl.when(last)
    def _():
        NX[...] = jnp.zeros(NX.shape, BF)

    def p0(k):
        for t in (2, 3, 1):
            m = p.member(t)
            cg[k].send(gus.at[m, :, :, cols(k)], WGU.at[p.y, p.i, z, :, :, cols(k)],
                       s_p0.at[k, t - 1], r_p0.at[k, t - 1], p.at(i=m))

    def acts(dst, q):
        for t in (2, 1):
            cp.send(slot(dst, 0), slot(dst, t), sem_h.at[q, 0, t - 1], sem_h.at[q, 1, t - 1], p.at(i=p.member(t)))

    def acts_wait(dst, q, t):
        cp.arrived(slot(dst, t), sem_h.at[q, 0, t - 1], sem_h.at[q, 1, t - 1], p.at(i=p.member(t)))

    def acts_forward(dst, q):
        acts_wait(dst, q, 2)
        cp.send(slot(dst, 2), slot(dst, 3), sem_h.at[q, 0, 2], sem_h.at[q, 1, 2], core_dev, group=True)

    def acts_forwarded(dst, q):
        cp.pending.append((True, lambda: pltpu.make_async_remote_copy(
            src_ref=slot(dst, 2), dst_ref=slot(dst, 3), send_sem=sem_h.at[q, 0, 2], recv_sem=sem_h.at[q, 1, 2],
            device_id=core_dev, device_id_type=MESH)))

    def gu_blk(k, y, zz):
        return WGU.at[y, :, zz, :, :, cols(k)]

    def ysend(k, zz):
        b = gu_blk(k, p.y, zz)
        cg[k].send(b, b, s_y.at[k, zz], r_y.at[k, zz], p.at(y=1 - p.y))

    def flow_ag(k):
        W = WD[k]
        for t in (1, 2, 3):
            m = p.member(t)
            cp.arrived(WGU.at[p.y, m, z, :, :, cols(k)], s_p0.at[k, t - 1], r_p0.at[k, t - 1], p.at(i=m))
        p.to_both_sides(cg[k], gu_blk(k, p.y, z), lambda to: s_z.at[k, to], r_z.at[k, z])
        b = W.at[p.y, z]
        cg[k].send(b, b, s_dy.at[k], r_dy.at[k], p.at(y=1 - p.y))
        p.to_both_sides(cg[k], b, lambda to: s_dz.at[k, p.y, to], r_dz.at[k, p.y, z])
        yield
        ysend(k, z)
        b = W.at[1 - p.y, z]
        cp.arrived(b, s_dy.at[k], r_dy.at[k], p.at())
        p.to_both_sides(cg[k], b, lambda to: s_dz.at[k, 1 - p.y, to], r_dz.at[k, 1 - p.y, z])
        for zz in p.others:
            yield
            b = gu_blk(k, p.y, zz)
            cp.arrived(b, s_z.at[k, zz], r_z.at[k, zz], p.at())
            p.relay(cg[k], b, zz, s_z.at[k, nz + zz], r_z.at[k, zz])
            ysend(k, zz)
            for y in (p.y, 1 - p.y):
                b = W.at[y, zz]
                cp.arrived(b, s_dz.at[k, y, zz], r_dz.at[k, y, zz], p.at())
                p.relay(cg[k], b, zz, s_dz.at[k, y, nz + zz], r_dz.at[k, y, zz])
        yield
        for zz in (z,) + p.others:
            cp.arrived(gu_blk(k, 1 - p.y, zz), s_y.at[k, zz], r_y.at[k, zz], p.at())

    targets = p.others[::-1] + (z,)

    def flow_rs_gu(k, w):
        c = cols(k)
        for zz in targets:
            cp.send(GGU.at[1 - p.y, :, zz, w, :, c], RY.at[:, zz, w, :, c],
                    s_gy.at[k, w, zz], r_gy.at[k, w, zz], p.at(y=1 - p.y))
        for zz in p.others[::-1]:
            yield
            cp.arrived(RY.at[:, zz, w, :, c], s_gy.at[k, w, zz], r_gy.at[k, w, zz], p.at())

            def add(j, _, zz=zz):
                GGU[p.y, j, zz, w, :, c] = (
                    GGU[p.y, j, zz, w, :, c].astype(F32) + RY[j, zz, w, :, c].astype(F32)).astype(BF)
                return 0
            lax.fori_loop(0, TP, add, 0)
            cp.send(GGU.at[p.y, :, zz, w, :, c], ZGU.at[z, :, w, :, c], s_gz.at[k, w, zz], r_gz.at[k, w, z],
                    p.at(z=zz))
        yield
        cp.arrived(RY.at[:, z, w, :, c], s_gy.at[k, w, z], r_gy.at[k, w, z], p.at())
        for zz in p.others:
            cp.arrived(ZGU.at[zz, :, w, :, c], s_gz.at[k, w, zz], r_gz.at[k, w, zz], p.at())

        def add_all(j, _):
            v = GGU[p.y, j, z, w, :, c].astype(F32) + RY[j, z, w, :, c].astype(F32)
            for zz in range(nz):
                v = v + ZGU[zz, j, w, :, c].astype(F32)
            GGU[p.y, j, z, w, :, c] = v.astype(BF)
            return 0
        lax.fori_loop(0, TP, add_all, 0)
        for t in (2, 3, 1):
            m = p.member(t)
            cp.send(GGU.at[p.y, m, z, w, :, c], ogu_o.at[p.i, w, :, c], s_gt.at[k, w, t - 1], r_gt.at[k, w, t - 1],
                    p.at(i=m))
        own_out.append(Load(11 + 2 * k + w, (GGU.at[p.y, p.i, z, w, :, c], ogu_o.at[p.i, w, :, c])).start())
        yield
        for t in (1, 2, 3):
            m = p.member(t)
            cp.arrived(ogu_o.at[m, w, :, c], s_gt.at[k, w, t - 1], r_gt.at[k, w, t - 1], p.at(i=m))

    def flow_rs_d(k):
        G, L, Y = GD[k], ZD[k], YD[k]
        for zz in targets:
            cp.send(G.at[1 - p.y, zz], Y.at[zz], s_ey.at[k, zz], r_ey.at[k, zz], p.at(y=1 - p.y))
        for zz in p.others[::-1]:
            yield
            cp.arrived(Y.at[zz], s_ey.at[k, zz], r_ey.at[k, zz], p.at())
            G[p.y, zz] = (G[p.y, zz].astype(F32) + Y[zz].astype(F32)).astype(BF)
            cp.send(G.at[p.y, zz], L.at[z], s_ez.at[k, zz], r_ez.at[k, z], p.at(z=zz))
        yield
        cp.arrived(Y.at[z], s_ey.at[k, z], r_ey.at[k, z], p.at())
        for zz in p.others:
            cp.arrived(L.at[zz], s_ez.at[k, zz], r_ez.at[k, zz], p.at())
        v = G[p.y, z].astype(F32) + Y[z].astype(F32)
        for zz in range(nz):
            v = v + L[zz].astype(F32)
        od_o[rws(k), :] = v

    live, own_out = [], []

    def pump(n=1, which=None):
        for _ in range(n):
            for f in list(live if which is None else which):
                if f in live and next(f, "end") == "end":
                    live.remove(f)

    def run(*gens):
        for g in gens:
            for _ in g:
                pass
            if g in live:
                live.remove(g)

    own_w.wait()
    all_here()
    gp = gather_pieces(width)
    gather = [gather_flow(p, cp, n, q, W[q[0]], s["gather"]) for n, q in enumerate(gp)]
    states = {}

    def gather_to(*stops):
        left = list(gather)
        while left:
            for f in list(left):
                if states.get(f) in stops:
                    left.remove(f)
                else:
                    states[f] = next(f)
    gather_to("first")
    own_gu.wait()
    own_d.wait()
    own_df.wait()
    gather_to("z")
    for k in range(K):
        p0(k)
    gather_to("last axis")
    acts(dF, 1)
    ag = [flow_ag(k) for k in range(K)]
    for g in ag:
        next(g)
    for g in ag:
        next(g)
    gather_to("core")

    def need(*panels):
        for f, q in zip(gather, gp):
            if q[0] in panels:
                next(f, None)

    def panel(q, buf, n):
        return Load(n, *[(W[q].at[:, :, :, :, :, h * half:(h + 1) * half], buf.at[:, h, :, :, :, :, pl.ds(0, half)]) for h in range(2)])

    def half_panel(buf, h):
        return buf[:, h, :, :, :, :, :half].reshape(width, half)

    need(4)
    Load(20, (W4, SM)).start().wait()
    GN[...] = SM[...].reshape(width, LANES).astype(F32).T[:8]
    need(0)
    wb = panel(0, dAb, 21).start()
    own_x.wait()

    def norm(v):
        inv = lax.rsqrt(jnp.mean(v * v, axis=-1, keepdims=True) + eps)
        return inv, v * inv

    def tiles(size):
        return [slice(t * size, (t + 1) * size) for t in range(rows // size)]

    def norm_one(m, _):
        rs = pl.ds(pl.multiple_of(m * 128, 128), 128)
        _, n1 = norm(SX[0, rs].astype(F32))
        SX[1, rs] = (n1 * GN[0:1]).astype(BF)
        return 0
    lax.fori_loop(0, rows // 128, norm_one, 0)
    save_h1 = Load(30, (SX.at[1], SV16.at[0])).start()

    def project(buf, dst):
        def one(h, _):
            dHa[dst, :, pl.ds(pl.multiple_of(h * half, half), half)] = mm(SX[1], half_panel(buf, h), NN)
            return 0
        lax.fori_loop(0, 2, one, 0)
    need(2)
    wu = panel(2, dGb, 23).start()
    wb.wait()
    project(dAb, 0)
    need(1)
    wc = panel(1, dAb, 21).start()
    wu.wait()
    project(dGb, 2)
    save_bu = Load(31, (dHa.at[0], SV32.at[0]), (dHa.at[2], SV32.at[2])).start()

    def make_bx(m, _):
        rs = pl.ds(pl.multiple_of(m * 128, 128), 128)
        SX[2, rs] = (dHa[0, rs] * dHa[2, rs]).astype(BF)
        return 0
    lax.fori_loop(0, rows // 128, make_bx, 0)
    s_h, r_h = s["s_h"], s["r_h"]
    for m in range(2):
        cp.send(SX.at[2, pl.ds((m + 1) * count - 16, 16)], PV.at[m], s_h.at[0, m], r_h.at[0, m],
                p.at(z=z + 1), inner_r)
    save_bx = Load(33, (SX.at[2], SV16.at[1])).start()
    live.extend(ag)
    pump(1, ag[:1])
    need(3)
    wo = panel(3, dGb, 23).start()
    wc.wait()
    project(dAb, 1)
    save_c = Load(34, (dHa.at[1], SV32.at[1])).start()
    for m in range(2):
        cp.arrived(PV.at[m], s_h.at[0, m], r_h.at[0, m], p.at(), inner_l)

    def earlier(v, prev, back):
        r = lax.broadcasted_iota(jnp.int32, v.shape, 0)
        n = prev.shape[0]
        moved = pltpu.roll(v, back, 0)
        moved = jnp.where(r == back - 1, prev[n - 1:n], moved)
        return jnp.where(r == 0, prev[n - back:n - back + 1], moved)

    def later(v, after, ahead):
        r = lax.broadcasted_iota(jnp.int32, v.shape, 0)
        n = v.shape[0]
        moved = pltpu.roll(v, n - ahead, 0)
        moved = jnp.where(r == n - ahead, after[0:1], moved)
        return jnp.where(r == n - 1, after[ahead - 1:ahead], moved)

    lanes = 256
    nl = width // lanes

    def conv(q, _):
        m, c = q // nl, q % nl
        ls = pl.ds(pl.multiple_of(c * lanes, lanes), lanes)
        rs = pl.ds(pl.multiple_of(m * count, count), count)
        v = SX[2, rs, ls].astype(F32)
        prev = PV[m, :, ls].astype(F32)
        mk = masks[m]
        total = GN[2:3, ls] * earlier(v, prev, 2) * mk[:count, 0:1]
        total = total + GN[3:4, ls] * earlier(v, prev, 1) * mk[:count, 1:2]
        total = total + GN[4:5, ls] * v * mk[:count, 2:3]
        dHa[3, rs, ls] = total
        LX[0, rs, ls] = (dHa[1, rs, ls] * total).astype(BF)
        return 0
    lax.fori_loop(0, 2 * nl, conv, 0)
    save_cv = Load(35, (dHa.at[3], SV32.at[3]), (LX.at[0], SV16.at[2])).start()
    save_bu.wait()
    pump(1, ag)
    wo.wait()

    def residual(h, _):
        hs = pl.ds(pl.multiple_of(h * half, half), half)
        dHa[0, :, hs] = SX[0, :, hs].astype(F32) + mm(LX[0], half_panel(dGb, h), NN)
        return 0
    lax.fori_loop(0, 2, residual, 0)

    def norm_two(m, _):
        rs = pl.ds(pl.multiple_of(m * nz * shard, nz * shard), nz * shard)
        _, n2 = norm(dHa[0, rs])
        H[0, 0, m // 2, m % 2] = (n2 * GN[1:2]).astype(BF).reshape(nz, shard, width)
        return 0
    lax.fori_loop(0, 4, norm_two, 0)
    save_r = Load(37, (dHa.at[0], SV32.at[4])).start()
    save_cv.wait()
    acts(H, 0)
    save_h1.wait()
    save_bx.wait()
    save_c.wait()
    save_r.wait()
    pump(1, ag)

    def half_blocks(v):
        return v.reshape(2, nz, shard, v.shape[-1])

    def fwd_mid(k, t):
        c0, cn = CH[k]
        c = cols(k)
        wg = WGU[:, :, :, 0, :, c].reshape(width, cn)
        wu = WGU[:, :, :, 1, :, c].reshape(width, cn)
        wd = WD[k][...].reshape(cn, width)

        def some(r, _):
            rs = pl.ds(pl.multiple_of(r * count, count), count)
            h = H[t // 2, t % 2, r].reshape(count, width)
            a = mm(h, wg, NN)
            g = mm(h, wu, NN)
            dz = mm(dF[t // 2, t % 2, r].reshape(count, width), wd, NT)
            sg = 1.0 / (1.0 + jnp.exp(-a))
            act = a * sg
            Zb[t, r, :, :, :, c] = half_blocks((act * g).astype(BF))
            da = (dz * g * sg * (1.0 + a * (1.0 - sg))).astype(BF)
            dg = (dz * act).astype(BF)
            dAb[t // 2, t % 2, r, :, :, :, :cn] = half_blocks(da)
            dGb[t // 2, t % 2, r, :, :, :, :cn] = half_blocks(dg)
            d = mm(da, wg, NT) + mm(dg, wu, NT)
            if k == 0:
                dHa[t, rs] = d
            else:
                dHa[t, rs] += d
            return 0
        lax.fori_loop(0, 2, some, 0)

    def ffn_out(slot_of, put):
        def some(q, _):
            n, r = q // 2, q % 2
            t = slot_of(n)
            f = None
            for k in range(K):
                v = mm(Zb[t, r, :, :, :, cols(k)].reshape(count, CH[k][1]), WD[k][...].reshape(CH[k][1], width), NN)
                f = v if f is None else f + v
            put(n, pl.ds(pl.multiple_of(r * count, count), count), f)
            return 0
        lax.fori_loop(0, 4, some, 0)

    tok = TP * rows

    def grads(k):
        c0, cn = CH[k]
        c = cols(k)
        for w, src in ((0, dAb), (1, dGb)):
            def body(m, _, w=w, src=src):
                y, j = m // 2, (m % 2) * 2
                f = 2 * nz * shard
                ms = pl.ds(pl.multiple_of(m * f, f), f)
                v = mm(H[:, :, :, :, :, :, ms].reshape(tok, f), src[:, :, :, :, :, :, :cn].reshape(tok, cn), TN)
                GGU[y, pl.ds(j, 2), :, w, :, c] = v.astype(BF).reshape(2, nz, shard, cn)
                return 0
            lax.fori_loop(0, TP, body, 0)
            begin((k, w), flow_rs_gu(k, w))
            if k == K - 1:
                advance(*(((0, 0), (0, 1)) if w == 0 else ((0, 0), (0, 1), (0, 2))))
        r = parts[k]
        if 128 % r == 0 and (nz * r) % 128 == 0:
            def down(b, _):
                ls = pl.ds(pl.multiple_of(c0 + b * 128, 128), 128)
                v = mm(Zb[:, :, :, :, :, ls].reshape(tok, 128), dF[...].reshape(tok, width), TN).astype(BF)
                n, per = 128 // r, nz * r // 128
                GD[k][b // per, pl.ds((b % per) * n, n)] = v.reshape(n, r, width)
                return 0
            lax.fori_loop(0, cn // 128, down, 0)
            begin((k, 2), flow_rs_d(k))
            return
        for b in range(cn // 128):
            zb = Zb[:, :, :, :, :, c0 + b * 128:c0 + (b + 1) * 128].reshape(tok, 128)
            v = mm(zb, dF[...].reshape(tok, width), TN).astype(BF)
            lo = b * 128
            while lo < (b + 1) * 128:
                pos, q = lo // r, lo % r
                n = min(r - q, (b + 1) * 128 - lo)
                GD[k][pos // nz, pos % nz, q:q + n] = v[lo - b * 128:lo - b * 128 + n]
                lo += n
        begin((k, 2), flow_rs_d(k))

    rs_flows = {}

    def begin(key, flow):
        next(flow)
        rs_flows[key] = flow
        live.append(flow)

    def advance(*keys):
        for key in keys:
            if rs_flows[key] in live:
                pump(1, [rs_flows[key]])

    def x_land(q, e):
        return LX.at[2 + q] if e == 2 else LX.at[e]

    def x_send1(q, e, value=None):
        if value is not None:
            SX[e] = value.astype(BF)
        cx.send(SX.at[e], x_land(q, e), s_x.at[q, e], r_x.at[q, e], core_dev, group=True)

    def x_sent(q, e):
        cx.pending.append((True, lambda: pltpu.make_async_remote_copy(
            src_ref=SX.at[e], dst_ref=x_land(q, e), send_sem=s_x.at[q, e], recv_sem=r_x.at[q, e],
            device_id=x_dev if e == 2 else core_dev, device_id_type=MESH)))

    def x_wait(q, e):
        cx.arrived(x_land(q, e), s_x.at[q, e], r_x.at[q, e], p.at(i=p.member(2 if e == 2 else 1)))

    def x_send2(q, acc):
        x_wait(q, 1)
        SX[2] = (acc[...] + LX[1].astype(F32)).astype(BF)
        cx.send(SX.at[2], x_land(q, 2), s_x.at[q, 2], r_x.at[q, 2], x_dev, group=True)

    def x_add(q, acc, e):
        x_wait(q, e)
        acc[...] += x_land(q, e)[...].astype(F32)

    acts_forward(dF, 1)
    acts_forwarded(dF, 1)
    before = 0
    for k in range(K):
        run(ag[k])
        if k == K - 1:
            cp.drain(before)
        if k == 0:
            acts_wait(H, 0, 1)
            acts_wait(dF, 1, 1)
            def others_here():
                acts_forward(H, 0)
                acts_wait(dF, 1, 3)
                acts_wait(H, 0, 3)

            def one(t, _):
                pl.when(t == 2)(others_here)
                fwd_mid(0, t)
                return 0
            lax.fori_loop(0, TP, one, 0)
            acts_forwarded(H, 0)
            pump(1, ag[1:2])
        else:
            def sums_out():
                x_send1(0, 1, dHa[3])
                x_send2(0, dHa.at[2])

            def one(n, _, k=k):
                fwd_mid(k, TP - 1 - n)
                if k == K - 1:
                    pl.when(n == 1)(sums_out)
                return 0
            lax.fori_loop(0, TP, one, 0)
            if k == K - 1:
                x_send1(0, 0, dHa[1])
                for e in (1, 2, 0):
                    x_sent(0, e)
                advance((0, 0), (0, 0), (0, 1))
        cg[k].drain()
        before = len(cp.pending)
        grads(k)
    wo = panel(3, dAb, 21).start()
    x_add(0, dHa.at[0], 0)
    pl.semaphore_signal(s["ready"], inc=1, device_id=p.at(i=p.member(1)), device_id_type=MESH)
    pr = Load(40, (SV32.at[4], dHa.at[2])).start()

    def keep(n, rs, v):
        dHa[1 + 2 * n, rs] = v

    def stage(n, rs, v):
        SX[n, rs] = v.astype(BF)
    ffn_out(lambda n: 2 - 2 * n, keep)
    cx.drain(1)
    cx.pending.append(cx.pending.pop(0))
    cx.drain(1)
    ffn_out(lambda n: 1 + 2 * n, stage)
    pl.semaphore_wait(s["ready"], 1)
    x_send1(1, 0)
    x_send1(1, 1)
    x_sent(1, 0)
    x_sent(1, 1)
    x_add(0, dHa.at[0], 2)
    cx.drain(1)
    x_send2(1, dHa.at[1])
    x_sent(1, 2)
    x_add(1, dHa.at[3], 0)

    pc = Load(41, (SV32.at[1], dHa.at[1])).start()
    cx.drain(2)
    py = Load(42, (SV16.at[2], SX.at[0]), (SV16.at[0], SX.at[1])).start()
    pr.wait()
    SG[...] = jnp.zeros(SG.shape, F32)

    def back_two(m, _):
        n = nz * shard
        rs = pl.ds(pl.multiple_of(m * n, n), n)
        r = dHa[2, rs]
        dHa[3, rs] += r
        inv, n2 = norm(r)
        d = dHa[0, rs]
        SG[1:2] += jnp.sum(d * n2, axis=0, keepdims=True)
        dn = d * GN[1:2]
        df = dF[0, 0, m // 2, m % 2].reshape(n, width).astype(F32)
        dr = df + inv * (dn - n2 * jnp.mean(dn * n2, axis=-1, keepdims=True))
        dHa[0, rs] = dr
        WD[0][m // 2, pl.ds((m % 2) * (nz // 2), nz // 2), :low] = dr.astype(BF).reshape(nz // 2, low, width)
        return 0
    lax.fori_loop(0, 4, back_two, 0)
    pcv = Load(44, (SV32.at[3], dHa.at[2])).start()
    advance((1, 0))
    wo.wait()
    pc.wait()
    pcv.wait()
    wbk = panel(0, dGb, 23).start()

    def back_y(m, _):
        rs = pl.ds(pl.multiple_of(m * count, count), count)
        do = WD[0][m, :, :low].reshape(count, width)
        dy = mm(do[:, :half], half_panel(dAb, 0), NT) + mm(do[:, half:], half_panel(dAb, 1), NT)
        LX[1, rs] = (dy * dHa[2, rs]).astype(BF)
        WD[1][m, :, :low] = (dy * dHa[1, rs]).astype(BF).reshape(nz, low, width)
        return 0
    lax.fori_loop(0, 2, back_y, 0)
    advance((1, 0))
    wck = panel(1, dAb, 21).start()
    for m in range(2):
        cp.send(WD[1].at[m, 0, pl.ds(0, 16)], NX.at[m], s_h.at[1, m], r_h.at[1, m], p.at(z=z - 1), inner_l)
    pu = Load(41, (SV32.at[2], dHa.at[1])).start()
    pb = Load(44, (SV32.at[0], dHa.at[2])).start()

    panels = (H.at[0], H.at[1], dF.at[0], dF.at[1], GS)
    sp = sum_pieces(width)

    mix = {}

    def start_sums(q):
        for n, piece in enumerate(sp):
            if piece[0] != q:
                continue
            _, c0, cn, _ = piece
            lc = Zb.at[q, :, :, :, :, pl.ds(c0, cn)] if q < 4 else Zb.at[3, :, :, :, :, pl.ds(width, LANES)]
            g = sum_flow(p, ct, n, piece, panels[q], lc, s["land"]["one"][n], s["land"]["two"][n],
                         s["land"]["path"][n], sums[q], s["sum"])
            next(g)
            live.append(g)
            mix.setdefault(q, []).append(g)

    def weight_grad(q, left, right):
        def body(m, _):
            f = 2 * nz * shard
            ms = pl.ds(pl.multiple_of(m * f, f), f)
            v = mm(left(ms), right(), TN)
            panels[q][m // 2, m % 2] = v.astype(BF).reshape(2, nz, shard, width)
            return 0
        lax.fori_loop(0, width // (2 * nz * shard), body, 0)
        start_sums(q)

    py.wait()
    weight_grad(3, lambda ms: SX[0, :, ms], lambda: WD[0][:, :, :low].reshape(rows, width))
    advance((1, 0), (1, 1))
    weight_grad(1, lambda ms: SX[1, :, ms], lambda: LX[1])
    pbx = Load(42, (SV16.at[1], SX.at[0])).start()
    advance((1, 1))
    pump(1, mix[3])
    for m in range(2):
        cp.arrived(NX.at[m], s_h.at[1, m], r_h.at[1, m], p.at(), inner_r)
    pu.wait()
    pb.wait()
    pbx.wait()

    def back_conv(q, _):
        m, c = q // nl, q % nl
        ls = pl.ds(pl.multiple_of(c * lanes, lanes), lanes)
        rs = pl.ds(pl.multiple_of(m * count, count), count)
        v = SX[0, rs, ls].astype(F32)
        prev = PV[m, :, ls].astype(F32)
        dcv = WD[1][m, :, :low, ls].reshape(count, lanes).astype(F32)
        after = NX[m, :, ls].astype(F32)
        mk = masks[m]
        w0, w1, w2 = (dcv * mk[:count, t:t + 1] for t in range(3))
        SG[2:3, ls] += jnp.sum(w0 * earlier(v, prev, 2), axis=0, keepdims=True)
        SG[3:4, ls] += jnp.sum(w1 * earlier(v, prev, 1), axis=0, keepdims=True)
        SG[4:5, ls] += jnp.sum(w2 * v, axis=0, keepdims=True)
        tail = mk[count:count + 8]
        d = GN[2:3, ls] * later(w0, after[:8] * tail[:, 0:1], 2)
        d = d + GN[3:4, ls] * later(w1, after[:8] * tail[:, 1:2], 1)
        d = d + GN[4:5, ls] * w2
        LX[0, rs, ls] = (d * dHa[1, rs, ls]).astype(BF)
        LX[2, rs, ls] = (d * dHa[2, rs, ls]).astype(BF)
        return 0
    lax.fori_loop(0, 2 * nl, back_conv, 0)
    advance((1, 1), (1, 2), (1, 2))
    pump(1, mix[1])
    weight_grad(0, lambda ms: SX[1, :, ms], lambda: LX[0])
    advance((1, 2), (0, 2), (0, 2))
    weight_grad(2, lambda ms: SX[1, :, ms], lambda: LX[2])
    pump(1, mix[0])
    pump(1, mix[3])
    px = Load(42, (x_in, SX.at[1])).start()

    def back_in(e, buf):
        def one(m, _):
            rs = pl.ds(pl.multiple_of(m * count, count), count)
            v = mm(LX[e, rs, :half], half_panel(buf, 0), NT) + mm(LX[e, rs, half:], half_panel(buf, 1), NT)
            if e == 0:
                dHa[1, rs] = v
            else:
                dHa[1, rs] += v
            return 0
        lax.fori_loop(0, 2, one, 0)
    wbk.wait()
    back_in(0, dGb)
    wuk = panel(2, dGb, 23).start()
    pump(1, mix[2])
    pump(1, mix[1])
    wck.wait()
    back_in(1, dAb)
    pump(1, mix[3])
    pump(1, mix[0])
    wuk.wait()
    back_in(2, dGb)
    px.wait()

    def back_one(m, _):
        rs = pl.ds(pl.multiple_of(m * 128, 128), 128)
        inv, n1 = norm(SX[1, rs].astype(F32))
        d = dHa[1, rs]
        SG[0:1] += jnp.sum(d * n1, axis=0, keepdims=True)
        dn = d * GN[0:1]
        SX[0, rs] = (dHa[0, rs] + inv * (dn - n1 * jnp.mean(dn * n1, axis=-1, keepdims=True))).astype(BF)
        return 0
    lax.fori_loop(0, rows // 128, back_one, 0)
    save_gx = Load(30, (SX.at[0], gx_o)).start()
    rest = jnp.zeros((LANES - 8, width), F32)
    GS[...] = jnp.concatenate([SG[...], rest], axis=0).T.astype(BF).reshape(GS.shape)
    start_sums(4)
    pump(1)
    x_add(1, dHa.at[3], 2)

    def finish(m, _):
        rs = pl.ds(pl.multiple_of(m * 128, 128), 128)
        SX[1, rs] = dHa[3, rs].astype(BF)
        return 0
    lax.fori_loop(0, rows // 128, finish, 0)
    save_out = Load(31, (SX.at[1], out_o)).start()
    while live:
        pump(1)
    save_gx.wait()
    save_out.wait()
    for c in own_out:
        c.wait()
    cp.drain()
    ct.drain()
    cx.drain()


def block_call(x, df, masks, blocks, gus, ds, parts, nz, cid):
    rows, width = x.shape
    shard, cols = gus.shape[2], gus.shape[3]
    K = len(parts)
    dr = ds.shape[0]
    V = pl.BlockSpec(memory_space=pltpu.VMEM)
    A = pl.BlockSpec(memory_space=pl.ANY)
    D = pltpu.SemaphoreType.DMA
    M = pltpu.VMEM
    maxc = max(parts) * 2 * nz
    sp = sum_pieces(width)
    ngather = len(gather_pieces(width))
    scratch = dict(
        H=M((2, 2, 2, 2, nz, shard, width), BF),
        dF=M((2, 2, 2, 2, nz, shard, width), BF),
        WGU=M((2, TP, nz, 2, shard, cols), BF),
        WD=[M((2, nz, r, width), BF) for r in parts],
        dHa=M((TP, rows, width), F32),
        Zb=M((TP, 2, 2, nz, shard, cols), BF),
        dAb=M((2, 2, 2, 2, nz, shard, maxc), BF),
        dGb=M((2, 2, 2, 2, nz, shard, maxc), BF),
        GD=[M((2, nz, r, width), BF) for r in parts],
        RY=M((TP, nz, 2, shard, cols), BF),
        ZGU=M((nz, TP, 2, shard, cols), BF),
        ZD=[M((nz, r, width), BF) for r in parts],
        YD=[M((nz, r, width), BF) for r in parts],
        LX=M((4, rows, width), BF),
        SX=M((3, rows, width), BF),
        GN=M((8, width), F32),
        SG=M((8, width), F32),
        SM=M((2, 2, 2, nz, shard, LANES), BF),
        PV=M((2, 16, width), BF),
        NX=M((2, 16, width), BF),
        land=sum_scratch(nz, shard, sp),
        gather=gather_sems(nz, ngather),
        sum=sum_sems(nz, len(sp)),
        sem=D((48,)), sem_h=D((2, 2, 3)), s_h=D((2, 2)), r_h=D((2, 2)),
        s_p0=D((K, 3)), r_p0=D((K, 3)),
        s_z=D((K, 2 * nz)), r_z=D((K, nz)), s_y=D((K, nz)), r_y=D((K, nz)),
        s_dz=D((K, 2, 2 * nz)), r_dz=D((K, 2, nz)), s_dy=D((K,)), r_dy=D((K,)),
        s_gy=D((K, 2, nz)), r_gy=D((K, 2, nz)), s_gz=D((K, 2, nz)), r_gz=D((K, 2, nz)),
        s_gt=D((K, 2, 3)), r_gt=D((K, 2, 3)),
        s_ez=D((K, nz)), r_ez=D((K, nz)), s_ey=D((K, nz)), r_ey=D((K, nz)),
        s_x=D((2, 3)), r_x=D((2, 3)), ready=pltpu.SemaphoreType.REGULAR,
    )
    S = jax.ShapeDtypeStruct
    wide = [width] * 4 + [LANES]
    outs = pl.pallas_call(
        functools.partial(block_body, parts, nz),
        name="block",
        out_shape=[
            S((rows, width), BF), S((rows, width), BF),
            S((TP, 2, shard, cols), BF), S((dr, width), F32),
            *[S((shard, w), F32) for w in (3 * width, width, LANES)],
            *[S((2, 2, 2, nz, shard, w), BF) for w in wide],
            S((5, rows, width), F32), S((3, rows, width), BF),
        ],
        in_specs=[A, A] + [V] * 6 + [A, A],
        out_specs=[A, A, A] + [V] * 4 + [A] * 7,
        scratch_shapes=[scratch],
        compiler_params=pltpu.CompilerParams(
            collective_id=cid, has_side_effects=True, vmem_limit_bytes=67_000_000),
    )(x, df.reshape(2, 2, nz, shard, width), masks, *blocks, gus, ds)
    return outs[:7]


def shifted(block, axis, distance):
    devices = range(lax.axis_size(axis))
    route = [(i - distance, i) for i in devices if i - distance in devices]
    return lax.ppermute(block, axis, route)


def matmul(left, right):
    return jnp.dot(left, right, preferred_element_type=jnp.float32)


def norm_parts(values):
    inverse = lax.rsqrt(jnp.mean(values * values, axis=-1, keepdims=True) + eps)
    return (inverse, values * inverse)


def norm_back(grad_hidden, normed, inverse, gain):
    grad_normed = grad_hidden * gain
    inner_mean = jnp.mean(grad_normed * normed, axis=-1, keepdims=True)
    return inverse * (grad_normed - normed * inner_mean)


def plain_device(
    tokens,
    segments,
    ln1_gain,
    in_weight,
    conv_kernel,
    out_weight,
    ln2_gain,
    gate_weight,
    up_weight,
    down_weight,
    cotangent,
):
    micro_count = tokens.shape[0]
    row_count = tokens.shape[2]
    width = tokens.shape[3]
    taps = conv_kernel.shape[0]
    offset = lax.axis_index("seq") * row_count
    low_gain1 = ln1_gain.astype(jnp.bfloat16)
    low_in = in_weight.astype(jnp.bfloat16)
    low_kernel = conv_kernel.astype(jnp.bfloat16)
    low_out = out_weight.astype(jnp.bfloat16)
    low_gain2 = ln2_gain.astype(jnp.bfloat16)
    low_gate = gate_weight.astype(jnp.bfloat16)
    low_up = up_weight.astype(jnp.bfloat16)
    low_down = down_weight.astype(jnp.bfloat16)
    shard_totals = None
    full_totals = None
    out_list = []
    grad_list = []
    for micro_index in range(micro_count):
        weights = (
            lax.all_gather(low_gain1, ("dp", "seq"), axis=0, tiled=True),
            lax.all_gather(low_in, ("dp", "seq"), axis=0, tiled=True),
            lax.all_gather(low_kernel, ("dp", "seq"), axis=1, tiled=True),
            lax.all_gather(low_out, ("dp", "seq"), axis=0, tiled=True),
            lax.all_gather(low_gain2, ("dp", "seq"), axis=0, tiled=True),
            lax.all_gather(low_gate, ("dp", "seq"), axis=0, tiled=True),
            lax.all_gather(low_up, ("dp", "seq"), axis=0, tiled=True),
            lax.all_gather(low_down, ("dp", "seq"), axis=0, tiled=True),
        )
        gain_one = weights[0].astype(jnp.float32)
        kernel = weights[2].astype(jnp.float32)
        gain_two = weights[4].astype(jnp.float32)
        seg_line = segments[micro_index, 0]
        fill = jnp.full((2,), -1, jnp.int32)
        seg_pad = jnp.concatenate([fill, seg_line, fill])
        window = lax.dynamic_slice_in_dim(seg_pad, offset, row_count + 4)
        masks = [
            (window[tap : tap + row_count + 2] == window[2 : row_count + 4]).astype(jnp.float32)
            for tap in range(taps)
        ]
        tokens_f = tokens[micro_index, 0].astype(jnp.float32)
        inverse_one, normed_one = norm_parts(tokens_f)
        hidden_one = (normed_one * gain_one).astype(jnp.bfloat16)
        projected = matmul(hidden_one, weights[1])
        b_part = projected[:, :width]
        c_part = projected[:, width : 2 * width]
        x_part = projected[:, 2 * width :]
        mixed = (b_part * x_part).astype(jnp.bfloat16)
        prev_rows = shifted(mixed[row_count - 2 :], "seq", 1)
        extended = jnp.concatenate([prev_rows, mixed], axis=0).astype(jnp.float32)
        conv_out = jnp.zeros((row_count, width), jnp.float32)
        for tap in range(taps):
            conv_out = (
                conv_out
                + kernel[tap] * extended[tap : tap + row_count] * masks[tap][:row_count, None]
            )
        gated = (c_part * conv_out).astype(jnp.bfloat16)
        resid = tokens_f + matmul(gated, weights[3])
        inverse_two, normed_two = norm_parts(resid)
        hidden_two = (normed_two * gain_two).astype(jnp.bfloat16)
        gate_pre = matmul(hidden_two, weights[5])
        up_pre = matmul(hidden_two, weights[6])
        sigmoid_gate = jax.nn.sigmoid(gate_pre)
        activated = gate_pre * sigmoid_gate
        inner = (activated * up_pre).astype(jnp.bfloat16)
        ffn_out = matmul(inner, weights[7])
        out_list.append((resid + ffn_out).astype(jnp.bfloat16))
        back_weights = (
            lax.all_gather(low_gain1, ("dp", "seq"), axis=0, tiled=True),
            lax.all_gather(low_in, ("dp", "seq"), axis=0, tiled=True),
            lax.all_gather(low_kernel, ("dp", "seq"), axis=1, tiled=True),
            lax.all_gather(low_out, ("dp", "seq"), axis=0, tiled=True),
            lax.all_gather(low_gain2, ("dp", "seq"), axis=0, tiled=True),
            lax.all_gather(low_gate, ("dp", "seq"), axis=0, tiled=True),
            lax.all_gather(low_up, ("dp", "seq"), axis=0, tiled=True),
            lax.all_gather(low_down, ("dp", "seq"), axis=0, tiled=True),
        )
        grad_final = cotangent[micro_index, 0]
        grad_inner = matmul(grad_final, back_weights[7].T)
        part_down = matmul(inner.T, grad_final)
        grad_gate_pre = (
            grad_inner * up_pre * sigmoid_gate * (1.0 + gate_pre * (1.0 - sigmoid_gate))
        ).astype(jnp.bfloat16)
        grad_up_pre = (grad_inner * activated).astype(jnp.bfloat16)
        grad_hidden_two = matmul(grad_gate_pre, back_weights[5].T) + matmul(
            grad_up_pre, back_weights[6].T
        )
        part_gate = matmul(hidden_two.T, grad_gate_pre)
        part_up = matmul(hidden_two.T, grad_up_pre)
        part_gain2 = jnp.sum(grad_hidden_two * normed_two, axis=0)
        grad_resid = grad_final.astype(jnp.float32) + norm_back(
            grad_hidden_two, normed_two, inverse_two, gain_two
        )
        grad_branch = grad_resid.astype(jnp.bfloat16)
        grad_gated = matmul(grad_branch, back_weights[3].T)
        part_out = matmul(gated.T, grad_branch)
        grad_c = grad_gated * conv_out
        grad_conv = (grad_gated * c_part).astype(jnp.bfloat16)
        next_rows = shifted(grad_conv[:2], "seq", -1)
        grad_extended = jnp.concatenate([grad_conv, next_rows], axis=0).astype(jnp.float32)
        grad_mixed = jnp.zeros((row_count, width), jnp.float32)
        kernel_terms = []
        for tap in range(taps):
            weighted = grad_extended * masks[tap][:, None]
            grad_mixed = grad_mixed + kernel[tap] * weighted[2 - tap : 2 - tap + row_count]
            kernel_terms.append(
                jnp.sum(weighted[:row_count] * extended[tap : tap + row_count], axis=0)
            )
        part_kernel = jnp.stack(kernel_terms, axis=0)
        grad_proj = jnp.concatenate(
            [grad_mixed * x_part, grad_c, grad_mixed * b_part], axis=1
        ).astype(jnp.bfloat16)
        grad_hidden_one = matmul(grad_proj, back_weights[1].T)
        part_in = matmul(hidden_one.T, grad_proj)
        part_gain1 = jnp.sum(grad_hidden_one * normed_one, axis=0)
        grad_input = grad_resid + norm_back(grad_hidden_one, normed_one, inverse_one, gain_one)
        grad_list.append(grad_input.astype(jnp.bfloat16))
        parts = (
            part_gain1,
            part_in,
            part_kernel,
            part_out,
            part_gain2,
            part_gate,
            part_up,
            part_down,
        )
        full_totals = (
            parts
            if full_totals is None
            else tuple((first + second for first, second in zip(full_totals, parts)))
        )
    shard_totals = (
        lax.psum_scatter(full_totals[0], ("dp", "seq"), scatter_dimension=0, tiled=True),
        lax.psum_scatter(full_totals[1], ("dp", "seq"), scatter_dimension=0, tiled=True),
        lax.psum_scatter(full_totals[2], ("dp", "seq"), scatter_dimension=1, tiled=True),
        lax.psum_scatter(full_totals[3], ("dp", "seq"), scatter_dimension=0, tiled=True),
        lax.psum_scatter(full_totals[4], ("dp", "seq"), scatter_dimension=0, tiled=True),
        lax.psum_scatter(full_totals[5], ("dp", "seq"), scatter_dimension=0, tiled=True),
        lax.psum_scatter(full_totals[6], ("dp", "seq"), scatter_dimension=0, tiled=True),
        lax.psum_scatter(full_totals[7], ("dp", "seq"), scatter_dimension=0, tiled=True),
    )
    output = jnp.stack(out_list, axis=0)[:, None]
    grad_tokens = jnp.stack(grad_list, axis=0)[:, None]
    return (
        output,
        grad_tokens,
        shard_totals[0],
        shard_totals[1],
        shard_totals[2],
        shard_totals[3],
        shard_totals[4],
        shard_totals[5],
        shard_totals[6],
        shard_totals[7],
    )


def cut_columns(w, parts, ny, nz):
    rows, shard = w.shape[0], w.shape[1] // (ny * TP * nz)
    cut = w.astype(BF).reshape(rows, ny, TP, nz, shard)
    pieces, start = [], 0
    for size in parts:
        piece = cut[..., start : start + size].transpose(2, 0, 1, 3, 4)
        pieces.append(piece.reshape(TP, rows, ny * nz * size))
        start += size
    return jnp.concatenate(pieces, axis=-1)


def join_columns(g, parts, ny, nz):
    rows = g.shape[2]
    pieces, start, npos = [], 0, ny * nz
    for size in parts:
        piece = g[..., npos * start : npos * (start + size)].reshape(TP, 2, rows, ny, nz, size)
        pieces.append(piece.transpose(1, 2, 3, 0, 4, 5))
        start += size
    return jnp.concatenate(pieces, axis=-1).reshape(2, rows, -1)


def fast_device(
    parts,
    tokens,
    segments,
    ln1_gain,
    in_weight,
    conv_kernel,
    out_weight,
    ln2_gain,
    gate_weight,
    up_weight,
    down_weight,
    cotangent,
):
    micro, _, count, width = tokens.shape
    taps = conv_kernel.shape[0]
    nz = lax.axis_size("seq")
    ny = lax.axis_size("dp") // TP
    rows = micro * count
    low_in = in_weight.astype(BF)
    small = jnp.concatenate([ln1_gain[None], ln2_gain[None], conv_kernel], axis=0).astype(BF)
    small = jnp.pad(small.T, ((0, 0), (0, LANES - taps - 2)))
    blocks = [low_in[:, q * width : (q + 1) * width] for q in range(3)]
    blocks += [out_weight.astype(BF), small]
    offset = lax.axis_index("seq") * count
    fill = jnp.full((micro, 2), -1, jnp.int32)
    seg_pad = jnp.concatenate([fill, segments[:, 0], fill, fill, fill, fill], axis=1)
    window = lax.dynamic_slice_in_dim(seg_pad, offset, count + 10, axis=1)
    masks = jnp.stack(
        [window[:, tap : tap + count + 8] == window[:, 2 : count + 10] for tap in range(taps)], axis=-1
    ).astype(F32)
    masks = jnp.pad(masks, ((0, 0), (0, 0), (0, LANES - taps)))
    gus = jnp.stack([cut_columns(w, parts, ny, nz) for w in (gate_weight, up_weight)], axis=1)
    output, gx, gu, gd, g_in, g_out, g_small = block_call(
        tokens.reshape(rows, width), cotangent.reshape(rows, width), masks, blocks, gus,
        down_weight.astype(BF), parts, nz, 0
    )
    g_gate, g_up = (g.astype(F32) for g in join_columns(gu, parts, ny, nz))
    g_small = g_small[:, : taps + 2].T
    shape = tokens.shape
    return (
        output.reshape(shape), gx.reshape(shape), g_small[0], g_in, g_small[2:], g_out,
        g_small[1], g_gate, g_up, gd,
    )


def row_parts(mesh, token_shape, down_shape):
    nd, nz = mesh.shape["dp"], mesh.shape["seq"]
    if nd != 2 * TP:
        return None
    per = down_shape[0] // (nd * nz)
    shard = token_shape[3] // (nd * nz)
    rows = token_shape[0] * (token_shape[2] // nz)
    if per <= 64 or per % 16 or shard % 16 or token_shape[1] != nd or token_shape[0] != 2:
        return None
    if rows != 4 * nz * shard or token_shape[3] != 2 * rows or 128 * nz != rows:
        return None
    return (per - 64, 64)


def solution(mesh):
    in_specs = (
        P(None, "dp", "seq", None),
        P(None, "dp", None),
        P(("dp", "seq")),
        P(("dp", "seq"), None),
        P(None, ("dp", "seq")),
        P(("dp", "seq"), None),
        P(("dp", "seq")),
        P(("dp", "seq"), None),
        P(("dp", "seq"), None),
        P(("dp", "seq"), None),
        P(None, "dp", "seq", None),
    )
    out_specs = (
        P(None, "dp", "seq", None),
        P(None, "dp", "seq", None),
        P(("dp", "seq")),
        P(("dp", "seq"), None),
        P(None, ("dp", "seq")),
        P(("dp", "seq"), None),
        P(("dp", "seq")),
        P(("dp", "seq"), None),
        P(("dp", "seq"), None),
        P(("dp", "seq"), None),
    )

    def run(*arrays):
        parts = row_parts(mesh, arrays[0].shape, arrays[9].shape)
        device = plain_device if parts is None else functools.partial(fast_device, parts)
        return jax.shard_map(
            device, mesh=mesh, in_specs=in_specs, out_specs=out_specs, check_vma=False
        )(*arrays)

    return run
```
